256 devices in a mesh: kv: 2 (over y_hi), blk: 128 (over x, y_lo, z, core).
Axes of the slice: x: 4, y: 4 (y_hi: 2, y_lo: 2; y = y_hi * 2 + y_lo), z: 8, core: 2. Of those that a mesh axis runs over, the one named last changes fastest.
Arguments:
- hidden_in: bfloat16 [65536, 1280], P('blk'), may hold values from -6 to 6
- w_query: bfloat16 [1280, 1280], P(None, 'kv'), may hold values from -0.15625 to 0.15625
- w_key: bfloat16 [1280, 1280], P(None, 'kv'), may hold values from -0.15625 to 0.15625
- w_value: bfloat16 [1280, 1280], P(None, 'kv'), may hold values from -0.15625 to 0.15625
- w_out: bfloat16 [1280, 1280], P('kv'), may hold values from -0.15625 to 0.15625
- head_gain: float32 [1280], P('kv'), may hold values from 1 to 2.5
- eigen_rate: float32 [1280], replicated, may hold values from 0.15 to 0.6
- pool_keys: bfloat16 [512, 256, 1280], P('blk', None, 'kv'), may hold values from -2 to 2
- pool_values: bfloat16 [512, 256, 1280], P('blk', None, 'kv'), may hold values from -6 to 6
- req_len: int32 [128], P('blk'), may hold values from 1 to 512, as said below
- prefix_len: int32 [128], P('blk'), may hold values from 0 to 4, as said below
- prefix_pages: int32 [128, 4], replicated, may hold values from 0 to 511, as said below
- placement: int32 [256], replicated, may hold values from 0 to 255, as said below
Outputs:
- layer_out: bfloat16 [65536, 1280], P('blk')
- new_keys: bfloat16 [256, 256, 1280], P('blk', None, 'kv')
- new_values: bfloat16 [256, 256, 1280], P('blk', None, 'kv')
The draws below stay inside these ranges and needn't reach their ends.
Inputs may be any that keep to these rules, and one draw needn't show every extreme that they name: `req_len`: some request has all 512 tokens live. `prefix_len`: some request has 4 cached pages. Page prefix_pages[r, s] lies among pages h * 4 to (h + 1) * 4 - 1 with h = (r + 1 + s * 32) mod 128, for every slot s. Each page once; placement[b] lies among pages e * 2 to (e + 1) * 2 - 1 with e = (b // 2 + (2 * (b mod 2) + 1) * 32) mod 128.
All inputs are finite; a program needn't handle non-finite values.
Results may differ from the reference program's by a relative error of at most 0.0067.
Values may be sent and summed in bfloat16 or wider, within the bound.
A program may use at most 128 MiB of HBM per device.

```python
import math
import jax
import jax.numpy as jnp
from jax import lax

D = 1280
HEADS = 20
HD = 64
PAGE = 256
TOK_DEV = 512
PMAX = 4
POOL_REQ = 4
REQS = 128
TOKENS = 65536
NEWPAGES = 256
POOL = 512


def draw_req_len(key, part):
    counts = jax.random.randint(key, (REQS,), 1, TOK_DEV + 1)
    chosen = jax.random.randint(jax.random.fold_in(key, 7), (), 0, REQS)
    return jnp.where(jnp.arange(REQS) == chosen, TOK_DEV, counts).astype(jnp.int32)


def draw_prefix_len(key, part):
    counts = jax.random.randint(key, (REQS,), 0, PMAX + 1)
    chosen = jax.random.randint(jax.random.fold_in(key, 11), (), 0, REQS)
    return jnp.where(jnp.arange(REQS) == chosen, PMAX, counts).astype(jnp.int32)


def draw_prefix_pages(key, part):
    request = jnp.arange(REQS, dtype=jnp.int32)[:, None]
    slot = jnp.arange(PMAX, dtype=jnp.int32)[None, :]
    holder = (request + 1 + slot * REQS // PMAX) % REQS
    local = jax.random.randint(jax.random.fold_in(key, 13), (REQS, PMAX), 0, POOL_REQ)
    local = jnp.where((request == REQS - 1) & (slot == 0), 0, local)
    local = jnp.where((request == REQS - 2) & (slot == 0), POOL_REQ - 1, local)
    return (holder * POOL_REQ + local).astype(jnp.int32)


def draw_placement(key, part):
    per_dev = TOK_DEV // PAGE
    scores = jax.random.randint(jax.random.fold_in(key, 17), (REQS, per_dev), 0, 1 << 20)
    scores = scores * per_dev + jnp.arange(per_dev, dtype=jnp.int32)[None, :]
    order = jnp.argsort(scores, axis=1).astype(jnp.int32)
    source = jnp.arange(REQS, dtype=jnp.int32)[:, None]
    block = jnp.arange(per_dev, dtype=jnp.int32)[None, :]
    target = (source + (2 * block + 1) * REQS // (2 * per_dev)) % REQS
    slot = order[target, block]
    return (target * per_dev + slot).reshape(-1).astype(jnp.int32)


def levels(stream_key, dims, pieces, smallest, high):
    factor_of, own = 1.0, jax.random.fold_in(stream_key, 6)
    for position, shards_of in pieces:
        heights = jnp.exp(jax.random.uniform(jax.random.fold_in(own, position), (shards_of,), jnp.float32, smallest / len(pieces), high / len(pieces)))
        factor_of = factor_of * jnp.repeat(heights, dims[position] // shards_of).reshape([-1 if axis == position else 1 for axis in range(len(dims))])
    return factor_of


def noise(rng, dims, scale, reach, split=(), held_as=jnp.bfloat16):
    factor_of = levels(rng, dims, split, -0.22, 0.18) if split else 1.0
    entries = jax.random.normal(rng, dims, jnp.float32) * scale * factor_of
    return jnp.minimum(jnp.maximum(entries, -reach), reach).astype(held_as)


def setup_inputs(seed: int = 0) -> dict:
    key_list = jax.random.split(jax.random.key(seed), 14)
    return {
        "hidden_in": noise(key_list[0], (TOKENS, D), 1.0, 6.0, ((0, 128),)),
        "w_query": noise(key_list[1], (D, D), D ** -0.5, 0.15625, ((1, 2),)),
        "w_key": noise(key_list[2], (D, D), D ** -0.5, 0.15625, ((1, 2),)),
        "w_value": noise(key_list[3], (D, D), D ** -0.5, 0.15625, ((1, 2),)),
        "w_out": noise(key_list[4], (D, D), D ** -0.5, 0.15625, ((0, 2),)),
        "head_gain": jnp.clip(jnp.exp(math.log(2.5) - 0.916290732 * jax.random.uniform(key_list[5], (D,), jnp.float32) ** levels(key_list[5], (D,), ((0, 2),), -0.2, 0.2)), 1.0, 2.5),
        "eigen_rate": jnp.clip(jnp.exp(jax.random.uniform(key_list[6], (D,), jnp.float32, math.log(0.15), math.log(0.6))), 0.15, 0.6),
        "pool_keys": jnp.clip(jax.random.uniform(key_list[7], (POOL, PAGE, D), jnp.float32, -2.0, 2.0) * levels(key_list[7], (POOL, PAGE, D), ((0, 128), (2, 2)), -0.4, 0.0), -2.0, 2.0).astype(jnp.bfloat16),
        "pool_values": noise(key_list[8], (POOL, PAGE, D), 1.0, 6.0, ((0, 128), (2, 2))),
        "req_len": draw_req_len(jax.random.fold_in(key_list[13], 71), 0),
        "prefix_len": draw_prefix_len(jax.random.fold_in(key_list[13], 71), 0),
        "prefix_pages": draw_prefix_pages(jax.random.fold_in(key_list[13], 71), 0),
        "placement": draw_placement(jax.random.fold_in(key_list[13], 71), 0),
    }


epsilon = 1e-06

def rms_scale(values):
    return values * lax.rsqrt(lax.optimization_barrier(jnp.mean(values * values, axis=-1, keepdims=True)) + epsilon)

def head_normed(projected, head_gain):
    count = projected.shape[0]
    split_heads = projected.reshape(count, -1, HD)
    return (rms_scale(split_heads).reshape(count, -1) * head_gain).astype(jnp.bfloat16)

def reference(hidden_in, w_query, w_key, w_value, w_out, head_gain, eigen_rate, pool_keys, pool_values, req_len, prefix_len, prefix_pages, placement):
    hidden_f = hidden_in.astype(jnp.float32)
    row_scale = lax.rsqrt(lax.optimization_barrier(jnp.mean(hidden_f * hidden_f, axis=-1, keepdims=True)) + epsilon)
    anchor = hidden_f * row_scale
    queries = head_normed(jnp.dot(hidden_in, w_query, preferred_element_type=jnp.float32), head_gain)
    key_rows = head_normed(jnp.dot(hidden_in, w_key, preferred_element_type=jnp.float32), head_gain)
    value_rows = (jnp.dot(hidden_in, w_value, preferred_element_type=jnp.float32) * row_scale).astype(jnp.bfloat16)

    def one_request(items):
        query_block, key_block, value_block, live_count, depth, pages = items
        cached_keys = pool_keys[pages].reshape(PMAX * PAGE, D)
        cached_values = pool_values[pages].reshape(PMAX * PAGE, D)
        all_keys = jnp.concatenate([key_block, cached_keys], axis=0)
        all_values = jnp.concatenate([value_block, cached_values], axis=0)
        row_index = jnp.arange(TOK_DEV, dtype=jnp.int32)[:, None]
        col_index = jnp.arange(TOK_DEV + PMAX * PAGE, dtype=jnp.int32)[None, :]
        own_part = (col_index <= row_index) & (col_index < live_count)
        cached_part = (col_index >= TOK_DEV) & ((col_index - TOK_DEV) // PAGE < depth)
        visible = own_part | cached_part
        query_heads = query_block.astype(jnp.float32).reshape(TOK_DEV, HEADS, HD)
        key_heads = all_keys.astype(jnp.float32).reshape(-1, HEADS, HD)
        value_heads = all_values.astype(jnp.float32).reshape(-1, HEADS, HD)
        scores = jnp.einsum('qhd,khd->hqk', query_heads, key_heads) / math.sqrt(HD)
        weights = jnp.where(visible[None], jnp.exp(scores), 0.0)
        totals = lax.optimization_barrier(jnp.sum(weights, axis=-1))
        rounded = lax.optimization_barrier(weights.astype(jnp.bfloat16)).astype(jnp.float32)
        mixed = jnp.einsum('hqk,khd->qhd', rounded, value_heads)
        return (mixed / totals.T[:, :, None]).astype(jnp.bfloat16).reshape(TOK_DEV, D)
    attended = lax.map(one_request, (queries.reshape(REQS, TOK_DEV, D), key_rows.reshape(REQS, TOK_DEV, D), value_rows.reshape(REQS, TOK_DEV, D), req_len, prefix_len, prefix_pages))
    attended = attended.reshape(TOKENS, D)
    branch = jnp.dot(attended, w_out, preferred_element_type=jnp.float32)
    updated = anchor + eigen_rate * (rms_scale(branch) - anchor)
    layer_out = rms_scale(updated).astype(jnp.bfloat16)
    key_pages = key_rows.reshape(NEWPAGES, PAGE, D)
    value_pages = value_rows.reshape(NEWPAGES, PAGE, D)
    new_keys = jnp.zeros_like(key_pages).at[placement].set(key_pages)
    new_values = jnp.zeros_like(value_pages).at[placement].set(value_pages)
    return (layer_out, new_keys, new_values)
```

```python
import math

import jax
import jax.numpy as jnp
from jax import lax
from jax.sharding import PartitionSpec as P

HD = 64
PAGE = 256
PMAX = 4


epsilon = 1e-06


def from_behind(block, axis, distance):
    devices = range(lax.axis_size(axis))
    route = [((i - distance) % len(devices), i) for i in devices]
    return lax.ppermute(block, axis, route)


def rms_scale(values):
    return values * lax.rsqrt(jnp.mean(values * values, axis=-1, keepdims=True) + epsilon)


def head_normed(projected, head_gain):
    count = projected.shape[0]
    split_heads = projected.reshape(count, -1, HD)
    return (rms_scale(split_heads).reshape(count, -1) * head_gain).astype(jnp.bfloat16)


def attend(query_heads, key_rows, value_rows, visible):
    key_heads = key_rows.reshape(key_rows.shape[0], -1, HD)
    value_heads = value_rows.reshape(value_rows.shape[0], -1, HD)
    scores = jnp.einsum(
        "qhd,khd->hqk", query_heads, key_heads, preferred_element_type=jnp.float32
    ) / math.sqrt(HD)
    weights = jnp.where(visible, jnp.exp(scores), 0.0)
    totals = jnp.sum(weights, axis=-1)
    mixed = jnp.einsum(
        "hqk,khd->qhd",
        weights.astype(jnp.bfloat16),
        value_heads,
        preferred_element_type=jnp.float32,
    )
    return (totals, mixed)


def in_kv_order(mine, other, axis):
    first = lax.axis_index("kv") == 0
    low = jnp.where(first, mine, other)
    high = jnp.where(first, other, mine)
    return jnp.concatenate([low, high], axis=axis)


def fetch_page(pool_keys, pool_values, prefix_pages, slot_index):
    devices = lax.axis_size("blk")
    here = lax.axis_index("blk")
    offset = slot_index * devices // PMAX + 1
    asker = (here - offset) % devices
    local = prefix_pages[asker, slot_index] % pool_keys.shape[0]
    send_keys = lax.dynamic_index_in_dim(pool_keys, local, 0, keepdims=False)
    send_values = lax.dynamic_index_in_dim(pool_values, local, 0, keepdims=False)
    return from_behind((send_keys, send_values), "blk", devices - offset)


def relay(key_rows, value_rows, placement):
    devices = lax.axis_size("blk")
    here = lax.axis_index("blk")
    blocks = key_rows.shape[0] // PAGE
    width = key_rows.shape[1]
    key_pages = key_rows.reshape(blocks, PAGE, width)
    value_pages = value_rows.reshape(blocks, PAGE, width)
    key_out = jnp.zeros_like(key_pages)
    value_out = jnp.zeros_like(value_pages)
    for block_index in range(blocks):
        offset = (2 * block_index + 1) * devices // (2 * blocks)
        key_recv, value_recv = from_behind(
            (key_pages[block_index], value_pages[block_index]), "blk", offset
        )
        source = (here - offset) % devices
        target = placement[source * blocks + block_index] % blocks
        key_out = lax.dynamic_update_index_in_dim(key_out, key_recv, target, 0)
        value_out = lax.dynamic_update_index_in_dim(value_out, value_recv, target, 0)
    return (key_out, value_out)


def body(
    hidden_in,
    w_query,
    w_key,
    w_value,
    w_out,
    head_gain,
    eigen_rate,
    pool_keys,
    pool_values,
    req_len,
    prefix_len,
    prefix_pages,
    placement,
):
    tokens_here = hidden_in.shape[0]
    other_w_out = from_behind(w_out, "kv", 1)
    width_half = w_query.shape[1]
    heads_here = width_half // HD
    hidden_f = hidden_in.astype(jnp.float32)
    row_scale = lax.rsqrt(jnp.mean(hidden_f * hidden_f, axis=-1, keepdims=True) + epsilon)
    anchor = hidden_f * row_scale
    queries = head_normed(
        jnp.dot(hidden_in, w_query, preferred_element_type=jnp.float32), head_gain
    )
    key_rows = head_normed(jnp.dot(hidden_in, w_key, preferred_element_type=jnp.float32), head_gain)
    value_rows = (
        jnp.dot(hidden_in, w_value, preferred_element_type=jnp.float32) * row_scale
    ).astype(jnp.bfloat16)
    live_count = req_len[0]
    depth = prefix_len[0]
    query_heads = queries.reshape(tokens_here, heads_here, HD)
    row_index = jnp.arange(tokens_here, dtype=jnp.int32)[:, None]
    col_index = jnp.arange(tokens_here, dtype=jnp.int32)[None, :]
    own_visible = ((col_index <= row_index) & (col_index < live_count))[None]
    totals, mixed = attend(query_heads, key_rows, value_rows, own_visible)
    fetched_keys = []
    fetched_values = []
    for slot_index in range(PMAX):
        page_keys, page_values = fetch_page(pool_keys, pool_values, prefix_pages, slot_index)
        fetched_keys.append(page_keys)
        fetched_values.append(page_values)
    cached_keys = jnp.concatenate(fetched_keys, axis=0)
    cached_values = jnp.concatenate(fetched_values, axis=0)
    page_number = jnp.arange(cached_keys.shape[0], dtype=jnp.int32) // PAGE
    cached_visible = (page_number < depth)[None, None, :]
    more_totals, more_mixed = attend(query_heads, cached_keys, cached_values, cached_visible)
    totals = totals + more_totals
    mixed = mixed + more_mixed
    attended = (mixed / totals.T[:, :, None]).astype(jnp.bfloat16).reshape(tokens_here, width_half)
    other_attended = from_behind(attended, "kv", 1)
    branch = jnp.dot(
        in_kv_order(attended, other_attended, 1),
        in_kv_order(w_out, other_w_out, 0),
        preferred_element_type=jnp.float32,
    )
    updated = anchor + eigen_rate * (rms_scale(branch) - anchor)
    layer_out = rms_scale(updated).astype(jnp.bfloat16)
    new_keys, new_values = relay(key_rows, value_rows, placement)
    return (layer_out, new_keys, new_values)


def solution(mesh):
    in_specs = (
        P("blk", None),
        P(None, "kv"),
        P(None, "kv"),
        P(None, "kv"),
        P("kv", None),
        P("kv"),
        P(),
        P("blk", None, "kv"),
        P("blk", None, "kv"),
        P("blk"),
        P("blk"),
        P(),
        P(),
    )
    out_specs = (P("blk", None), P("blk", None, "kv"), P("blk", None, "kv"))
    return jax.shard_map(body, mesh=mesh, in_specs=in_specs, out_specs=out_specs, check_vma=False)
```

```python
import math

import jax
import jax.numpy as jnp
from jax import lax
from jax.experimental import pallas as pl
from jax.experimental.pallas import tpu as pltpu
from jax.sharding import PartitionSpec as P

HD = 64
PAGE = 256
PMAX = 4


epsilon = 1e-06


def from_behind(block, axis, distance):
    devices = range(lax.axis_size(axis))
    route = [((i - distance) % len(devices), i) for i in devices]
    return lax.ppermute(block, axis, route)


def rms_scale(values):
    return values * lax.rsqrt(jnp.mean(values * values, axis=-1, keepdims=True) + epsilon)


def head_normed(projected, head_gain):
    count = projected.shape[0]
    split_heads = projected.reshape(count, -1, HD)
    return (rms_scale(split_heads).reshape(count, -1) * head_gain).astype(jnp.bfloat16)


def attend(query_heads, key_rows, value_rows, visible):
    key_heads = key_rows.reshape(key_rows.shape[0], -1, HD)
    value_heads = value_rows.reshape(value_rows.shape[0], -1, HD)
    scores = jnp.einsum(
        "qhd,khd->hqk", query_heads, key_heads, preferred_element_type=jnp.float32
    ) / math.sqrt(HD)
    weights = jnp.where(visible, jnp.exp(scores), 0.0)
    totals = jnp.sum(weights, axis=-1)
    mixed = jnp.einsum(
        "hqk,khd->qhd",
        weights.astype(jnp.bfloat16),
        value_heads,
        preferred_element_type=jnp.float32,
    )
    return (totals, mixed)


def in_kv_order(mine, other, axis):
    first = lax.axis_index("kv") == 0
    low = jnp.where(first, mine, other)
    high = jnp.where(first, other, mine)
    return jnp.concatenate([low, high], axis=axis)


def attention_kernel(live_ref, depth_ref, q_ref, k_ref, v_ref, *refs):
    page_refs, out_ref = refs[:-1], refs[-1]
    tile = q_ref.shape[0]
    own = k_ref.shape[0]
    live = live_ref[0]
    depth = depth_ref[0]
    query = q_ref[...]
    lane = lax.broadcasted_iota(jnp.int32, query.shape, 1)
    first = lane < HD
    row = pl.program_id(1) * tile + lax.broadcasted_iota(jnp.int32, (tile, own), 0)
    col = lax.broadcasted_iota(jnp.int32, (tile, own), 1)
    own_visible = (col <= row) & (col < live)
    contract = (((1,), (1,)), ((), ()))
    results = []
    for in_head in (first, jnp.logical_not(first)):
        query_head = jnp.where(in_head, query, jnp.zeros_like(query))
        scores = lax.dot_general(
            query_head, k_ref[...], contract, preferred_element_type=jnp.float32
        ) * (1.0 / math.sqrt(HD))
        weights = jnp.where(own_visible, jnp.exp(scores), 0.0)
        total = jnp.sum(weights, axis=1, keepdims=True)
        mixed = jnp.dot(
            weights.astype(jnp.bfloat16), v_ref[...], preferred_element_type=jnp.float32
        )
        for page in range(PMAX):
            key_page = page_refs[page]
            value_page = page_refs[PMAX + page]
            scores = lax.dot_general(
                query_head, key_page[...], contract, preferred_element_type=jnp.float32
            ) * (1.0 / math.sqrt(HD))
            weights = jnp.where(page < depth, jnp.exp(scores), 0.0)
            total = total + jnp.sum(weights, axis=1, keepdims=True)
            mixed = mixed + jnp.dot(
                weights.astype(jnp.bfloat16), value_page[...], preferred_element_type=jnp.float32
            )
        results.append(mixed / total)
    out_ref[...] = jnp.where(first, results[0], results[1]).astype(out_ref.dtype)


def attention(queries, key_rows, value_rows, page_keys, page_values, req_len, prefix_len):
    tokens, width = queries.shape
    tile = 128
    lanes = 2 * HD
    grid = (width // lanes, tokens // tile)
    own_spec = pl.BlockSpec((tokens, lanes), lambda h, t, *_: (0, h))
    page_spec = pl.BlockSpec((PAGE, lanes), lambda h, t, *_: (0, h))
    tile_spec = pl.BlockSpec((tile, lanes), lambda h, t, *_: (t, h))
    grid_spec = pltpu.PrefetchScalarGridSpec(
        num_scalar_prefetch=2,
        grid=grid,
        in_specs=[tile_spec, own_spec, own_spec] + [page_spec] * (2 * PMAX),
        out_specs=tile_spec,
    )
    return pl.pallas_call(
        attention_kernel,
        out_shape=jax.ShapeDtypeStruct((tokens, width), jnp.bfloat16),
        grid_spec=grid_spec,
    )(req_len, prefix_len, queries, key_rows, value_rows, *page_keys, *page_values)


def fetch_page(pool_keys, pool_values, prefix_pages, slot_index):
    devices = lax.axis_size("blk")
    here = lax.axis_index("blk")
    offset = slot_index * devices // PMAX + 1
    asker = (here - offset) % devices
    local = prefix_pages[asker, slot_index] % pool_keys.shape[0]
    send_keys = lax.dynamic_index_in_dim(pool_keys, local, 0, keepdims=False)
    send_values = lax.dynamic_index_in_dim(pool_values, local, 0, keepdims=False)
    return from_behind((send_keys, send_values), "blk", devices - offset)


def relay(key_rows, value_rows, placement):
    devices = lax.axis_size("blk")
    here = lax.axis_index("blk")
    blocks = key_rows.shape[0] // PAGE
    width = key_rows.shape[1]
    key_pages = key_rows.reshape(blocks, PAGE, width)
    value_pages = value_rows.reshape(blocks, PAGE, width)
    key_out = jnp.zeros_like(key_pages)
    value_out = jnp.zeros_like(value_pages)
    for block_index in range(blocks):
        offset = (2 * block_index + 1) * devices // (2 * blocks)
        key_recv, value_recv = from_behind(
            (key_pages[block_index], value_pages[block_index]), "blk", offset
        )
        source = (here - offset) % devices
        target = placement[source * blocks + block_index] % blocks
        key_out = lax.dynamic_update_index_in_dim(key_out, key_recv, target, 0)
        value_out = lax.dynamic_update_index_in_dim(value_out, value_recv, target, 0)
    return (key_out, value_out)


def body(
    hidden_in,
    w_query,
    w_key,
    w_value,
    w_out,
    head_gain,
    eigen_rate,
    pool_keys,
    pool_values,
    req_len,
    prefix_len,
    prefix_pages,
    placement,
):
    tokens_here = hidden_in.shape[0]
    other_w_out = from_behind(w_out, "kv", 1)
    width_half = w_query.shape[1]
    heads_here = width_half // HD
    hidden_f = hidden_in.astype(jnp.float32)
    row_scale = lax.rsqrt(jnp.mean(hidden_f * hidden_f, axis=-1, keepdims=True) + epsilon)
    anchor = hidden_f * row_scale
    queries = head_normed(
        jnp.dot(hidden_in, w_query, preferred_element_type=jnp.float32), head_gain
    )
    key_rows = head_normed(jnp.dot(hidden_in, w_key, preferred_element_type=jnp.float32), head_gain)
    value_rows = (
        jnp.dot(hidden_in, w_value, preferred_element_type=jnp.float32) * row_scale
    ).astype(jnp.bfloat16)
    fetched_keys = []
    fetched_values = []
    for slot_index in range(PMAX):
        page_keys, page_values = fetch_page(pool_keys, pool_values, prefix_pages, slot_index)
        fetched_keys.append(page_keys)
        fetched_values.append(page_values)
    attended = attention(
        queries, key_rows, value_rows, fetched_keys, fetched_values, req_len, prefix_len
    )
    other_attended = from_behind(attended, "kv", 1)
    branch = jnp.dot(
        in_kv_order(attended, other_attended, 1),
        in_kv_order(w_out, other_w_out, 0),
        preferred_element_type=jnp.float32,
    )
    updated = anchor + eigen_rate * (rms_scale(branch) - anchor)
    layer_out = rms_scale(updated).astype(jnp.bfloat16)
    new_keys, new_values = relay(key_rows, value_rows, placement)
    return (layer_out, new_keys, new_values)


def solution(mesh):
    in_specs = (
        P("blk", None),
        P(None, "kv"),
        P(None, "kv"),
        P(None, "kv"),
        P("kv", None),
        P("kv"),
        P(),
        P("blk", None, "kv"),
        P("blk", None, "kv"),
        P("blk"),
        P("blk"),
        P(),
        P(),
    )
    out_specs = (P("blk", None), P("blk", None, "kv"), P("blk", None, "kv"))
    return jax.shard_map(body, mesh=mesh, in_specs=in_specs, out_specs=out_specs, check_vma=False)
```

```python
import math

import jax
import jax.numpy as jnp
from jax import lax
from jax.experimental import pallas as pl
from jax.experimental.pallas import tpu as pltpu
from jax.sharding import PartitionSpec as P

HD = 64
PAGE = 256
PMAX = 4


epsilon = 1e-06


def from_behind(block, axis, distance):
    devices = range(lax.axis_size(axis))
    route = [((i - distance) % len(devices), i) for i in devices]
    return lax.ppermute(block, axis, route)


def rms_scale(values):
    return values * lax.rsqrt(jnp.mean(values * values, axis=-1, keepdims=True) + epsilon)


def head_normed(projected, head_gain):
    count = projected.shape[0]
    split_heads = projected.reshape(count, -1, HD)
    return (rms_scale(split_heads).reshape(count, -1) * head_gain).astype(jnp.bfloat16)


def attend(query_heads, key_rows, value_rows, visible):
    key_heads = key_rows.reshape(key_rows.shape[0], -1, HD)
    value_heads = value_rows.reshape(value_rows.shape[0], -1, HD)
    scores = jnp.einsum(
        "qhd,khd->hqk", query_heads, key_heads, preferred_element_type=jnp.float32
    ) / math.sqrt(HD)
    weights = jnp.where(visible, jnp.exp(scores), 0.0)
    totals = jnp.sum(weights, axis=-1)
    mixed = jnp.einsum(
        "hqk,khd->qhd",
        weights.astype(jnp.bfloat16),
        value_heads,
        preferred_element_type=jnp.float32,
    )
    return (totals, mixed)


def in_kv_order(mine, other, axis):
    first = lax.axis_index("kv") == 0
    low = jnp.where(first, mine, other)
    high = jnp.where(first, other, mine)
    return jnp.concatenate([low, high], axis=axis)


def attention_kernel(live_ref, depth_ref, q_ref, k_ref, v_ref, *refs):
    page_refs = refs[: 2 * PMAX]
    out_ref, other_ref, held, send_sems, recv_sems = refs[2 * PMAX :]
    tile, lanes = q_ref.shape
    own = k_ref.shape[0]
    h, t = pl.program_id(0), pl.program_id(1)
    tiles_down = pl.num_programs(1)
    steps = pl.num_programs(0) * tiles_down
    step = h * tiles_down + t
    partner = (1 - lax.axis_index("kv"), lax.axis_index("blk"))

    @pl.when(step == 0)
    def _():
        barrier = pltpu.get_barrier_semaphore()
        pl.semaphore_signal(barrier, inc=1, device_id=partner, device_id_type=pl.DeviceIdType.MESH)
        pl.semaphore_wait(barrier, 1)

    def tile_copy(index):
        rows = pl.ds(pl.multiple_of((index % tiles_down) * tile, tile), tile)
        cols = pl.ds(pl.multiple_of((index // tiles_down) * lanes, lanes), lanes)
        return pltpu.make_async_remote_copy(
            src_ref=held.at[index % 2],
            dst_ref=other_ref.at[rows, cols],
            send_sem=send_sems.at[index],
            recv_sem=recv_sems.at[index],
            device_id=partner,
            device_id_type=pl.DeviceIdType.MESH,
        )

    live = live_ref[0]
    depth = depth_ref[0]
    query = q_ref[...]
    lane = lax.broadcasted_iota(jnp.int32, query.shape, 1)
    first = lane < HD
    row = t * tile + lax.broadcasted_iota(jnp.int32, (tile, own), 0)
    col = lax.broadcasted_iota(jnp.int32, (tile, own), 1)
    own_visible = (col <= row) & (col < live)
    contract = (((1,), (1,)), ((), ()))
    results = []
    for in_head in (first, jnp.logical_not(first)):
        query_head = jnp.where(in_head, query, jnp.zeros_like(query))
        scores = lax.dot_general(
            query_head, k_ref[...], contract, preferred_element_type=jnp.float32
        ) * (1.0 / math.sqrt(HD))
        weights = jnp.where(own_visible, jnp.exp(scores), 0.0)
        total = jnp.sum(weights, axis=1, keepdims=True)
        mixed = jnp.dot(
            weights.astype(jnp.bfloat16), v_ref[...], preferred_element_type=jnp.float32
        )
        for page in range(PMAX):
            key_page = page_refs[page]
            value_page = page_refs[PMAX + page]
            scores = lax.dot_general(
                query_head, key_page[...], contract, preferred_element_type=jnp.float32
            ) * (1.0 / math.sqrt(HD))
            weights = jnp.where(page < depth, jnp.exp(scores), 0.0)
            total = total + jnp.sum(weights, axis=1, keepdims=True)
            mixed = mixed + jnp.dot(
                weights.astype(jnp.bfloat16), value_page[...], preferred_element_type=jnp.float32
            )
        results.append(mixed / total)
    result = jnp.where(first, results[0], results[1]).astype(out_ref.dtype)
    out_ref[...] = result

    @pl.when(step >= 2)
    def _():
        tile_copy(step - 2).wait_send()

    held[step % 2] = result
    tile_copy(step).start()

    @pl.when(step == steps - 1)
    def _():
        tile_copy(step - 1).wait_send()
        tile_copy(step).wait_send()

        def drain(index, carry):
            tile_copy(index).wait_recv()
            return carry

        lax.fori_loop(0, steps, drain, 0)


def attention(queries, key_rows, value_rows, page_keys, page_values, req_len, prefix_len):
    tokens, width = queries.shape
    tile = 128
    lanes = 2 * HD
    grid = (width // lanes, tokens // tile)
    steps = grid[0] * grid[1]
    own_spec = pl.BlockSpec((tokens, lanes), lambda h, t, *_: (0, h))
    page_spec = pl.BlockSpec((PAGE, lanes), lambda h, t, *_: (0, h))
    tile_spec = pl.BlockSpec((tile, lanes), lambda h, t, *_: (t, h))
    grid_spec = pltpu.PrefetchScalarGridSpec(
        num_scalar_prefetch=2,
        grid=grid,
        in_specs=[tile_spec, own_spec, own_spec] + [page_spec] * (2 * PMAX),
        out_specs=[tile_spec, pl.BlockSpec(memory_space=pl.ANY)],
        scratch_shapes=[
            pltpu.VMEM((2, tile, lanes), jnp.bfloat16),
            pltpu.SemaphoreType.DMA((steps,)),
            pltpu.SemaphoreType.DMA((steps,)),
        ],
    )
    shape = jax.ShapeDtypeStruct((tokens, width), jnp.bfloat16)
    return pl.pallas_call(
        attention_kernel,
        out_shape=(shape, shape),
        grid_spec=grid_spec,
        compiler_params=pltpu.CompilerParams(
            collective_id=0,
            has_side_effects=True,
            dimension_semantics=("arbitrary", "arbitrary"),
        ),
    )(req_len, prefix_len, queries, key_rows, value_rows, *page_keys, *page_values)


def fetch_page(pool_keys, pool_values, prefix_pages, slot_index):
    devices = lax.axis_size("blk")
    here = lax.axis_index("blk")
    offset = slot_index * devices // PMAX + 1
    asker = (here - offset) % devices
    local = prefix_pages[asker, slot_index] % pool_keys.shape[0]
    send_keys = lax.dynamic_index_in_dim(pool_keys, local, 0, keepdims=False)
    send_values = lax.dynamic_index_in_dim(pool_values, local, 0, keepdims=False)
    return from_behind((send_keys, send_values), "blk", devices - offset)


def relay(key_rows, value_rows, placement):
    devices = lax.axis_size("blk")
    here = lax.axis_index("blk")
    blocks = key_rows.shape[0] // PAGE
    width = key_rows.shape[1]
    key_pages = key_rows.reshape(blocks, PAGE, width)
    value_pages = value_rows.reshape(blocks, PAGE, width)
    key_out = jnp.zeros_like(key_pages)
    value_out = jnp.zeros_like(value_pages)
    for block_index in range(blocks):
        offset = (2 * block_index + 1) * devices // (2 * blocks)
        key_recv, value_recv = from_behind(
            (key_pages[block_index], value_pages[block_index]), "blk", offset
        )
        source = (here - offset) % devices
        target = placement[source * blocks + block_index] % blocks
        key_out = lax.dynamic_update_index_in_dim(key_out, key_recv, target, 0)
        value_out = lax.dynamic_update_index_in_dim(value_out, value_recv, target, 0)
    return (key_out, value_out)


def body(
    hidden_in,
    w_query,
    w_key,
    w_value,
    w_out,
    head_gain,
    eigen_rate,
    pool_keys,
    pool_values,
    req_len,
    prefix_len,
    prefix_pages,
    placement,
):
    tokens_here = hidden_in.shape[0]
    other_w_out = from_behind(w_out, "kv", 1)
    width_half = w_query.shape[1]
    heads_here = width_half // HD
    hidden_f = hidden_in.astype(jnp.float32)
    row_scale = lax.rsqrt(jnp.mean(hidden_f * hidden_f, axis=-1, keepdims=True) + epsilon)
    anchor = hidden_f * row_scale
    queries = head_normed(
        jnp.dot(hidden_in, w_query, preferred_element_type=jnp.float32), head_gain
    )
    key_rows = head_normed(jnp.dot(hidden_in, w_key, preferred_element_type=jnp.float32), head_gain)
    value_rows = (
        jnp.dot(hidden_in, w_value, preferred_element_type=jnp.float32) * row_scale
    ).astype(jnp.bfloat16)
    fetched_keys = []
    fetched_values = []
    for slot_index in range(PMAX):
        page_keys, page_values = fetch_page(pool_keys, pool_values, prefix_pages, slot_index)
        fetched_keys.append(page_keys)
        fetched_values.append(page_values)
    attended, other_attended = attention(
        queries, key_rows, value_rows, fetched_keys, fetched_values, req_len, prefix_len
    )
    branch = jnp.dot(
        in_kv_order(attended, other_attended, 1),
        in_kv_order(w_out, other_w_out, 0),
        preferred_element_type=jnp.float32,
    )
    updated = anchor + eigen_rate * (rms_scale(branch) - anchor)
    layer_out = rms_scale(updated).astype(jnp.bfloat16)
    new_keys, new_values = relay(key_rows, value_rows, placement)
    return (layer_out, new_keys, new_values)


def solution(mesh):
    in_specs = (
        P("blk", None),
        P(None, "kv"),
        P(None, "kv"),
        P(None, "kv"),
        P("kv", None),
        P("kv"),
        P(),
        P("blk", None, "kv"),
        P("blk", None, "kv"),
        P("blk"),
        P("blk"),
        P(),
        P(),
    )
    out_specs = (P("blk", None), P("blk", None, "kv"), P("blk", None, "kv"))
    return jax.shard_map(body, mesh=mesh, in_specs=in_specs, out_specs=out_specs, check_vma=False)
```

```python
import math

import jax
import jax.numpy as jnp
from jax import lax
from jax.experimental import pallas as pl
from jax.experimental.pallas import tpu as pltpu
from jax.sharding import PartitionSpec as P

HD = 64
PAGE = 256
PMAX = 4


epsilon = 1e-06


def from_behind(block, axis, distance):
    devices = range(lax.axis_size(axis))
    route = [((i - distance) % len(devices), i) for i in devices]
    return lax.ppermute(block, axis, route)


def rms_scale(values):
    return values * lax.rsqrt(jnp.mean(values * values, axis=-1, keepdims=True) + epsilon)


def head_normed(projected, head_gain):
    count = projected.shape[0]
    split_heads = projected.reshape(count, -1, HD)
    return (rms_scale(split_heads).reshape(count, -1) * head_gain).astype(jnp.bfloat16)


def attend(query_heads, key_rows, value_rows, visible):
    key_heads = key_rows.reshape(key_rows.shape[0], -1, HD)
    value_heads = value_rows.reshape(value_rows.shape[0], -1, HD)
    scores = jnp.einsum(
        "qhd,khd->hqk", query_heads, key_heads, preferred_element_type=jnp.float32
    ) / math.sqrt(HD)
    weights = jnp.where(visible, jnp.exp(scores), 0.0)
    totals = jnp.sum(weights, axis=-1)
    mixed = jnp.einsum(
        "hqk,khd->qhd",
        weights.astype(jnp.bfloat16),
        value_heads,
        preferred_element_type=jnp.float32,
    )
    return (totals, mixed)


def in_kv_order(mine, other, axis):
    first = lax.axis_index("kv") == 0
    low = jnp.where(first, mine, other)
    high = jnp.where(first, other, mine)
    return jnp.concatenate([low, high], axis=axis)


def attention_kernel(live_ref, depth_ref, q_ref, k_ref, v_ref, *refs):
    page_refs, out_ref = refs[:-1], refs[-1]
    tile = q_ref.shape[0]
    own = k_ref.shape[0]
    live = live_ref[0]
    depth = depth_ref[0]
    query = q_ref[...]
    lane = lax.broadcasted_iota(jnp.int32, query.shape, 1)
    first = lane < HD
    row = pl.program_id(1) * tile + lax.broadcasted_iota(jnp.int32, (tile, own), 0)
    col = lax.broadcasted_iota(jnp.int32, (tile, own), 1)
    own_visible = (col <= row) & (col < live)
    contract = (((1,), (1,)), ((), ()))
    results = []
    for in_head in (first, jnp.logical_not(first)):
        query_head = jnp.where(in_head, query, jnp.zeros_like(query))
        scores = lax.dot_general(
            query_head, k_ref[...], contract, preferred_element_type=jnp.float32
        ) * (1.0 / math.sqrt(HD))
        weights = jnp.where(own_visible, jnp.exp(scores), 0.0)
        total = jnp.sum(weights, axis=1, keepdims=True)
        mixed = jnp.dot(
            weights.astype(jnp.bfloat16), v_ref[...], preferred_element_type=jnp.float32
        )
        for page in range(PMAX):
            key_page = page_refs[page]
            value_page = page_refs[PMAX + page]
            scores = lax.dot_general(
                query_head, key_page[...], contract, preferred_element_type=jnp.float32
            ) * (1.0 / math.sqrt(HD))
            weights = jnp.where(page < depth, jnp.exp(scores), 0.0)
            total = total + jnp.sum(weights, axis=1, keepdims=True)
            mixed = mixed + jnp.dot(
                weights.astype(jnp.bfloat16), value_page[...], preferred_element_type=jnp.float32
            )
        results.append(mixed / total)
    out_ref[...] = jnp.where(first, results[0], results[1]).astype(out_ref.dtype)


def attention(queries, key_rows, value_rows, pages, req_len, prefix_len):
    tokens, width = queries.shape
    tile = 128
    lanes = 2 * HD
    grid = (width // lanes, tokens // tile)
    own_spec = pl.BlockSpec((tokens, lanes), lambda h, t, *_: (0, h))
    key_spec = pl.BlockSpec((None, PAGE, lanes), lambda h, t, *_: (0, 0, h))
    value_spec = pl.BlockSpec((None, PAGE, lanes), lambda h, t, *_: (1, 0, h))
    tile_spec = pl.BlockSpec((tile, lanes), lambda h, t, *_: (t, h))
    grid_spec = pltpu.PrefetchScalarGridSpec(
        num_scalar_prefetch=2,
        grid=grid,
        in_specs=[tile_spec, own_spec, own_spec] + [key_spec] * PMAX + [value_spec] * PMAX,
        out_specs=tile_spec,
    )
    return pl.pallas_call(
        attention_kernel,
        out_shape=jax.ShapeDtypeStruct((tokens, width), jnp.bfloat16),
        grid_spec=grid_spec,
    )(req_len, prefix_len, queries, key_rows, value_rows, *pages, *pages)


def fetch_page(pool_keys, pool_values, prefix_pages, slot_index):
    devices = lax.axis_size("blk")
    here = lax.axis_index("blk")
    offset = slot_index * devices // PMAX + 1
    asker = (here - offset) % devices
    local = prefix_pages[asker, slot_index] % pool_keys.shape[0]
    send_keys = lax.dynamic_index_in_dim(pool_keys, local, 0, keepdims=False)
    send_values = lax.dynamic_index_in_dim(pool_values, local, 0, keepdims=False)
    return from_behind(jnp.stack([send_keys, send_values]), "blk", devices - offset)


def relay(key_rows, value_rows, placement):
    devices = lax.axis_size("blk")
    here = lax.axis_index("blk")
    blocks = key_rows.shape[0] // PAGE
    width = key_rows.shape[1]
    key_pages = key_rows.reshape(blocks, PAGE, width)
    value_pages = value_rows.reshape(blocks, PAGE, width)
    key_out = jnp.zeros_like(key_pages)
    value_out = jnp.zeros_like(value_pages)
    for block_index in range(blocks):
        offset = (2 * block_index + 1) * devices // (2 * blocks)
        received = from_behind(
            jnp.stack([key_pages[block_index], value_pages[block_index]]), "blk", offset
        )
        source = (here - offset) % devices
        target = placement[source * blocks + block_index] % blocks
        key_out = lax.dynamic_update_index_in_dim(key_out, received[0], target, 0)
        value_out = lax.dynamic_update_index_in_dim(value_out, received[1], target, 0)
    return (key_out, value_out)


def body(
    hidden_in,
    w_query,
    w_key,
    w_value,
    w_out,
    head_gain,
    eigen_rate,
    pool_keys,
    pool_values,
    req_len,
    prefix_len,
    prefix_pages,
    placement,
):
    tokens_here = hidden_in.shape[0]
    other_w_out = from_behind(w_out, "kv", 1)
    width_half = w_query.shape[1]
    heads_here = width_half // HD
    hidden_f = hidden_in.astype(jnp.float32)
    row_scale = lax.rsqrt(jnp.mean(hidden_f * hidden_f, axis=-1, keepdims=True) + epsilon)
    anchor = hidden_f * row_scale
    queries = head_normed(
        jnp.dot(hidden_in, w_query, preferred_element_type=jnp.float32), head_gain
    )
    key_rows = head_normed(jnp.dot(hidden_in, w_key, preferred_element_type=jnp.float32), head_gain)
    value_rows = (
        jnp.dot(hidden_in, w_value, preferred_element_type=jnp.float32) * row_scale
    ).astype(jnp.bfloat16)
    fetched = [
        fetch_page(pool_keys, pool_values, prefix_pages, slot_index) for slot_index in range(PMAX)
    ]
    key_rows, value_rows, fetched = lax.optimization_barrier((key_rows, value_rows, fetched))
    attended = attention(queries, key_rows, value_rows, fetched, req_len, prefix_len)
    other_attended = from_behind(attended, "kv", 1)
    branch = jnp.dot(
        in_kv_order(attended, other_attended, 1),
        in_kv_order(w_out, other_w_out, 0),
        preferred_element_type=jnp.float32,
    )
    updated = anchor + eigen_rate * (rms_scale(branch) - anchor)
    layer_out = rms_scale(updated).astype(jnp.bfloat16)
    new_keys, new_values = relay(key_rows, value_rows, placement)
    return (layer_out, new_keys, new_values)


def solution(mesh):
    in_specs = (
        P("blk", None),
        P(None, "kv"),
        P(None, "kv"),
        P(None, "kv"),
        P("kv", None),
        P("kv"),
        P(),
        P("blk", None, "kv"),
        P("blk", None, "kv"),
        P("blk"),
        P("blk"),
        P(),
        P(),
    )
    out_specs = (P("blk", None), P("blk", None, "kv"), P("blk", None, "kv"))
    return jax.shard_map(body, mesh=mesh, in_specs=in_specs, out_specs=out_specs, check_vma=False)
```

```python
import math

import jax
import jax.numpy as jnp
from jax import lax
from jax.experimental import pallas as pl
from jax.experimental.pallas import tpu as pltpu
from jax.sharding import PartitionSpec as P

HD = 64
PAGE = 256
PMAX = 4


epsilon = 1e-06


def from_behind(block, axis, distance):
    devices = range(lax.axis_size(axis))
    route = [((i - distance) % len(devices), i) for i in devices]
    return lax.ppermute(block, axis, route)


def rms_scale(values):
    return values * lax.rsqrt(jnp.mean(values * values, axis=-1, keepdims=True) + epsilon)


def head_normed(projected, head_gain):
    count = projected.shape[0]
    split_heads = projected.reshape(count, -1, HD)
    return (rms_scale(split_heads).reshape(count, -1) * head_gain).astype(jnp.bfloat16)


def attend(query_heads, key_rows, value_rows, visible):
    key_heads = key_rows.reshape(key_rows.shape[0], -1, HD)
    value_heads = value_rows.reshape(value_rows.shape[0], -1, HD)
    scores = jnp.einsum(
        "qhd,khd->hqk", query_heads, key_heads, preferred_element_type=jnp.float32
    ) / math.sqrt(HD)
    weights = jnp.where(visible, jnp.exp(scores), 0.0)
    totals = jnp.sum(weights, axis=-1)
    mixed = jnp.einsum(
        "hqk,khd->qhd",
        weights.astype(jnp.bfloat16),
        value_heads,
        preferred_element_type=jnp.float32,
    )
    return (totals, mixed)


def in_kv_order(mine, other, axis):
    first = lax.axis_index("kv") == 0
    low = jnp.where(first, mine, other)
    high = jnp.where(first, other, mine)
    return jnp.concatenate([low, high], axis=axis)


def attention_kernel(live_ref, depth_ref, q_ref, k_ref, v_ref, *refs):
    page_refs, out_ref = refs[:-1], refs[-1]
    tile = q_ref.shape[0]
    own = k_ref.shape[0]
    live = live_ref[0]
    depth = depth_ref[0]
    query = q_ref[...]
    lane = lax.broadcasted_iota(jnp.int32, query.shape, 1)
    first = lane < HD
    row = pl.program_id(1) * tile + lax.broadcasted_iota(jnp.int32, (tile, own), 0)
    col = lax.broadcasted_iota(jnp.int32, (tile, own), 1)
    own_visible = (col <= row) & (col < live)
    contract = (((1,), (1,)), ((), ()))
    results = []
    for in_head in (first, jnp.logical_not(first)):
        query_head = jnp.where(in_head, query, jnp.zeros_like(query))
        scores = lax.dot_general(
            query_head, k_ref[...], contract, preferred_element_type=jnp.float32
        ) * (1.0 / math.sqrt(HD))
        weights = jnp.where(own_visible, jnp.exp(scores), 0.0)
        total = jnp.sum(weights, axis=1, keepdims=True)
        mixed = jnp.dot(
            weights.astype(jnp.bfloat16), v_ref[...], preferred_element_type=jnp.float32
        )
        for page in range(PMAX):
            key_page = page_refs[page]
            value_page = page_refs[PMAX + page]
            scores = lax.dot_general(
                query_head, key_page[...], contract, preferred_element_type=jnp.float32
            ) * (1.0 / math.sqrt(HD))
            weights = jnp.where(page < depth, jnp.exp(scores), 0.0)
            total = total + jnp.sum(weights, axis=1, keepdims=True)
            mixed = mixed + jnp.dot(
                weights.astype(jnp.bfloat16), value_page[...], preferred_element_type=jnp.float32
            )
        results.append(mixed / total)
    out_ref[...] = jnp.where(first, results[0], results[1]).astype(out_ref.dtype)


def attention(queries, key_rows, value_rows, pages, req_len, prefix_len):
    tokens, width = queries.shape
    tile = 128
    lanes = 2 * HD
    grid = (width // lanes, tokens // tile)
    own_spec = pl.BlockSpec((tokens, lanes), lambda h, t, *_: (0, h))
    key_spec = pl.BlockSpec((None, PAGE, lanes), lambda h, t, *_: (0, 0, h))
    value_spec = pl.BlockSpec((None, PAGE, lanes), lambda h, t, *_: (1, 0, h))
    tile_spec = pl.BlockSpec((tile, lanes), lambda h, t, *_: (t, h))
    grid_spec = pltpu.PrefetchScalarGridSpec(
        num_scalar_prefetch=2,
        grid=grid,
        in_specs=[tile_spec, own_spec, own_spec] + [key_spec] * PMAX + [value_spec] * PMAX,
        out_specs=tile_spec,
    )
    return pl.pallas_call(
        attention_kernel,
        out_shape=jax.ShapeDtypeStruct((tokens, width), jnp.bfloat16),
        grid_spec=grid_spec,
    )(req_len, prefix_len, queries, key_rows, value_rows, *pages, *pages)


def fetch_page(pool_keys, pool_values, prefix_pages, slot_index):
    devices = lax.axis_size("blk")
    here = lax.axis_index("blk")
    offset = slot_index * devices // PMAX + 1
    asker = (here - offset) % devices
    local = prefix_pages[asker, slot_index] % pool_keys.shape[0]
    send_keys = lax.dynamic_index_in_dim(pool_keys, local, 0, keepdims=False)
    send_values = lax.dynamic_index_in_dim(pool_values, local, 0, keepdims=False)
    return from_behind(jnp.stack([send_keys, send_values]), "blk", devices - offset)


def relay(key_rows, value_rows, placement):
    devices = lax.axis_size("blk")
    here = lax.axis_index("blk")
    blocks = key_rows.shape[0] // PAGE
    width = key_rows.shape[1]
    key_pages = key_rows.reshape(blocks, PAGE, width)
    value_pages = value_rows.reshape(blocks, PAGE, width)
    key_out = jnp.zeros_like(key_pages)
    value_out = jnp.zeros_like(value_pages)
    for block_index in range(blocks):
        offset = (2 * block_index + 1) * devices // (2 * blocks)
        received = from_behind(
            jnp.stack([key_pages[block_index], value_pages[block_index]]), "blk", offset
        )
        source = (here - offset) % devices
        target = placement[source * blocks + block_index] % blocks
        key_out = lax.dynamic_update_index_in_dim(key_out, received[0], target, 0)
        value_out = lax.dynamic_update_index_in_dim(value_out, received[1], target, 0)
    return (key_out, value_out)


def body(
    hidden_in,
    w_query,
    w_key,
    w_value,
    w_out,
    head_gain,
    eigen_rate,
    pool_keys,
    pool_values,
    req_len,
    prefix_len,
    prefix_pages,
    placement,
):
    tokens_here = hidden_in.shape[0]
    other_w_out = from_behind(w_out, "kv", 1)
    width_half = w_query.shape[1]
    heads_here = width_half // HD
    hidden_f = hidden_in.astype(jnp.float32)
    row_scale = lax.rsqrt(jnp.mean(hidden_f * hidden_f, axis=-1, keepdims=True) + epsilon)
    anchor = hidden_f * row_scale
    queries = head_normed(
        jnp.dot(hidden_in, w_query, preferred_element_type=jnp.float32), head_gain
    )
    key_rows = head_normed(jnp.dot(hidden_in, w_key, preferred_element_type=jnp.float32), head_gain)
    value_rows = (
        jnp.dot(hidden_in, w_value, preferred_element_type=jnp.float32) * row_scale
    ).astype(jnp.bfloat16)
    fetched = [
        fetch_page(pool_keys, pool_values, prefix_pages, slot_index) for slot_index in range(PMAX)
    ]
    key_rows, value_rows, fetched, other_w_out = lax.optimization_barrier(
        (key_rows, value_rows, fetched, other_w_out)
    )
    attended = attention(queries, key_rows, value_rows, fetched, req_len, prefix_len)
    other_attended = from_behind(attended, "kv", 1)
    branch = jnp.dot(
        in_kv_order(attended, other_attended, 1),
        in_kv_order(w_out, other_w_out, 0),
        preferred_element_type=jnp.float32,
    )
    updated = anchor + eigen_rate * (rms_scale(branch) - anchor)
    layer_out = rms_scale(updated).astype(jnp.bfloat16)
    new_keys, new_values = relay(key_rows, value_rows, placement)
    return (layer_out, new_keys, new_values)


def solution(mesh):
    in_specs = (
        P("blk", None),
        P(None, "kv"),
        P(None, "kv"),
        P(None, "kv"),
        P("kv", None),
        P("kv"),
        P(),
        P("blk", None, "kv"),
        P("blk", None, "kv"),
        P("blk"),
        P("blk"),
        P(),
        P(),
    )
    out_specs = (P("blk", None), P("blk", None, "kv"), P("blk", None, "kv"))
    return jax.shard_map(body, mesh=mesh, in_specs=in_specs, out_specs=out_specs, check_vma=False)
```

```python
import math

import jax
import jax.numpy as jnp
from jax import lax
from jax.experimental import pallas as pl
from jax.experimental.pallas import tpu as pltpu
from jax.sharding import PartitionSpec as P

HD = 64
PAGE = 256
PMAX = 4


epsilon = 1e-06


def from_behind(block, axis, distance):
    devices = range(lax.axis_size(axis))
    route = [((i - distance) % len(devices), i) for i in devices]
    return lax.ppermute(block, axis, route)


def rms_scale(values):
    return values * lax.rsqrt(jnp.mean(values * values, axis=-1, keepdims=True) + epsilon)


def head_normed(projected, head_gain):
    count = projected.shape[0]
    split_heads = projected.reshape(count, -1, HD)
    return (rms_scale(split_heads).reshape(count, -1) * head_gain).astype(jnp.bfloat16)


def attend(query_heads, key_rows, value_rows, visible):
    key_heads = key_rows.reshape(key_rows.shape[0], -1, HD)
    value_heads = value_rows.reshape(value_rows.shape[0], -1, HD)
    scores = jnp.einsum(
        "qhd,khd->hqk", query_heads, key_heads, preferred_element_type=jnp.float32
    ) / math.sqrt(HD)
    weights = jnp.where(visible, jnp.exp(scores), 0.0)
    totals = jnp.sum(weights, axis=-1)
    mixed = jnp.einsum(
        "hqk,khd->qhd",
        weights.astype(jnp.bfloat16),
        value_heads,
        preferred_element_type=jnp.float32,
    )
    return (totals, mixed)


def in_kv_order(mine, other, axis):
    first = lax.axis_index("kv") == 0
    low = jnp.where(first, mine, other)
    high = jnp.where(first, other, mine)
    return jnp.concatenate([low, high], axis=axis)


def projection_kernel(x_ref, scale_ref, wq_ref, wk_ref, wv_ref, gain_ref, q_ref, k_ref, v_ref):
    hidden = x_ref[...]
    lane = lax.broadcasted_iota(jnp.int32, q_ref.shape, 1)
    first = lane < HD

    def normed(w_ref):
        projected = jnp.dot(hidden, w_ref[...], preferred_element_type=jnp.float32)
        squares = projected * projected
        low = jnp.sum(jnp.where(first, squares, 0.0), axis=1, keepdims=True)
        high = jnp.sum(jnp.where(first, 0.0, squares), axis=1, keepdims=True)
        mean = jnp.where(first, low, high) / HD
        return projected * lax.rsqrt(mean + epsilon) * gain_ref[...]

    q_ref[...] = normed(wq_ref).astype(q_ref.dtype)
    k_ref[...] = normed(wk_ref).astype(k_ref.dtype)
    projected = jnp.dot(hidden, wv_ref[...], preferred_element_type=jnp.float32)
    v_ref[...] = (projected * scale_ref[...]).astype(v_ref.dtype)


def projections(hidden_in, row_scale, w_query, w_key, w_value, head_gain):
    tokens, width = hidden_in.shape
    lanes = 2 * HD
    columns = w_query.shape[1]
    weight_spec = pl.BlockSpec((width, lanes), lambda j: (0, j))
    out_spec = pl.BlockSpec((tokens, lanes), lambda j: (0, j))
    shape = jax.ShapeDtypeStruct((tokens, columns), jnp.bfloat16)
    return pl.pallas_call(
        projection_kernel,
        out_shape=(shape, shape, shape),
        grid=(columns // lanes,),
        in_specs=[
            pl.BlockSpec((tokens, width), lambda j: (0, 0)),
            pl.BlockSpec((tokens, 1), lambda j: (0, 0)),
            weight_spec,
            weight_spec,
            weight_spec,
            pl.BlockSpec((1, lanes), lambda j: (0, j)),
        ],
        out_specs=[out_spec, out_spec, out_spec],
    )(hidden_in, row_scale, w_query, w_key, w_value, head_gain.reshape(1, columns))


def attention_kernel(live_ref, depth_ref, q_ref, k_ref, v_ref, *refs):
    page_refs, out_ref = refs[:-1], refs[-1]
    tile = q_ref.shape[0]
    own = k_ref.shape[0]
    live = live_ref[0]
    depth = depth_ref[0]
    query = q_ref[...]
    lane = lax.broadcasted_iota(jnp.int32, query.shape, 1)
    first = lane < HD
    row = pl.program_id(1) * tile + lax.broadcasted_iota(jnp.int32, (tile, own), 0)
    col = lax.broadcasted_iota(jnp.int32, (tile, own), 1)
    own_visible = (col <= row) & (col < live)
    contract = (((1,), (1,)), ((), ()))
    results = []
    for in_head in (first, jnp.logical_not(first)):
        query_head = jnp.where(in_head, query, jnp.zeros_like(query))
        scores = lax.dot_general(
            query_head, k_ref[...], contract, preferred_element_type=jnp.float32
        ) * (1.0 / math.sqrt(HD))
        weights = jnp.where(own_visible, jnp.exp(scores), 0.0)
        total = jnp.sum(weights, axis=1, keepdims=True)
        mixed = jnp.dot(
            weights.astype(jnp.bfloat16), v_ref[...], preferred_element_type=jnp.float32
        )
        for page in range(PMAX):
            key_page = page_refs[page]
            value_page = page_refs[PMAX + page]
            scores = lax.dot_general(
                query_head, key_page[...], contract, preferred_element_type=jnp.float32
            ) * (1.0 / math.sqrt(HD))
            weights = jnp.where(page < depth, jnp.exp(scores), 0.0)
            total = total + jnp.sum(weights, axis=1, keepdims=True)
            mixed = mixed + jnp.dot(
                weights.astype(jnp.bfloat16), value_page[...], preferred_element_type=jnp.float32
            )
        results.append(mixed / total)
    out_ref[...] = jnp.where(first, results[0], results[1]).astype(out_ref.dtype)


def attention(queries, key_rows, value_rows, pages, req_len, prefix_len):
    tokens, width = queries.shape
    tile = 128
    lanes = 2 * HD
    grid = (width // lanes, tokens // tile)
    own_spec = pl.BlockSpec((tokens, lanes), lambda h, t, *_: (0, h))
    key_spec = pl.BlockSpec((None, PAGE, lanes), lambda h, t, *_: (0, 0, h))
    value_spec = pl.BlockSpec((None, PAGE, lanes), lambda h, t, *_: (1, 0, h))
    tile_spec = pl.BlockSpec((tile, lanes), lambda h, t, *_: (t, h))
    grid_spec = pltpu.PrefetchScalarGridSpec(
        num_scalar_prefetch=2,
        grid=grid,
        in_specs=[tile_spec, own_spec, own_spec] + [key_spec] * PMAX + [value_spec] * PMAX,
        out_specs=tile_spec,
    )
    return pl.pallas_call(
        attention_kernel,
        out_shape=jax.ShapeDtypeStruct((tokens, width), jnp.bfloat16),
        grid_spec=grid_spec,
    )(req_len, prefix_len, queries, key_rows, value_rows, *pages, *pages)


def fetch_page(pool_keys, pool_values, prefix_pages, slot_index):
    devices = lax.axis_size("blk")
    here = lax.axis_index("blk")
    offset = slot_index * devices // PMAX + 1
    asker = (here - offset) % devices
    local = prefix_pages[asker, slot_index] % pool_keys.shape[0]
    send_keys = lax.dynamic_index_in_dim(pool_keys, local, 0, keepdims=False)
    send_values = lax.dynamic_index_in_dim(pool_values, local, 0, keepdims=False)
    return from_behind(jnp.stack([send_keys, send_values]), "blk", devices - offset)


def relay(key_rows, value_rows, placement):
    devices = lax.axis_size("blk")
    here = lax.axis_index("blk")
    blocks = key_rows.shape[0] // PAGE
    width = key_rows.shape[1]
    key_pages = key_rows.reshape(blocks, PAGE, width)
    value_pages = value_rows.reshape(blocks, PAGE, width)
    key_out = jnp.zeros_like(key_pages)
    value_out = jnp.zeros_like(value_pages)
    for block_index in range(blocks):
        offset = (2 * block_index + 1) * devices // (2 * blocks)
        received = from_behind(
            jnp.stack([key_pages[block_index], value_pages[block_index]]), "blk", offset
        )
        source = (here - offset) % devices
        target = placement[source * blocks + block_index] % blocks
        key_out = lax.dynamic_update_index_in_dim(key_out, received[0], target, 0)
        value_out = lax.dynamic_update_index_in_dim(value_out, received[1], target, 0)
    return (key_out, value_out)


def body(
    hidden_in,
    w_query,
    w_key,
    w_value,
    w_out,
    head_gain,
    eigen_rate,
    pool_keys,
    pool_values,
    req_len,
    prefix_len,
    prefix_pages,
    placement,
):
    tokens_here = hidden_in.shape[0]
    other_w_out = from_behind(w_out, "kv", 1)
    width_half = w_query.shape[1]
    heads_here = width_half // HD
    hidden_f = hidden_in.astype(jnp.float32)
    row_scale = lax.rsqrt(jnp.mean(hidden_f * hidden_f, axis=-1, keepdims=True) + epsilon)
    anchor = hidden_f * row_scale
    queries, key_rows, value_rows = projections(
        hidden_in, row_scale, w_query, w_key, w_value, head_gain
    )
    fetched = [
        fetch_page(pool_keys, pool_values, prefix_pages, slot_index) for slot_index in range(PMAX)
    ]
    key_rows, value_rows, fetched = lax.optimization_barrier((key_rows, value_rows, fetched))
    attended = attention(queries, key_rows, value_rows, fetched, req_len, prefix_len)
    other_attended = from_behind(attended, "kv", 1)
    branch = jnp.dot(
        in_kv_order(attended, other_attended, 1),
        in_kv_order(w_out, other_w_out, 0),
        preferred_element_type=jnp.float32,
    )
    updated = anchor + eigen_rate * (rms_scale(branch) - anchor)
    layer_out = rms_scale(updated).astype(jnp.bfloat16)
    new_keys, new_values = relay(key_rows, value_rows, placement)
    return (layer_out, new_keys, new_values)


def solution(mesh):
    in_specs = (
        P("blk", None),
        P(None, "kv"),
        P(None, "kv"),
        P(None, "kv"),
        P("kv", None),
        P("kv"),
        P(),
        P("blk", None, "kv"),
        P("blk", None, "kv"),
        P("blk"),
        P("blk"),
        P(),
        P(),
    )
    out_specs = (P("blk", None), P("blk", None, "kv"), P("blk", None, "kv"))
    return jax.shard_map(body, mesh=mesh, in_specs=in_specs, out_specs=out_specs, check_vma=False)
```

```python
import math

import jax
import jax.numpy as jnp
from jax import lax
from jax.experimental import pallas as pl
from jax.experimental.pallas import tpu as pltpu
from jax.sharding import PartitionSpec as P

HD = 64
PAGE = 256
PMAX = 4


epsilon = 1e-06


def from_behind(block, axis, distance):
    devices = range(lax.axis_size(axis))
    route = [((i - distance) % len(devices), i) for i in devices]
    return lax.ppermute(block, axis, route)


def rms_scale(values):
    return values * lax.rsqrt(jnp.mean(values * values, axis=-1, keepdims=True) + epsilon)


def head_normed(projected, head_gain):
    count = projected.shape[0]
    split_heads = projected.reshape(count, -1, HD)
    return (rms_scale(split_heads).reshape(count, -1) * head_gain).astype(jnp.bfloat16)


def attend(query_heads, key_rows, value_rows, visible):
    key_heads = key_rows.reshape(key_rows.shape[0], -1, HD)
    value_heads = value_rows.reshape(value_rows.shape[0], -1, HD)
    scores = jnp.einsum(
        "qhd,khd->hqk", query_heads, key_heads, preferred_element_type=jnp.float32
    ) / math.sqrt(HD)
    weights = jnp.where(visible, jnp.exp(scores), 0.0)
    totals = jnp.sum(weights, axis=-1)
    mixed = jnp.einsum(
        "hqk,khd->qhd",
        weights.astype(jnp.bfloat16),
        value_heads,
        preferred_element_type=jnp.float32,
    )
    return (totals, mixed)


def in_kv_order(mine, other, axis):
    first = lax.axis_index("kv") == 0
    low = jnp.where(first, mine, other)
    high = jnp.where(first, other, mine)
    return jnp.concatenate([low, high], axis=axis)


def projection_kernel(x_ref, scale_ref, wq_ref, wk_ref, wv_ref, gain_ref, q_ref, k_ref, v_ref):
    hidden = x_ref[...]
    lane = lax.broadcasted_iota(jnp.int32, q_ref.shape, 1)
    first = lane < HD

    def normed(w_ref):
        projected = jnp.dot(hidden, w_ref[...], preferred_element_type=jnp.float32)
        squares = projected * projected
        low = jnp.sum(jnp.where(first, squares, 0.0), axis=1, keepdims=True)
        high = jnp.sum(jnp.where(first, 0.0, squares), axis=1, keepdims=True)
        mean = jnp.where(first, low, high) / HD
        return projected * lax.rsqrt(mean + epsilon) * gain_ref[...]

    q_ref[...] = normed(wq_ref).astype(q_ref.dtype)
    k_ref[...] = normed(wk_ref).astype(k_ref.dtype)
    projected = jnp.dot(hidden, wv_ref[...], preferred_element_type=jnp.float32)
    v_ref[...] = (projected * scale_ref[...]).astype(v_ref.dtype)


def projections(hidden_in, row_scale, w_query, w_key, w_value, head_gain):
    tokens, width = hidden_in.shape
    lanes = 2 * HD
    columns = w_query.shape[1]
    weight_spec = pl.BlockSpec((width, lanes), lambda j: (0, j))
    out_spec = pl.BlockSpec((tokens, lanes), lambda j: (0, j))
    shape = jax.ShapeDtypeStruct((tokens, columns), jnp.bfloat16)
    return pl.pallas_call(
        projection_kernel,
        out_shape=(shape, shape, shape),
        grid=(columns // lanes,),
        in_specs=[
            pl.BlockSpec((tokens, width), lambda j: (0, 0)),
            pl.BlockSpec((tokens, 1), lambda j: (0, 0)),
            weight_spec,
            weight_spec,
            weight_spec,
            pl.BlockSpec((1, lanes), lambda j: (0, j)),
        ],
        out_specs=[out_spec, out_spec, out_spec],
    )(hidden_in, row_scale, w_query, w_key, w_value, head_gain.reshape(1, columns))


def attention_kernel(live_ref, depth_ref, q_ref, k_ref, v_ref, *refs):
    page_refs, out_ref = refs[:-1], refs[-1]
    tile = q_ref.shape[0]
    own = k_ref.shape[0]
    live = live_ref[0]
    depth = depth_ref[0]
    query = q_ref[...]
    lane = lax.broadcasted_iota(jnp.int32, query.shape, 1)
    first = lane < HD
    row = pl.program_id(1) * tile + lax.broadcasted_iota(jnp.int32, (tile, own), 0)
    col = lax.broadcasted_iota(jnp.int32, (tile, own), 1)
    own_visible = (col <= row) & (col < live)
    contract = (((1,), (1,)), ((), ()))
    results = []
    for in_head in (first, jnp.logical_not(first)):
        query_head = jnp.where(in_head, query, jnp.zeros_like(query))
        scores = lax.dot_general(
            query_head, k_ref[...], contract, preferred_element_type=jnp.float32
        ) * (1.0 / math.sqrt(HD))
        weights = jnp.where(own_visible, jnp.exp(scores), 0.0)
        total = jnp.sum(weights, axis=1, keepdims=True)
        mixed = jnp.dot(
            weights.astype(jnp.bfloat16), v_ref[...], preferred_element_type=jnp.float32
        )
        for page in range(PMAX):
            key_page = page_refs[page]
            value_page = page_refs[PMAX + page]
            scores = lax.dot_general(
                query_head, key_page[...], contract, preferred_element_type=jnp.float32
            ) * (1.0 / math.sqrt(HD))
            weights = jnp.where(page < depth, jnp.exp(scores), 0.0)
            total = total + jnp.sum(weights, axis=1, keepdims=True)
            mixed = mixed + jnp.dot(
                weights.astype(jnp.bfloat16), value_page[...], preferred_element_type=jnp.float32
            )
        results.append(mixed / total)
    out_ref[...] = jnp.where(first, results[0], results[1]).astype(out_ref.dtype)


def attention(queries, key_rows, value_rows, pages, req_len, prefix_len):
    tokens, width = queries.shape
    tile = 128
    lanes = 2 * HD
    grid = (width // lanes, tokens // tile)
    own_spec = pl.BlockSpec((tokens, lanes), lambda h, t, *_: (0, h))
    key_spec = pl.BlockSpec((None, PAGE, lanes), lambda h, t, *_: (0, 0, h))
    value_spec = pl.BlockSpec((None, PAGE, lanes), lambda h, t, *_: (1, 0, h))
    tile_spec = pl.BlockSpec((tile, lanes), lambda h, t, *_: (t, h))
    grid_spec = pltpu.PrefetchScalarGridSpec(
        num_scalar_prefetch=2,
        grid=grid,
        in_specs=[tile_spec, own_spec, own_spec] + [key_spec] * PMAX + [value_spec] * PMAX,
        out_specs=tile_spec,
    )
    return pl.pallas_call(
        attention_kernel,
        out_shape=jax.ShapeDtypeStruct((tokens, width), jnp.bfloat16),
        grid_spec=grid_spec,
    )(req_len, prefix_len, queries, key_rows, value_rows, *pages, *pages)


def fetch_page(pool_keys, pool_values, prefix_pages, slot_index):
    devices = lax.axis_size("blk")
    here = lax.axis_index("blk")
    offset = slot_index * devices // PMAX + 1
    asker = (here - offset) % devices
    local = prefix_pages[asker, slot_index] % pool_keys.shape[0]
    send_keys = lax.dynamic_index_in_dim(pool_keys, local, 0, keepdims=False)
    send_values = lax.dynamic_index_in_dim(pool_values, local, 0, keepdims=False)
    return from_behind(jnp.stack([send_keys, send_values]), "blk", devices - offset)


def relay(key_rows, value_rows, placement):
    devices = lax.axis_size("blk")
    here = lax.axis_index("blk")
    blocks = key_rows.shape[0] // PAGE
    width = key_rows.shape[1]
    key_pages = key_rows.reshape(blocks, PAGE, width)
    value_pages = value_rows.reshape(blocks, PAGE, width)
    key_out = jnp.zeros_like(key_pages)
    value_out = jnp.zeros_like(value_pages)
    for block_index in range(blocks):
        offset = (2 * block_index + 1) * devices // (2 * blocks)
        received = from_behind(
            jnp.stack([key_pages[block_index], value_pages[block_index]]), "blk", offset
        )
        source = (here - offset) % devices
        target = placement[source * blocks + block_index] % blocks
        key_out = lax.dynamic_update_index_in_dim(key_out, received[0], target, 0)
        value_out = lax.dynamic_update_index_in_dim(value_out, received[1], target, 0)
    return (key_out, value_out)


def body(
    hidden_in,
    w_query,
    w_key,
    w_value,
    w_out,
    head_gain,
    eigen_rate,
    pool_keys,
    pool_values,
    req_len,
    prefix_len,
    prefix_pages,
    placement,
):
    tokens_here = hidden_in.shape[0]
    other_w_out = from_behind(w_out, "kv", 1)
    width_half = w_query.shape[1]
    heads_here = width_half // HD
    hidden_f = hidden_in.astype(jnp.float32)
    row_scale = lax.rsqrt(jnp.mean(hidden_f * hidden_f, axis=-1, keepdims=True) + epsilon)
    anchor = hidden_f * row_scale
    queries, key_rows, value_rows = projections(
        hidden_in, row_scale, w_query, w_key, w_value, head_gain
    )
    fetched = [
        fetch_page(pool_keys, pool_values, prefix_pages, slot_index) for slot_index in range(PMAX)
    ]
    attended = attention(queries, key_rows, value_rows, fetched, req_len, prefix_len)
    other_attended = from_behind(attended, "kv", 1)
    branch = jnp.dot(
        in_kv_order(attended, other_attended, 1),
        in_kv_order(w_out, other_w_out, 0),
        preferred_element_type=jnp.float32,
    )
    updated = anchor + eigen_rate * (rms_scale(branch) - anchor)
    layer_out = rms_scale(updated).astype(jnp.bfloat16)
    new_keys, new_values = relay(key_rows, value_rows, placement)
    return (layer_out, new_keys, new_values)


def solution(mesh):
    in_specs = (
        P("blk", None),
        P(None, "kv"),
        P(None, "kv"),
        P(None, "kv"),
        P("kv", None),
        P("kv"),
        P(),
        P("blk", None, "kv"),
        P("blk", None, "kv"),
        P("blk"),
        P("blk"),
        P(),
        P(),
    )
    out_specs = (P("blk", None), P("blk", None, "kv"), P("blk", None, "kv"))
    return jax.shard_map(body, mesh=mesh, in_specs=in_specs, out_specs=out_specs, check_vma=False)
```

```python
import functools
import math

import jax
import jax.numpy as jnp
from jax import lax
from jax.experimental import pallas as pl
from jax.experimental.pallas import tpu as pltpu
from jax.sharding import PartitionSpec as P

HD = 64
PAGE = 256
PMAX = 4


epsilon = 1e-06


def from_behind(block, axis, distance):
    devices = range(lax.axis_size(axis))
    route = [((i - distance) % len(devices), i) for i in devices]
    return lax.ppermute(block, axis, route)


def rms_scale(values):
    return values * lax.rsqrt(jnp.mean(values * values, axis=-1, keepdims=True) + epsilon)


def head_normed(projected, head_gain):
    count = projected.shape[0]
    split_heads = projected.reshape(count, -1, HD)
    return (rms_scale(split_heads).reshape(count, -1) * head_gain).astype(jnp.bfloat16)


def attend(query_heads, key_rows, value_rows, visible):
    key_heads = key_rows.reshape(key_rows.shape[0], -1, HD)
    value_heads = value_rows.reshape(value_rows.shape[0], -1, HD)
    scores = jnp.einsum(
        "qhd,khd->hqk", query_heads, key_heads, preferred_element_type=jnp.float32
    ) / math.sqrt(HD)
    weights = jnp.where(visible, jnp.exp(scores), 0.0)
    totals = jnp.sum(weights, axis=-1)
    mixed = jnp.einsum(
        "hqk,khd->qhd",
        weights.astype(jnp.bfloat16),
        value_heads,
        preferred_element_type=jnp.float32,
    )
    return (totals, mixed)


def in_kv_order(mine, other, axis):
    first = lax.axis_index("kv") == 0
    low = jnp.where(first, mine, other)
    high = jnp.where(first, other, mine)
    return jnp.concatenate([low, high], axis=axis)


def projection_kernel(x_ref, scale_ref, wq_ref, wk_ref, wv_ref, gain_ref, q_ref, k_ref, v_ref):
    hidden = x_ref[...]
    lane = lax.broadcasted_iota(jnp.int32, q_ref.shape, 1)
    first = lane < HD

    def normed(w_ref):
        projected = jnp.dot(hidden, w_ref[...], preferred_element_type=jnp.float32)
        squares = projected * projected
        low = jnp.sum(jnp.where(first, squares, 0.0), axis=1, keepdims=True)
        high = jnp.sum(jnp.where(first, 0.0, squares), axis=1, keepdims=True)
        mean = jnp.where(first, low, high) / HD
        return projected * lax.rsqrt(mean + epsilon) * gain_ref[...]

    q_ref[...] = normed(wq_ref).astype(q_ref.dtype)
    k_ref[...] = normed(wk_ref).astype(k_ref.dtype)
    projected = jnp.dot(hidden, wv_ref[...], preferred_element_type=jnp.float32)
    v_ref[...] = (projected * scale_ref[...]).astype(v_ref.dtype)


def projections(hidden_in, row_scale, w_query, w_key, w_value, head_gain):
    tokens, width = hidden_in.shape
    lanes = 2 * HD
    columns = w_query.shape[1]
    weight_spec = pl.BlockSpec((width, lanes), lambda j: (0, j))
    out_spec = pl.BlockSpec((tokens, lanes), lambda j: (0, j))
    shape = jax.ShapeDtypeStruct((tokens, columns), jnp.bfloat16)
    return pl.pallas_call(
        projection_kernel,
        out_shape=(shape, shape, shape),
        grid=(columns // lanes,),
        in_specs=[
            pl.BlockSpec((tokens, width), lambda j: (0, 0)),
            pl.BlockSpec((tokens, 1), lambda j: (0, 0)),
            weight_spec,
            weight_spec,
            weight_spec,
            pl.BlockSpec((1, lanes), lambda j: (0, j)),
        ],
        out_specs=[out_spec, out_spec, out_spec],
    )(hidden_in, row_scale, w_query, w_key, w_value, head_gain.reshape(1, columns))


def attention_kernel(live_ref, depth_ref, q_ref, k_ref, v_ref, *refs):
    page_refs, out_ref = refs[:-1], refs[-1]
    tile = q_ref.shape[0]
    own = k_ref.shape[0]
    live = live_ref[0]
    depth = depth_ref[0]
    query = q_ref[...]
    lane = lax.broadcasted_iota(jnp.int32, query.shape, 1)
    first = lane < HD
    row = pl.program_id(1) * tile + lax.broadcasted_iota(jnp.int32, (tile, own), 0)
    col = lax.broadcasted_iota(jnp.int32, (tile, own), 1)
    own_visible = (col <= row) & (col < live)
    contract = (((1,), (1,)), ((), ()))
    results = []
    for in_head in (first, jnp.logical_not(first)):
        query_head = jnp.where(in_head, query, jnp.zeros_like(query))
        scores = lax.dot_general(
            query_head, k_ref[...], contract, preferred_element_type=jnp.float32
        ) * (1.0 / math.sqrt(HD))
        weights = jnp.where(own_visible, jnp.exp(scores), 0.0)
        total = jnp.sum(weights, axis=1, keepdims=True)
        mixed = jnp.dot(
            weights.astype(jnp.bfloat16), v_ref[...], preferred_element_type=jnp.float32
        )
        for page in range(PMAX):
            key_page = page_refs[page]
            value_page = page_refs[PMAX + page]
            scores = lax.dot_general(
                query_head, key_page[...], contract, preferred_element_type=jnp.float32
            ) * (1.0 / math.sqrt(HD))
            weights = jnp.where(page < depth, jnp.exp(scores), 0.0)
            total = total + jnp.sum(weights, axis=1, keepdims=True)
            mixed = mixed + jnp.dot(
                weights.astype(jnp.bfloat16), value_page[...], preferred_element_type=jnp.float32
            )
        results.append(mixed / total)
    out_ref[...] = jnp.where(first, results[0], results[1]).astype(out_ref.dtype)


def attention(queries, key_rows, value_rows, pages, req_len, prefix_len):
    tokens, width = queries.shape
    tile = 128
    lanes = 2 * HD
    grid = (width // lanes, tokens // tile)
    own_spec = pl.BlockSpec((tokens, lanes), lambda h, t, *_: (0, h))
    key_spec = pl.BlockSpec((None, PAGE, lanes), lambda h, t, *_: (0, 0, h))
    value_spec = pl.BlockSpec((None, PAGE, lanes), lambda h, t, *_: (1, 0, h))
    tile_spec = pl.BlockSpec((tile, lanes), lambda h, t, *_: (t, h))
    grid_spec = pltpu.PrefetchScalarGridSpec(
        num_scalar_prefetch=2,
        grid=grid,
        in_specs=[tile_spec, own_spec, own_spec] + [key_spec] * PMAX + [value_spec] * PMAX,
        out_specs=tile_spec,
    )
    return pl.pallas_call(
        attention_kernel,
        out_shape=jax.ShapeDtypeStruct((tokens, width), jnp.bfloat16),
        grid_spec=grid_spec,
    )(req_len, prefix_len, queries, key_rows, value_rows, *pages, *pages)


def gather_kernel(devices, pages_ref, keys_hbm, values_hbm, *refs):
    outs, sems = refs[:PMAX], refs[PMAX]
    here = lax.axis_index("blk")
    count = keys_hbm.shape[0]
    copies = []
    for slot_index in range(PMAX):
        offset = slot_index * devices // PMAX + 1
        asker = lax.rem(here + (devices - offset), devices)
        local = lax.rem(pages_ref[asker, slot_index], count)
        for part, source in enumerate((keys_hbm, values_hbm)):
            copy = pltpu.make_async_copy(
                source.at[local], outs[slot_index].at[part], sems.at[2 * slot_index + part]
            )
            copy.start()
            copies.append(copy)
    for copy in copies:
        copy.wait()


def fetch_pages(pool_keys, pool_values, prefix_pages):
    devices = lax.axis_size("blk")
    page_shape = jax.ShapeDtypeStruct((2,) + pool_keys.shape[1:], pool_keys.dtype)
    grid_spec = pltpu.PrefetchScalarGridSpec(
        num_scalar_prefetch=1,
        grid=(),
        in_specs=[pl.BlockSpec(memory_space=pl.ANY)] * 2,
        out_specs=[pl.BlockSpec(memory_space=pltpu.VMEM)] * PMAX,
        scratch_shapes=[pltpu.SemaphoreType.DMA((2 * PMAX,))],
    )
    gathered = pl.pallas_call(
        functools.partial(gather_kernel, devices),
        out_shape=[page_shape] * PMAX,
        grid_spec=grid_spec,
    )(prefix_pages, pool_keys, pool_values)
    return [
        from_behind(gathered[slot_index], "blk", devices - (slot_index * devices // PMAX + 1))
        for slot_index in range(PMAX)
    ]


def relay(key_rows, value_rows, placement):
    devices = lax.axis_size("blk")
    here = lax.axis_index("blk")
    blocks = key_rows.shape[0] // PAGE
    width = key_rows.shape[1]
    key_pages = key_rows.reshape(blocks, PAGE, width)
    value_pages = value_rows.reshape(blocks, PAGE, width)
    key_out = jnp.zeros_like(key_pages)
    value_out = jnp.zeros_like(value_pages)
    for block_index in range(blocks):
        offset = (2 * block_index + 1) * devices // (2 * blocks)
        received = from_behind(
            jnp.stack([key_pages[block_index], value_pages[block_index]]), "blk", offset
        )
        source = (here - offset) % devices
        target = placement[source * blocks + block_index] % blocks
        key_out = lax.dynamic_update_index_in_dim(key_out, received[0], target, 0)
        value_out = lax.dynamic_update_index_in_dim(value_out, received[1], target, 0)
    return (key_out, value_out)


def body(
    hidden_in,
    w_query,
    w_key,
    w_value,
    w_out,
    head_gain,
    eigen_rate,
    pool_keys,
    pool_values,
    req_len,
    prefix_len,
    prefix_pages,
    placement,
):
    tokens_here = hidden_in.shape[0]
    other_w_out = from_behind(w_out, "kv", 1)
    width_half = w_query.shape[1]
    heads_here = width_half // HD
    hidden_f = hidden_in.astype(jnp.float32)
    row_scale = lax.rsqrt(jnp.mean(hidden_f * hidden_f, axis=-1, keepdims=True) + epsilon)
    anchor = hidden_f * row_scale
    queries, key_rows, value_rows = projections(
        hidden_in, row_scale, w_query, w_key, w_value, head_gain
    )
    fetched = fetch_pages(pool_keys, pool_values, prefix_pages)
    attended = attention(queries, key_rows, value_rows, fetched, req_len, prefix_len)
    other_attended = from_behind(attended, "kv", 1)
    branch = jnp.dot(
        in_kv_order(attended, other_attended, 1),
        in_kv_order(w_out, other_w_out, 0),
        preferred_element_type=jnp.float32,
    )
    updated = anchor + eigen_rate * (rms_scale(branch) - anchor)
    layer_out = rms_scale(updated).astype(jnp.bfloat16)
    new_keys, new_values = relay(key_rows, value_rows, placement)
    return (layer_out, new_keys, new_values)


def solution(mesh):
    in_specs = (
        P("blk", None),
        P(None, "kv"),
        P(None, "kv"),
        P(None, "kv"),
        P("kv", None),
        P("kv"),
        P(),
        P("blk", None, "kv"),
        P("blk", None, "kv"),
        P("blk"),
        P("blk"),
        P(),
        P(),
    )
    out_specs = (P("blk", None), P("blk", None, "kv"), P("blk", None, "kv"))
    return jax.shard_map(body, mesh=mesh, in_specs=in_specs, out_specs=out_specs, check_vma=False)
```

```python
import functools
import math

import jax
import jax.numpy as jnp
from jax import lax
from jax.experimental import pallas as pl
from jax.experimental.pallas import tpu as pltpu
from jax.sharding import PartitionSpec as P

HD = 64
PAGE = 256
PMAX = 4


epsilon = 1e-06


def from_behind(block, axis, distance):
    devices = range(lax.axis_size(axis))
    route = [((i - distance) % len(devices), i) for i in devices]
    return lax.ppermute(block, axis, route)


def rms_scale(values):
    return values * lax.rsqrt(jnp.mean(values * values, axis=-1, keepdims=True) + epsilon)


def head_normed(projected, head_gain):
    count = projected.shape[0]
    split_heads = projected.reshape(count, -1, HD)
    return (rms_scale(split_heads).reshape(count, -1) * head_gain).astype(jnp.bfloat16)


def attend(query_heads, key_rows, value_rows, visible):
    key_heads = key_rows.reshape(key_rows.shape[0], -1, HD)
    value_heads = value_rows.reshape(value_rows.shape[0], -1, HD)
    scores = jnp.einsum(
        "qhd,khd->hqk", query_heads, key_heads, preferred_element_type=jnp.float32
    ) / math.sqrt(HD)
    weights = jnp.where(visible, jnp.exp(scores), 0.0)
    totals = jnp.sum(weights, axis=-1)
    mixed = jnp.einsum(
        "hqk,khd->qhd",
        weights.astype(jnp.bfloat16),
        value_heads,
        preferred_element_type=jnp.float32,
    )
    return (totals, mixed)


def in_kv_order(mine, other, axis):
    first = lax.axis_index("kv") == 0
    low = jnp.where(first, mine, other)
    high = jnp.where(first, other, mine)
    return jnp.concatenate([low, high], axis=axis)


def projection_kernel(x_ref, scale_ref, wq_ref, wk_ref, wv_ref, gain_ref, q_ref, k_ref, v_ref):
    hidden = x_ref[...]
    lane = lax.broadcasted_iota(jnp.int32, q_ref.shape, 1)
    first = lane < HD

    def normed(w_ref):
        projected = jnp.dot(hidden, w_ref[...], preferred_element_type=jnp.float32)
        squares = projected * projected
        low = jnp.sum(jnp.where(first, squares, 0.0), axis=1, keepdims=True)
        high = jnp.sum(jnp.where(first, 0.0, squares), axis=1, keepdims=True)
        mean = jnp.where(first, low, high) / HD
        return projected * lax.rsqrt(mean + epsilon) * gain_ref[...]

    q_ref[...] = normed(wq_ref).astype(q_ref.dtype)
    k_ref[...] = normed(wk_ref).astype(k_ref.dtype)
    projected = jnp.dot(hidden, wv_ref[...], preferred_element_type=jnp.float32)
    v_ref[...] = (projected * scale_ref[...]).astype(v_ref.dtype)


def projections(hidden_in, row_scale, w_query, w_key, w_value, head_gain):
    tokens, width = hidden_in.shape
    lanes = 2 * HD
    columns = w_query.shape[1]
    weight_spec = pl.BlockSpec((width, lanes), lambda j: (0, j))
    out_spec = pl.BlockSpec((tokens, lanes), lambda j: (0, j))
    shape = jax.ShapeDtypeStruct((tokens, columns), jnp.bfloat16)
    return pl.pallas_call(
        projection_kernel,
        out_shape=(shape, shape, shape),
        grid=(columns // lanes,),
        in_specs=[
            pl.BlockSpec((tokens, width), lambda j: (0, 0)),
            pl.BlockSpec((tokens, 1), lambda j: (0, 0)),
            weight_spec,
            weight_spec,
            weight_spec,
            pl.BlockSpec((1, lanes), lambda j: (0, j)),
        ],
        out_specs=[out_spec, out_spec, out_spec],
    )(hidden_in, row_scale, w_query, w_key, w_value, head_gain.reshape(1, columns))


def head_scores(query_head, key_ref):
    contract = (((1,), (1,)), ((), ()))
    return lax.dot_general(
        query_head, key_ref[...], contract, preferred_element_type=jnp.float32
    ) * (1.0 / math.sqrt(HD))


def own_kernel(live_ref, q_ref, k_ref, v_ref, mixed_ref, total_ref):
    tile = q_ref.shape[0]
    own = k_ref.shape[0]
    live = live_ref[0]
    query = q_ref[...]
    lane = lax.broadcasted_iota(jnp.int32, query.shape, 1)
    first = lane < HD
    row = pl.program_id(1) * tile + lax.broadcasted_iota(jnp.int32, (tile, own), 0)
    col = lax.broadcasted_iota(jnp.int32, (tile, own), 1)
    own_visible = (col <= row) & (col < live)
    mixes = []
    totals = []
    for in_head in (first, jnp.logical_not(first)):
        query_head = jnp.where(in_head, query, jnp.zeros_like(query))
        weights = jnp.where(own_visible, jnp.exp(head_scores(query_head, k_ref)), 0.0)
        totals.append(jnp.sum(weights, axis=1, keepdims=True))
        mixes.append(
            jnp.dot(weights.astype(jnp.bfloat16), v_ref[...], preferred_element_type=jnp.float32)
        )
    mixed_ref[...] = jnp.where(first, mixes[0], mixes[1])
    total_ref[...] = jnp.where(first, totals[0], totals[1])


def cached_kernel(depth_ref, q_ref, mixed_ref, total_ref, *refs):
    page_refs, out_ref = refs[:-1], refs[-1]
    depth = depth_ref[0]
    query = q_ref[...]
    lane = lax.broadcasted_iota(jnp.int32, query.shape, 1)
    first = lane < HD
    mixes = []
    totals = []
    for in_head in (first, jnp.logical_not(first)):
        query_head = jnp.where(in_head, query, jnp.zeros_like(query))
        total = None
        mixed = mixed_ref[...]
        for page in range(PMAX):
            weights = jnp.where(
                page < depth, jnp.exp(head_scores(query_head, page_refs[page])), 0.0
            )
            page_total = jnp.sum(weights, axis=1, keepdims=True)
            total = page_total if total is None else total + page_total
            mixed = mixed + jnp.dot(
                weights.astype(jnp.bfloat16), page_refs[PMAX + page][...],
                preferred_element_type=jnp.float32,
            )
        totals.append(total)
        mixes.append(mixed)
    total = total_ref[...] + jnp.where(first, totals[0], totals[1])
    out_ref[...] = (jnp.where(first, mixes[0], mixes[1]) / total).astype(out_ref.dtype)


def attention(queries, key_rows, value_rows, pages, req_len, prefix_len):
    tokens, width = queries.shape
    tile = 128
    lanes = 2 * HD
    grid = (width // lanes, tokens // tile)
    own_spec = pl.BlockSpec((tokens, lanes), lambda h, t, *_: (0, h))
    key_spec = pl.BlockSpec((None, PAGE, lanes), lambda h, t, *_: (0, 0, h))
    value_spec = pl.BlockSpec((None, PAGE, lanes), lambda h, t, *_: (1, 0, h))
    tile_spec = pl.BlockSpec((tile, lanes), lambda h, t, *_: (t, h))
    partial = jax.ShapeDtypeStruct((tokens, width), jnp.float32)
    mixed, total = pl.pallas_call(
        own_kernel,
        out_shape=(partial, partial),
        grid_spec=pltpu.PrefetchScalarGridSpec(
            num_scalar_prefetch=1,
            grid=grid,
            in_specs=[tile_spec, own_spec, own_spec],
            out_specs=[tile_spec, tile_spec],
        ),
        cost_estimate=pl.CostEstimate(
            flops=8 * tokens * tokens * width,
            transcendentals=tokens * tokens * width // HD,
            bytes_accessed=2 * 3 * tokens * width + 8 * tokens * width,
        ),
    )(req_len, queries, key_rows, value_rows)
    keys = PMAX * PAGE
    return pl.pallas_call(
        cached_kernel,
        out_shape=jax.ShapeDtypeStruct((tokens, width), jnp.bfloat16),
        grid_spec=pltpu.PrefetchScalarGridSpec(
            num_scalar_prefetch=1,
            grid=grid,
            in_specs=[tile_spec, tile_spec, tile_spec] + [key_spec] * PMAX + [value_spec] * PMAX,
            out_specs=tile_spec,
        ),
        cost_estimate=pl.CostEstimate(
            flops=8 * tokens * keys * width,
            transcendentals=tokens * keys * width // HD,
            bytes_accessed=2 * (tokens + 2 * keys) * width + 8 * tokens * width,
        ),
    )(prefix_len, queries, mixed, total, *pages, *pages)


def gather_kernel(devices, pages_ref, keys_hbm, values_hbm, *refs):
    outs, sems = refs[:PMAX], refs[PMAX]
    here = lax.axis_index("blk")
    count = keys_hbm.shape[0]
    copies = []
    for slot_index in range(PMAX):
        offset = slot_index * devices // PMAX + 1
        asker = lax.rem(here + (devices - offset), devices)
        local = lax.rem(pages_ref[asker, slot_index], count)
        for part, source in enumerate((keys_hbm, values_hbm)):
            copy = pltpu.make_async_copy(
                source.at[local], outs[slot_index].at[part], sems.at[2 * slot_index + part]
            )
            copy.start()
            copies.append(copy)
    for copy in copies:
        copy.wait()


def fetch_pages(pool_keys, pool_values, prefix_pages):
    devices = lax.axis_size("blk")
    page_shape = jax.ShapeDtypeStruct((2,) + pool_keys.shape[1:], pool_keys.dtype)
    grid_spec = pltpu.PrefetchScalarGridSpec(
        num_scalar_prefetch=1,
        grid=(),
        in_specs=[pl.BlockSpec(memory_space=pl.ANY)] * 2,
        out_specs=[pl.BlockSpec(memory_space=pltpu.VMEM)] * PMAX,
        scratch_shapes=[pltpu.SemaphoreType.DMA((2 * PMAX,))],
    )
    gathered = pl.pallas_call(
        functools.partial(gather_kernel, devices),
        out_shape=[page_shape] * PMAX,
        grid_spec=grid_spec,
    )(prefix_pages, pool_keys, pool_values)
    return [
        from_behind(gathered[slot_index], "blk", devices - (slot_index * devices // PMAX + 1))
        for slot_index in range(PMAX)
    ]


def relay(key_rows, value_rows, placement):
    devices = lax.axis_size("blk")
    here = lax.axis_index("blk")
    blocks = key_rows.shape[0] // PAGE
    width = key_rows.shape[1]
    key_pages = key_rows.reshape(blocks, PAGE, width)
    value_pages = value_rows.reshape(blocks, PAGE, width)
    key_out = jnp.zeros_like(key_pages)
    value_out = jnp.zeros_like(value_pages)
    for block_index in range(blocks):
        offset = (2 * block_index + 1) * devices // (2 * blocks)
        received = from_behind(
            jnp.stack([key_pages[block_index], value_pages[block_index]]), "blk", offset
        )
        source = (here - offset) % devices
        target = placement[source * blocks + block_index] % blocks
        key_out = lax.dynamic_update_index_in_dim(key_out, received[0], target, 0)
        value_out = lax.dynamic_update_index_in_dim(value_out, received[1], target, 0)
    return (key_out, value_out)


def body(
    hidden_in,
    w_query,
    w_key,
    w_value,
    w_out,
    head_gain,
    eigen_rate,
    pool_keys,
    pool_values,
    req_len,
    prefix_len,
    prefix_pages,
    placement,
):
    tokens_here = hidden_in.shape[0]
    other_w_out = from_behind(w_out, "kv", 1)
    width_half = w_query.shape[1]
    heads_here = width_half // HD
    hidden_f = hidden_in.astype(jnp.float32)
    row_scale = lax.rsqrt(jnp.mean(hidden_f * hidden_f, axis=-1, keepdims=True) + epsilon)
    anchor = hidden_f * row_scale
    queries, key_rows, value_rows = projections(
        hidden_in, row_scale, w_query, w_key, w_value, head_gain
    )
    fetched = fetch_pages(pool_keys, pool_values, prefix_pages)
    attended = attention(queries, key_rows, value_rows, fetched, req_len, prefix_len)
    other_attended = from_behind(attended, "kv", 1)
    branch = jnp.dot(
        in_kv_order(attended, other_attended, 1),
        in_kv_order(w_out, other_w_out, 0),
        preferred_element_type=jnp.float32,
    )
    updated = anchor + eigen_rate * (rms_scale(branch) - anchor)
    layer_out = rms_scale(updated).astype(jnp.bfloat16)
    new_keys, new_values = relay(key_rows, value_rows, placement)
    return (layer_out, new_keys, new_values)


def solution(mesh):
    in_specs = (
        P("blk", None),
        P(None, "kv"),
        P(None, "kv"),
        P(None, "kv"),
        P("kv", None),
        P("kv"),
        P(),
        P("blk", None, "kv"),
        P("blk", None, "kv"),
        P("blk"),
        P("blk"),
        P(),
        P(),
    )
    out_specs = (P("blk", None), P("blk", None, "kv"), P("blk", None, "kv"))
    return jax.shard_map(body, mesh=mesh, in_specs=in_specs, out_specs=out_specs, check_vma=False)
```

```python
import functools
import math

import jax
import jax.numpy as jnp
from jax import lax
from jax.experimental import pallas as pl
from jax.experimental.pallas import tpu as pltpu
from jax.sharding import PartitionSpec as P

HD = 64
PAGE = 256
PMAX = 4


epsilon = 1e-06


def from_behind(block, axis, distance):
    devices = range(lax.axis_size(axis))
    route = [((i - distance) % len(devices), i) for i in devices]
    return lax.ppermute(block, axis, route)


def rms_scale(values):
    return values * lax.rsqrt(jnp.mean(values * values, axis=-1, keepdims=True) + epsilon)


def head_normed(projected, head_gain):
    count = projected.shape[0]
    split_heads = projected.reshape(count, -1, HD)
    return (rms_scale(split_heads).reshape(count, -1) * head_gain).astype(jnp.bfloat16)


def attend(query_heads, key_rows, value_rows, visible):
    key_heads = key_rows.reshape(key_rows.shape[0], -1, HD)
    value_heads = value_rows.reshape(value_rows.shape[0], -1, HD)
    scores = jnp.einsum(
        "qhd,khd->hqk", query_heads, key_heads, preferred_element_type=jnp.float32
    ) / math.sqrt(HD)
    weights = jnp.where(visible, jnp.exp(scores), 0.0)
    totals = jnp.sum(weights, axis=-1)
    mixed = jnp.einsum(
        "hqk,khd->qhd",
        weights.astype(jnp.bfloat16),
        value_heads,
        preferred_element_type=jnp.float32,
    )
    return (totals, mixed)


def in_kv_order(mine, other, axis):
    first = lax.axis_index("kv") == 0
    low = jnp.where(first, mine, other)
    high = jnp.where(first, other, mine)
    return jnp.concatenate([low, high], axis=axis)


def projection_kernel(x_ref, scale_ref, wq_ref, wk_ref, wv_ref, gain_ref, q_ref, k_ref, v_ref):
    hidden = x_ref[...]
    lane = lax.broadcasted_iota(jnp.int32, q_ref.shape, 1)
    first = lane < HD

    def normed(w_ref):
        projected = jnp.dot(hidden, w_ref[...], preferred_element_type=jnp.float32)
        squares = projected * projected
        low = jnp.sum(jnp.where(first, squares, 0.0), axis=1, keepdims=True)
        high = jnp.sum(jnp.where(first, 0.0, squares), axis=1, keepdims=True)
        mean = jnp.where(first, low, high) / HD
        return projected * lax.rsqrt(mean + epsilon) * gain_ref[...]

    q_ref[...] = normed(wq_ref).astype(q_ref.dtype)
    k_ref[...] = normed(wk_ref).astype(k_ref.dtype)
    projected = jnp.dot(hidden, wv_ref[...], preferred_element_type=jnp.float32)
    v_ref[...] = (projected * scale_ref[...]).astype(v_ref.dtype)


def projections(hidden_in, row_scale, w_query, w_key, w_value, head_gain):
    tokens, width = hidden_in.shape
    lanes = 2 * HD
    columns = w_query.shape[1]
    weight_spec = pl.BlockSpec((width, lanes), lambda j: (0, j))
    out_spec = pl.BlockSpec((tokens, lanes), lambda j: (0, j))
    shape = jax.ShapeDtypeStruct((tokens, columns), jnp.bfloat16)
    return pl.pallas_call(
        projection_kernel,
        out_shape=(shape, shape, shape),
        grid=(columns // lanes,),
        in_specs=[
            pl.BlockSpec((tokens, width), lambda j: (0, 0)),
            pl.BlockSpec((tokens, 1), lambda j: (0, 0)),
            weight_spec,
            weight_spec,
            weight_spec,
            pl.BlockSpec((1, lanes), lambda j: (0, j)),
        ],
        out_specs=[out_spec, out_spec, out_spec],
    )(hidden_in, row_scale, w_query, w_key, w_value, head_gain.reshape(1, columns))


def attention_kernel(live_ref, depth_ref, q_ref, k_ref, v_ref, *refs):
    page_refs, out_ref = refs[:-1], refs[-1]
    tile = q_ref.shape[0]
    own = k_ref.shape[0]
    live = live_ref[0]
    depth = depth_ref[0]
    query = q_ref[...]
    lane = lax.broadcasted_iota(jnp.int32, query.shape, 1)
    first = lane < HD
    row = pl.program_id(1) * tile + lax.broadcasted_iota(jnp.int32, (tile, own), 0)
    col = lax.broadcasted_iota(jnp.int32, (tile, own), 1)
    own_visible = (col <= row) & (col < live)
    contract = (((1,), (1,)), ((), ()))
    results = []
    for in_head in (first, jnp.logical_not(first)):
        query_head = jnp.where(in_head, query, jnp.zeros_like(query))
        scores = lax.dot_general(
            query_head, k_ref[...], contract, preferred_element_type=jnp.float32
        ) * (1.0 / math.sqrt(HD))
        weights = jnp.where(own_visible, jnp.exp(scores), 0.0)
        total = jnp.sum(weights, axis=1, keepdims=True)
        mixed = jnp.dot(
            weights.astype(jnp.bfloat16), v_ref[...], preferred_element_type=jnp.float32
        )
        for page in range(PMAX):
            key_page = page_refs[page]
            value_page = page_refs[PMAX + page]
            scores = lax.dot_general(
                query_head, key_page[...], contract, preferred_element_type=jnp.float32
            ) * (1.0 / math.sqrt(HD))
            weights = jnp.where(page < depth, jnp.exp(scores), 0.0)
            total = total + jnp.sum(weights, axis=1, keepdims=True)
            mixed = mixed + jnp.dot(
                weights.astype(jnp.bfloat16), value_page[...], preferred_element_type=jnp.float32
            )
        results.append(mixed / total)
    out_ref[...] = jnp.where(first, results[0], results[1]).astype(out_ref.dtype)


def attention(queries, key_rows, value_rows, pages, req_len, prefix_len):
    tokens, width = queries.shape
    tile = 256
    lanes = 2 * HD
    grid = (width // lanes, tokens // tile)
    own_spec = pl.BlockSpec((tokens, lanes), lambda h, t, *_: (0, h))
    key_spec = pl.BlockSpec((None, PAGE, lanes), lambda h, t, *_: (0, 0, h))
    value_spec = pl.BlockSpec((None, PAGE, lanes), lambda h, t, *_: (1, 0, h))
    tile_spec = pl.BlockSpec((tile, lanes), lambda h, t, *_: (t, h))
    grid_spec = pltpu.PrefetchScalarGridSpec(
        num_scalar_prefetch=2,
        grid=grid,
        in_specs=[tile_spec, own_spec, own_spec] + [key_spec] * PMAX + [value_spec] * PMAX,
        out_specs=tile_spec,
    )
    return pl.pallas_call(
        attention_kernel,
        out_shape=jax.ShapeDtypeStruct((tokens, width), jnp.bfloat16),
        grid_spec=grid_spec,
    )(req_len, prefix_len, queries, key_rows, value_rows, *pages, *pages)


def gather_kernel(devices, pages_ref, keys_hbm, values_hbm, *refs):
    outs, sems = refs[:PMAX], refs[PMAX]
    here = lax.axis_index("blk")
    count = keys_hbm.shape[0]
    copies = []
    for slot_index in range(PMAX):
        offset = slot_index * devices // PMAX + 1
        asker = lax.rem(here + (devices - offset), devices)
        local = lax.rem(pages_ref[asker, slot_index], count)
        for part, source in enumerate((keys_hbm, values_hbm)):
            copy = pltpu.make_async_copy(
                source.at[local], outs[slot_index].at[part], sems.at[2 * slot_index + part]
            )
            copy.start()
            copies.append(copy)
    for copy in copies:
        copy.wait()


def fetch_pages(pool_keys, pool_values, prefix_pages):
    devices = lax.axis_size("blk")
    page_shape = jax.ShapeDtypeStruct((2,) + pool_keys.shape[1:], pool_keys.dtype)
    grid_spec = pltpu.PrefetchScalarGridSpec(
        num_scalar_prefetch=1,
        grid=(),
        in_specs=[pl.BlockSpec(memory_space=pl.ANY)] * 2,
        out_specs=[pl.BlockSpec(memory_space=pltpu.VMEM)] * PMAX,
        scratch_shapes=[pltpu.SemaphoreType.DMA((2 * PMAX,))],
    )
    gathered = pl.pallas_call(
        functools.partial(gather_kernel, devices),
        out_shape=[page_shape] * PMAX,
        grid_spec=grid_spec,
    )(prefix_pages, pool_keys, pool_values)
    return [
        from_behind(gathered[slot_index], "blk", devices - (slot_index * devices // PMAX + 1))
        for slot_index in range(PMAX)
    ]


def relay(key_rows, value_rows, placement):
    devices = lax.axis_size("blk")
    here = lax.axis_index("blk")
    blocks = key_rows.shape[0] // PAGE
    width = key_rows.shape[1]
    key_pages = key_rows.reshape(blocks, PAGE, width)
    value_pages = value_rows.reshape(blocks, PAGE, width)
    key_out = jnp.zeros_like(key_pages)
    value_out = jnp.zeros_like(value_pages)
    for block_index in range(blocks):
        offset = (2 * block_index + 1) * devices // (2 * blocks)
        received = from_behind(
            jnp.stack([key_pages[block_index], value_pages[block_index]]), "blk", offset
        )
        source = (here - offset) % devices
        target = placement[source * blocks + block_index] % blocks
        key_out = lax.dynamic_update_index_in_dim(key_out, received[0], target, 0)
        value_out = lax.dynamic_update_index_in_dim(value_out, received[1], target, 0)
    return (key_out, value_out)


def body(
    hidden_in,
    w_query,
    w_key,
    w_value,
    w_out,
    head_gain,
    eigen_rate,
    pool_keys,
    pool_values,
    req_len,
    prefix_len,
    prefix_pages,
    placement,
):
    tokens_here = hidden_in.shape[0]
    other_w_out = from_behind(w_out, "kv", 1)
    width_half = w_query.shape[1]
    heads_here = width_half // HD
    hidden_f = hidden_in.astype(jnp.float32)
    row_scale = lax.rsqrt(jnp.mean(hidden_f * hidden_f, axis=-1, keepdims=True) + epsilon)
    anchor = hidden_f * row_scale
    queries, key_rows, value_rows = projections(
        hidden_in, row_scale, w_query, w_key, w_value, head_gain
    )
    fetched = fetch_pages(pool_keys, pool_values, prefix_pages)
    attended = attention(queries, key_rows, value_rows, fetched, req_len, prefix_len)
    other_attended = from_behind(attended, "kv", 1)
    branch = jnp.dot(
        in_kv_order(attended, other_attended, 1),
        in_kv_order(w_out, other_w_out, 0),
        preferred_element_type=jnp.float32,
    )
    updated = anchor + eigen_rate * (rms_scale(branch) - anchor)
    layer_out = rms_scale(updated).astype(jnp.bfloat16)
    new_keys, new_values = relay(key_rows, value_rows, placement)
    return (layer_out, new_keys, new_values)


def solution(mesh):
    in_specs = (
        P("blk", None),
        P(None, "kv"),
        P(None, "kv"),
        P(None, "kv"),
        P("kv", None),
        P("kv"),
        P(),
        P("blk", None, "kv"),
        P("blk", None, "kv"),
        P("blk"),
        P("blk"),
        P(),
        P(),
    )
    out_specs = (P("blk", None), P("blk", None, "kv"), P("blk", None, "kv"))
    return jax.shard_map(body, mesh=mesh, in_specs=in_specs, out_specs=out_specs, check_vma=False)
```

```python
import functools
import math

import jax
import jax.numpy as jnp
from jax import lax
from jax.experimental import pallas as pl
from jax.experimental.pallas import tpu as pltpu
from jax.sharding import PartitionSpec as P

HD = 64
PAGE = 256
PMAX = 4


epsilon = 1e-06


def from_behind(block, axis, distance):
    devices = range(lax.axis_size(axis))
    route = [((i - distance) % len(devices), i) for i in devices]
    return lax.ppermute(block, axis, route)


def rms_scale(values):
    return values * lax.rsqrt(jnp.mean(values * values, axis=-1, keepdims=True) + epsilon)


def head_normed(projected, head_gain):
    count = projected.shape[0]
    split_heads = projected.reshape(count, -1, HD)
    return (rms_scale(split_heads).reshape(count, -1) * head_gain).astype(jnp.bfloat16)


def attend(query_heads, key_rows, value_rows, visible):
    key_heads = key_rows.reshape(key_rows.shape[0], -1, HD)
    value_heads = value_rows.reshape(value_rows.shape[0], -1, HD)
    scores = jnp.einsum(
        "qhd,khd->hqk", query_heads, key_heads, preferred_element_type=jnp.float32
    ) / math.sqrt(HD)
    weights = jnp.where(visible, jnp.exp(scores), 0.0)
    totals = jnp.sum(weights, axis=-1)
    mixed = jnp.einsum(
        "hqk,khd->qhd",
        weights.astype(jnp.bfloat16),
        value_heads,
        preferred_element_type=jnp.float32,
    )
    return (totals, mixed)


def in_kv_order(mine, other, axis):
    first = lax.axis_index("kv") == 0
    low = jnp.where(first, mine, other)
    high = jnp.where(first, other, mine)
    return jnp.concatenate([low, high], axis=axis)


def projection_kernel(x_ref, scale_ref, wq_ref, wk_ref, wv_ref, gain_ref, q_ref, k_ref, v_ref):
    hidden = x_ref[...]
    lane = lax.broadcasted_iota(jnp.int32, q_ref.shape, 1)
    first = lane < HD

    def normed(w_ref):
        projected = jnp.dot(hidden, w_ref[...], preferred_element_type=jnp.float32)
        squares = projected * projected
        low = jnp.sum(jnp.where(first, squares, 0.0), axis=1, keepdims=True)
        high = jnp.sum(jnp.where(first, 0.0, squares), axis=1, keepdims=True)
        mean = jnp.where(first, low, high) / HD
        return projected * lax.rsqrt(mean + epsilon) * gain_ref[...]

    q_ref[...] = normed(wq_ref).astype(q_ref.dtype)
    k_ref[...] = normed(wk_ref).astype(k_ref.dtype)
    projected = jnp.dot(hidden, wv_ref[...], preferred_element_type=jnp.float32)
    v_ref[...] = (projected * scale_ref[...]).astype(v_ref.dtype)


def projections(hidden_in, row_scale, w_query, w_key, w_value, head_gain):
    tokens, width = hidden_in.shape
    lanes = 2 * HD
    columns = w_query.shape[1]
    weight_spec = pl.BlockSpec((width, lanes), lambda j: (0, j))
    out_spec = pl.BlockSpec((tokens, lanes), lambda j: (0, j))
    shape = jax.ShapeDtypeStruct((tokens, columns), jnp.bfloat16)
    return pl.pallas_call(
        projection_kernel,
        out_shape=(shape, shape, shape),
        grid=(columns // lanes,),
        in_specs=[
            pl.BlockSpec((tokens, width), lambda j: (0, 0)),
            pl.BlockSpec((tokens, 1), lambda j: (0, 0)),
            weight_spec,
            weight_spec,
            weight_spec,
            pl.BlockSpec((1, lanes), lambda j: (0, j)),
        ],
        out_specs=[out_spec, out_spec, out_spec],
    )(hidden_in, row_scale, w_query, w_key, w_value, head_gain.reshape(1, columns))


def attention_kernel(live_ref, depth_ref, q_ref, k_ref, v_ref, *refs):
    page_refs, out_ref = refs[:-1], refs[-1]
    tile = q_ref.shape[0]
    own = k_ref.shape[0]
    live = live_ref[0]
    depth = depth_ref[0]
    query = q_ref[...]
    lane = lax.broadcasted_iota(jnp.int32, query.shape, 1)
    first = lane < HD
    row = pl.program_id(1) * tile + lax.broadcasted_iota(jnp.int32, (tile, own), 0)
    col = lax.broadcasted_iota(jnp.int32, (tile, own), 1)
    own_visible = (col <= row) & (col < live)
    contract = (((1,), (1,)), ((), ()))
    results = []
    for in_head in (first, jnp.logical_not(first)):
        query_head = jnp.where(in_head, query, jnp.zeros_like(query))
        scores = lax.dot_general(
            query_head, k_ref[...], contract, preferred_element_type=jnp.float32
        ) * (1.0 / math.sqrt(HD))
        weights = jnp.where(own_visible, jnp.exp(scores), 0.0)
        total = jnp.sum(weights, axis=1, keepdims=True)
        mixed = jnp.dot(
            weights.astype(jnp.bfloat16), v_ref[...], preferred_element_type=jnp.float32
        )
        for page in range(PMAX):
            key_page = page_refs[page]
            value_page = page_refs[PMAX + page]
            scores = lax.dot_general(
                query_head, key_page[...], contract, preferred_element_type=jnp.float32
            ) * (1.0 / math.sqrt(HD))
            weights = jnp.where(page < depth, jnp.exp(scores), 0.0)
            total = total + jnp.sum(weights, axis=1, keepdims=True)
            mixed = mixed + jnp.dot(
                weights.astype(jnp.bfloat16), value_page[...], preferred_element_type=jnp.float32
            )
        results.append(mixed / total)
    out_ref[...] = jnp.where(first, results[0], results[1]).astype(out_ref.dtype)


def attention(queries, key_rows, value_rows, pages, req_len, prefix_len, first_pair, pairs):
    tokens = queries.shape[0]
    tile = 256
    lanes = 2 * HD
    width = pairs * lanes
    grid = (pairs, tokens // tile)
    own_spec = pl.BlockSpec((tokens, lanes), lambda h, t, *_: (0, h + first_pair))
    key_spec = pl.BlockSpec((None, PAGE, lanes), lambda h, t, *_: (0, 0, h + first_pair))
    value_spec = pl.BlockSpec((None, PAGE, lanes), lambda h, t, *_: (1, 0, h + first_pair))
    tile_spec = pl.BlockSpec((tile, lanes), lambda h, t, *_: (t, h + first_pair))
    out_spec = pl.BlockSpec((tile, lanes), lambda h, t, *_: (t, h))
    grid_spec = pltpu.PrefetchScalarGridSpec(
        num_scalar_prefetch=2,
        grid=grid,
        in_specs=[tile_spec, own_spec, own_spec] + [key_spec] * PMAX + [value_spec] * PMAX,
        out_specs=out_spec,
    )
    return pl.pallas_call(
        attention_kernel,
        out_shape=jax.ShapeDtypeStruct((tokens, width), jnp.bfloat16),
        grid_spec=grid_spec,
    )(req_len, prefix_len, queries, key_rows, value_rows, *pages, *pages)


def gather_kernel(devices, pages_ref, keys_hbm, values_hbm, *refs):
    outs, sems = refs[:PMAX], refs[PMAX]
    here = lax.axis_index("blk")
    count = keys_hbm.shape[0]
    copies = []
    for slot_index in range(PMAX):
        offset = slot_index * devices // PMAX + 1
        asker = lax.rem(here + (devices - offset), devices)
        local = lax.rem(pages_ref[asker, slot_index], count)
        for part, source in enumerate((keys_hbm, values_hbm)):
            copy = pltpu.make_async_copy(
                source.at[local], outs[slot_index].at[part], sems.at[2 * slot_index + part]
            )
            copy.start()
            copies.append(copy)
    for copy in copies:
        copy.wait()


def fetch_pages(pool_keys, pool_values, prefix_pages):
    devices = lax.axis_size("blk")
    page_shape = jax.ShapeDtypeStruct((2,) + pool_keys.shape[1:], pool_keys.dtype)
    grid_spec = pltpu.PrefetchScalarGridSpec(
        num_scalar_prefetch=1,
        grid=(),
        in_specs=[pl.BlockSpec(memory_space=pl.ANY)] * 2,
        out_specs=[pl.BlockSpec(memory_space=pltpu.VMEM)] * PMAX,
        scratch_shapes=[pltpu.SemaphoreType.DMA((2 * PMAX,))],
    )
    gathered = pl.pallas_call(
        functools.partial(gather_kernel, devices),
        out_shape=[page_shape] * PMAX,
        grid_spec=grid_spec,
    )(prefix_pages, pool_keys, pool_values)
    return [
        from_behind(gathered[slot_index], "blk", devices - (slot_index * devices // PMAX + 1))
        for slot_index in range(PMAX)
    ]


def relay(key_rows, value_rows, placement):
    devices = lax.axis_size("blk")
    here = lax.axis_index("blk")
    blocks = key_rows.shape[0] // PAGE
    width = key_rows.shape[1]
    key_pages = key_rows.reshape(blocks, PAGE, width)
    value_pages = value_rows.reshape(blocks, PAGE, width)
    key_out = jnp.zeros_like(key_pages)
    value_out = jnp.zeros_like(value_pages)
    for block_index in range(blocks):
        offset = (2 * block_index + 1) * devices // (2 * blocks)
        received = from_behind(
            jnp.stack([key_pages[block_index], value_pages[block_index]]), "blk", offset
        )
        source = (here - offset) % devices
        target = placement[source * blocks + block_index] % blocks
        key_out = lax.dynamic_update_index_in_dim(key_out, received[0], target, 0)
        value_out = lax.dynamic_update_index_in_dim(value_out, received[1], target, 0)
    return (key_out, value_out)


def body(
    hidden_in,
    w_query,
    w_key,
    w_value,
    w_out,
    head_gain,
    eigen_rate,
    pool_keys,
    pool_values,
    req_len,
    prefix_len,
    prefix_pages,
    placement,
):
    tokens_here = hidden_in.shape[0]
    other_w_out = from_behind(w_out, "kv", 1)
    width_half = w_query.shape[1]
    heads_here = width_half // HD
    hidden_f = hidden_in.astype(jnp.float32)
    row_scale = lax.rsqrt(jnp.mean(hidden_f * hidden_f, axis=-1, keepdims=True) + epsilon)
    anchor = hidden_f * row_scale
    queries, key_rows, value_rows = projections(
        hidden_in, row_scale, w_query, w_key, w_value, head_gain
    )
    fetched = fetch_pages(pool_keys, pool_values, prefix_pages)
    pairs_here = width_half // (2 * HD)
    split = (pairs_here + 1) // 2
    parts = [
        attention(queries, key_rows, value_rows, fetched, req_len, prefix_len, first, count)
        for first, count in ((0, split), (split, pairs_here - split))
    ]
    other_parts = [from_behind(part, "kv", 1) for part in parts]
    attended = jnp.concatenate(parts, axis=1)
    other_attended = jnp.concatenate(other_parts, axis=1)
    branch = jnp.dot(
        in_kv_order(attended, other_attended, 1),
        in_kv_order(w_out, other_w_out, 0),
        preferred_element_type=jnp.float32,
    )
    updated = anchor + eigen_rate * (rms_scale(branch) - anchor)
    layer_out = rms_scale(updated).astype(jnp.bfloat16)
    new_keys, new_values = relay(key_rows, value_rows, placement)
    return (layer_out, new_keys, new_values)


def solution(mesh):
    in_specs = (
        P("blk", None),
        P(None, "kv"),
        P(None, "kv"),
        P(None, "kv"),
        P("kv", None),
        P("kv"),
        P(),
        P("blk", None, "kv"),
        P("blk", None, "kv"),
        P("blk"),
        P("blk"),
        P(),
        P(),
    )
    out_specs = (P("blk", None), P("blk", None, "kv"), P("blk", None, "kv"))
    return jax.shard_map(body, mesh=mesh, in_specs=in_specs, out_specs=out_specs, check_vma=False)
```

```python
import functools
import math

import jax
import jax.numpy as jnp
from jax import lax
from jax.experimental import pallas as pl
from jax.experimental.pallas import tpu as pltpu
from jax.sharding import PartitionSpec as P

HD = 64
PAGE = 256
PMAX = 4


epsilon = 1e-06


def from_behind(block, axis, distance):
    devices = range(lax.axis_size(axis))
    route = [((i - distance) % len(devices), i) for i in devices]
    return lax.ppermute(block, axis, route)


def rms_scale(values):
    return values * lax.rsqrt(jnp.mean(values * values, axis=-1, keepdims=True) + epsilon)


def head_normed(projected, head_gain):
    count = projected.shape[0]
    split_heads = projected.reshape(count, -1, HD)
    return (rms_scale(split_heads).reshape(count, -1) * head_gain).astype(jnp.bfloat16)


def attend(query_heads, key_rows, value_rows, visible):
    key_heads = key_rows.reshape(key_rows.shape[0], -1, HD)
    value_heads = value_rows.reshape(value_rows.shape[0], -1, HD)
    scores = jnp.einsum(
        "qhd,khd->hqk", query_heads, key_heads, preferred_element_type=jnp.float32
    ) / math.sqrt(HD)
    weights = jnp.where(visible, jnp.exp(scores), 0.0)
    totals = jnp.sum(weights, axis=-1)
    mixed = jnp.einsum(
        "hqk,khd->qhd",
        weights.astype(jnp.bfloat16),
        value_heads,
        preferred_element_type=jnp.float32,
    )
    return (totals, mixed)


def other_half_once_per_chip(w_out):
    rows = w_out.shape[0] // 2
    core = lax.axis_index("blk") % 2
    mine = lax.dynamic_slice_in_dim(w_out, core * rows, rows, 0)
    pulled = from_behind(mine, "kv", 1)
    devices = lax.axis_size("blk")
    swapped = lax.ppermute(pulled, "blk", [(i, i ^ 1) for i in range(devices)])
    first = core == 0
    return jnp.concatenate(
        [jnp.where(first, pulled, swapped), jnp.where(first, swapped, pulled)], axis=0
    )


def in_kv_order(mine, other, axis):
    first = lax.axis_index("kv") == 0
    low = jnp.where(first, mine, other)
    high = jnp.where(first, other, mine)
    return jnp.concatenate([low, high], axis=axis)


def projection_kernel(x_ref, scale_ref, wq_ref, wk_ref, wv_ref, gain_ref, q_ref, k_ref, v_ref):
    hidden = x_ref[...]
    lane = lax.broadcasted_iota(jnp.int32, q_ref.shape, 1)
    first = lane < HD

    def normed(w_ref):
        projected = jnp.dot(hidden, w_ref[...], preferred_element_type=jnp.float32)
        squares = projected * projected
        low = jnp.sum(jnp.where(first, squares, 0.0), axis=1, keepdims=True)
        high = jnp.sum(jnp.where(first, 0.0, squares), axis=1, keepdims=True)
        mean = jnp.where(first, low, high) / HD
        return projected * lax.rsqrt(mean + epsilon) * gain_ref[...]

    q_ref[...] = normed(wq_ref).astype(q_ref.dtype)
    k_ref[...] = normed(wk_ref).astype(k_ref.dtype)
    projected = jnp.dot(hidden, wv_ref[...], preferred_element_type=jnp.float32)
    v_ref[...] = (projected * scale_ref[...]).astype(v_ref.dtype)


def projections(hidden_in, row_scale, w_query, w_key, w_value, head_gain):
    tokens, width = hidden_in.shape
    lanes = 2 * HD
    columns = w_query.shape[1]
    weight_spec = pl.BlockSpec((width, lanes), lambda j: (0, j))
    out_spec = pl.BlockSpec((tokens, lanes), lambda j: (0, j))
    shape = jax.ShapeDtypeStruct((tokens, columns), jnp.bfloat16)
    return pl.pallas_call(
        projection_kernel,
        out_shape=(shape, shape, shape),
        grid=(columns // lanes,),
        in_specs=[
            pl.BlockSpec((tokens, width), lambda j: (0, 0)),
            pl.BlockSpec((tokens, 1), lambda j: (0, 0)),
            weight_spec,
            weight_spec,
            weight_spec,
            pl.BlockSpec((1, lanes), lambda j: (0, j)),
        ],
        out_specs=[out_spec, out_spec, out_spec],
    )(hidden_in, row_scale, w_query, w_key, w_value, head_gain.reshape(1, columns))


def attention_kernel(live_ref, depth_ref, q_ref, k_ref, v_ref, *refs):
    page_refs, out_ref = refs[:-1], refs[-1]
    tile = q_ref.shape[0]
    own = k_ref.shape[0]
    live = live_ref[0]
    depth = depth_ref[0]
    query = q_ref[...]
    lane = lax.broadcasted_iota(jnp.int32, query.shape, 1)
    first = lane < HD
    row = pl.program_id(1) * tile + lax.broadcasted_iota(jnp.int32, (tile, own), 0)
    col = lax.broadcasted_iota(jnp.int32, (tile, own), 1)
    own_visible = (col <= row) & (col < live)
    contract = (((1,), (1,)), ((), ()))
    results = []
    for in_head in (first, jnp.logical_not(first)):
        query_head = jnp.where(in_head, query, jnp.zeros_like(query))
        scores = lax.dot_general(
            query_head, k_ref[...], contract, preferred_element_type=jnp.float32
        ) * (1.0 / math.sqrt(HD))
        weights = jnp.where(own_visible, jnp.exp(scores), 0.0)
        total = jnp.sum(weights, axis=1, keepdims=True)
        mixed = jnp.dot(
            weights.astype(jnp.bfloat16), v_ref[...], preferred_element_type=jnp.float32
        )
        for page in range(PMAX):
            key_page = page_refs[page]
            value_page = page_refs[PMAX + page]
            scores = lax.dot_general(
                query_head, key_page[...], contract, preferred_element_type=jnp.float32
            ) * (1.0 / math.sqrt(HD))
            weights = jnp.where(page < depth, jnp.exp(scores), 0.0)
            total = total + jnp.sum(weights, axis=1, keepdims=True)
            mixed = mixed + jnp.dot(
                weights.astype(jnp.bfloat16), value_page[...], preferred_element_type=jnp.float32
            )
        results.append(mixed / total)
    out_ref[...] = jnp.where(first, results[0], results[1]).astype(out_ref.dtype)


def attention(queries, key_rows, value_rows, pages, req_len, prefix_len, first_pair, pairs):
    tokens = queries.shape[0]
    tile = 256
    lanes = 2 * HD
    width = pairs * lanes
    grid = (pairs, tokens // tile)
    own_spec = pl.BlockSpec((tokens, lanes), lambda h, t, *_: (0, h + first_pair))
    key_spec = pl.BlockSpec((None, PAGE, lanes), lambda h, t, *_: (0, 0, h + first_pair))
    value_spec = pl.BlockSpec((None, PAGE, lanes), lambda h, t, *_: (1, 0, h + first_pair))
    tile_spec = pl.BlockSpec((tile, lanes), lambda h, t, *_: (t, h + first_pair))
    out_spec = pl.BlockSpec((tile, lanes), lambda h, t, *_: (t, h))
    grid_spec = pltpu.PrefetchScalarGridSpec(
        num_scalar_prefetch=2,
        grid=grid,
        in_specs=[tile_spec, own_spec, own_spec] + [key_spec] * PMAX + [value_spec] * PMAX,
        out_specs=out_spec,
    )
    return pl.pallas_call(
        attention_kernel,
        out_shape=jax.ShapeDtypeStruct((tokens, width), jnp.bfloat16),
        grid_spec=grid_spec,
    )(req_len, prefix_len, queries, key_rows, value_rows, *pages, *pages)


def gather_kernel(devices, pages_ref, keys_hbm, values_hbm, *refs):
    outs, sems = refs[:PMAX], refs[PMAX]
    here = lax.axis_index("blk")
    count = keys_hbm.shape[0]
    copies = []
    for slot_index in range(PMAX):
        offset = slot_index * devices // PMAX + 1
        asker = lax.rem(here + (devices - offset), devices)
        local = lax.rem(pages_ref[asker, slot_index], count)
        for part, source in enumerate((keys_hbm, values_hbm)):
            copy = pltpu.make_async_copy(
                source.at[local], outs[slot_index].at[part], sems.at[2 * slot_index + part]
            )
            copy.start()
            copies.append(copy)
    for copy in copies:
        copy.wait()


def fetch_pages(pool_keys, pool_values, prefix_pages):
    devices = lax.axis_size("blk")
    page_shape = jax.ShapeDtypeStruct((2,) + pool_keys.shape[1:], pool_keys.dtype)
    grid_spec = pltpu.PrefetchScalarGridSpec(
        num_scalar_prefetch=1,
        grid=(),
        in_specs=[pl.BlockSpec(memory_space=pl.ANY)] * 2,
        out_specs=[pl.BlockSpec(memory_space=pltpu.VMEM)] * PMAX,
        scratch_shapes=[pltpu.SemaphoreType.DMA((2 * PMAX,))],
    )
    gathered = pl.pallas_call(
        functools.partial(gather_kernel, devices),
        out_shape=[page_shape] * PMAX,
        grid_spec=grid_spec,
    )(prefix_pages, pool_keys, pool_values)
    return [
        from_behind(gathered[slot_index], "blk", devices - (slot_index * devices // PMAX + 1))
        for slot_index in range(PMAX)
    ]


def relay(key_rows, value_rows, placement):
    devices = lax.axis_size("blk")
    here = lax.axis_index("blk")
    blocks = key_rows.shape[0] // PAGE
    width = key_rows.shape[1]
    key_pages = key_rows.reshape(blocks, PAGE, width)
    value_pages = value_rows.reshape(blocks, PAGE, width)
    key_out = jnp.zeros_like(key_pages)
    value_out = jnp.zeros_like(value_pages)
    for block_index in range(blocks):
        offset = (2 * block_index + 1) * devices // (2 * blocks)
        received = from_behind(
            jnp.stack([key_pages[block_index], value_pages[block_index]]), "blk", offset
        )
        source = (here - offset) % devices
        target = placement[source * blocks + block_index] % blocks
        key_out = lax.dynamic_update_index_in_dim(key_out, received[0], target, 0)
        value_out = lax.dynamic_update_index_in_dim(value_out, received[1], target, 0)
    return (key_out, value_out)


def body(
    hidden_in,
    w_query,
    w_key,
    w_value,
    w_out,
    head_gain,
    eigen_rate,
    pool_keys,
    pool_values,
    req_len,
    prefix_len,
    prefix_pages,
    placement,
):
    tokens_here = hidden_in.shape[0]
    other_w_out = other_half_once_per_chip(w_out)
    width_half = w_query.shape[1]
    heads_here = width_half // HD
    hidden_f = hidden_in.astype(jnp.float32)
    row_scale = lax.rsqrt(jnp.mean(hidden_f * hidden_f, axis=-1, keepdims=True) + epsilon)
    anchor = hidden_f * row_scale
    queries, key_rows, value_rows = projections(
        hidden_in, row_scale, w_query, w_key, w_value, head_gain
    )
    fetched = fetch_pages(pool_keys, pool_values, prefix_pages)
    pairs_here = width_half // (2 * HD)
    split = (pairs_here + 1) // 2
    parts = [
        attention(queries, key_rows, value_rows, fetched, req_len, prefix_len, first, count)
        for first, count in ((0, split), (split, pairs_here - split))
    ]
    other_parts = [from_behind(part, "kv", 1) for part in parts]
    attended = jnp.concatenate(parts, axis=1)
    other_attended = jnp.concatenate(other_parts, axis=1)
    branch = jnp.dot(
        in_kv_order(attended, other_attended, 1),
        in_kv_order(w_out, other_w_out, 0),
        preferred_element_type=jnp.float32,
    )
    updated = anchor + eigen_rate * (rms_scale(branch) - anchor)
    layer_out = rms_scale(updated).astype(jnp.bfloat16)
    new_keys, new_values = relay(key_rows, value_rows, placement)
    return (layer_out, new_keys, new_values)


def solution(mesh):
    in_specs = (
        P("blk", None),
        P(None, "kv"),
        P(None, "kv"),
        P(None, "kv"),
        P("kv", None),
        P("kv"),
        P(),
        P("blk", None, "kv"),
        P("blk", None, "kv"),
        P("blk"),
        P("blk"),
        P(),
        P(),
    )
    out_specs = (P("blk", None), P("blk", None, "kv"), P("blk", None, "kv"))
    return jax.shard_map(body, mesh=mesh, in_specs=in_specs, out_specs=out_specs, check_vma=False)
```

```python
import functools
import math

import jax
import jax.numpy as jnp
from jax import lax
from jax.experimental import pallas as pl
from jax.experimental.pallas import tpu as pltpu
from jax.sharding import PartitionSpec as P

HD = 64
PAGE = 256
PMAX = 4


epsilon = 1e-06


def from_behind(block, axis, distance):
    devices = range(lax.axis_size(axis))
    route = [((i - distance) % len(devices), i) for i in devices]
    return lax.ppermute(block, axis, route)


def rms_scale(values):
    return values * lax.rsqrt(jnp.mean(values * values, axis=-1, keepdims=True) + epsilon)


def head_normed(projected, head_gain):
    count = projected.shape[0]
    split_heads = projected.reshape(count, -1, HD)
    return (rms_scale(split_heads).reshape(count, -1) * head_gain).astype(jnp.bfloat16)


def attend(query_heads, key_rows, value_rows, visible):
    key_heads = key_rows.reshape(key_rows.shape[0], -1, HD)
    value_heads = value_rows.reshape(value_rows.shape[0], -1, HD)
    scores = jnp.einsum(
        "qhd,khd->hqk", query_heads, key_heads, preferred_element_type=jnp.float32
    ) / math.sqrt(HD)
    weights = jnp.where(visible, jnp.exp(scores), 0.0)
    totals = jnp.sum(weights, axis=-1)
    mixed = jnp.einsum(
        "hqk,khd->qhd",
        weights.astype(jnp.bfloat16),
        value_heads,
        preferred_element_type=jnp.float32,
    )
    return (totals, mixed)


def other_half_once_per_chip(w_out):
    rows = w_out.shape[0] // 2
    core = lax.axis_index("blk") % 2
    mine = lax.dynamic_slice_in_dim(w_out, core * rows, rows, 0)
    pulled = from_behind(mine, "kv", 1)
    devices = lax.axis_size("blk")
    swapped = lax.ppermute(pulled, "blk", [(i, i ^ 1) for i in range(devices)])
    first = core == 0
    return jnp.concatenate(
        [jnp.where(first, pulled, swapped), jnp.where(first, swapped, pulled)], axis=0
    )


def in_kv_order(mine, other, axis):
    first = lax.axis_index("kv") == 0
    low = jnp.where(first, mine, other)
    high = jnp.where(first, other, mine)
    return jnp.concatenate([low, high], axis=axis)


def projection_kernel(x_ref, scale_ref, wq_ref, wk_ref, wv_ref, gain_ref, q_ref, k_ref, v_ref):
    hidden = x_ref[...]
    lane = lax.broadcasted_iota(jnp.int32, q_ref.shape, 1)
    first = lane < HD

    def normed(w_ref):
        projected = jnp.dot(hidden, w_ref[...], preferred_element_type=jnp.float32)
        squares = projected * projected
        low = jnp.sum(jnp.where(first, squares, 0.0), axis=1, keepdims=True)
        high = jnp.sum(jnp.where(first, 0.0, squares), axis=1, keepdims=True)
        mean = jnp.where(first, low, high) / HD
        return projected * lax.rsqrt(mean + epsilon) * gain_ref[...]

    q_ref[...] = normed(wq_ref).astype(q_ref.dtype)
    k_ref[...] = normed(wk_ref).astype(k_ref.dtype)
    projected = jnp.dot(hidden, wv_ref[...], preferred_element_type=jnp.float32)
    v_ref[...] = (projected * scale_ref[...]).astype(v_ref.dtype)


def projections(hidden_in, row_scale, w_query, w_key, w_value, head_gain):
    tokens, width = hidden_in.shape
    lanes = 2 * HD
    columns = w_query.shape[1]
    weight_spec = pl.BlockSpec((width, lanes), lambda j: (0, j))
    out_spec = pl.BlockSpec((tokens, lanes), lambda j: (0, j))
    shape = jax.ShapeDtypeStruct((tokens, columns), jnp.bfloat16)
    return pl.pallas_call(
        projection_kernel,
        out_shape=(shape, shape, shape),
        grid=(columns // lanes,),
        in_specs=[
            pl.BlockSpec((tokens, width), lambda j: (0, 0)),
            pl.BlockSpec((tokens, 1), lambda j: (0, 0)),
            weight_spec,
            weight_spec,
            weight_spec,
            pl.BlockSpec((1, lanes), lambda j: (0, j)),
        ],
        out_specs=[out_spec, out_spec, out_spec],
    )(hidden_in, row_scale, w_query, w_key, w_value, head_gain.reshape(1, columns))


def attention_kernel(live_ref, depth_ref, q_ref, k_ref, v_ref, *refs):
    page_refs, out_ref = refs[:-1], refs[-1]
    tile = q_ref.shape[0]
    own = k_ref.shape[0]
    live = live_ref[0]
    depth = depth_ref[0]
    query = q_ref[...]
    lane = lax.broadcasted_iota(jnp.int32, query.shape, 1)
    first = lane < HD
    row = pl.program_id(1) * tile + lax.broadcasted_iota(jnp.int32, (tile, own), 0)
    col = lax.broadcasted_iota(jnp.int32, (tile, own), 1)
    own_visible = (col <= row) & (col < live)
    contract = (((1,), (1,)), ((), ()))
    results = []
    for in_head in (first, jnp.logical_not(first)):
        query_head = jnp.where(in_head, query, jnp.zeros_like(query))
        scores = lax.dot_general(
            query_head, k_ref[...], contract, preferred_element_type=jnp.float32
        ) * (1.0 / math.sqrt(HD))
        weights = jnp.where(own_visible, jnp.exp(scores), 0.0)
        total = jnp.sum(weights, axis=1, keepdims=True)
        mixed = jnp.dot(
            weights.astype(jnp.bfloat16), v_ref[...], preferred_element_type=jnp.float32
        )
        for page in range(PMAX):
            key_page = page_refs[page]
            value_page = page_refs[PMAX + page]
            scores = lax.dot_general(
                query_head, key_page[...], contract, preferred_element_type=jnp.float32
            ) * (1.0 / math.sqrt(HD))
            weights = jnp.where(page < depth, jnp.exp(scores), 0.0)
            total = total + jnp.sum(weights, axis=1, keepdims=True)
            mixed = mixed + jnp.dot(
                weights.astype(jnp.bfloat16), value_page[...], preferred_element_type=jnp.float32
            )
        results.append(mixed / total)
    out_ref[...] = jnp.where(first, results[0], results[1]).astype(out_ref.dtype)


def attention(queries, key_rows, value_rows, pages, req_len, prefix_len, first_pair, pairs):
    tokens = queries.shape[0]
    tile = 256
    lanes = 2 * HD
    width = pairs * lanes
    grid = (pairs, tokens // tile)
    own_spec = pl.BlockSpec((tokens, lanes), lambda h, t, *_: (0, h + first_pair))
    key_spec = pl.BlockSpec((None, PAGE, lanes), lambda h, t, *_: (0, 0, h + first_pair))
    value_spec = pl.BlockSpec((None, PAGE, lanes), lambda h, t, *_: (1, 0, h + first_pair))
    tile_spec = pl.BlockSpec((tile, lanes), lambda h, t, *_: (t, h + first_pair))
    out_spec = pl.BlockSpec((tile, lanes), lambda h, t, *_: (t, h))
    grid_spec = pltpu.PrefetchScalarGridSpec(
        num_scalar_prefetch=2,
        grid=grid,
        in_specs=[tile_spec, own_spec, own_spec] + [key_spec] * PMAX + [value_spec] * PMAX,
        out_specs=out_spec,
    )
    return pl.pallas_call(
        attention_kernel,
        out_shape=jax.ShapeDtypeStruct((tokens, width), jnp.bfloat16),
        grid_spec=grid_spec,
    )(req_len, prefix_len, queries, key_rows, value_rows, *pages, *pages)


def gather_kernel(devices, pages_ref, keys_hbm, values_hbm, *refs):
    outs, sems = refs[:PMAX], refs[PMAX]
    here = lax.axis_index("blk")
    count = keys_hbm.shape[0]
    copies = []
    for slot_index in range(PMAX):
        offset = slot_index * devices // PMAX + 1
        asker = lax.rem(here + (devices - offset), devices)
        local = lax.rem(pages_ref[asker, slot_index], count)
        for part, source in enumerate((keys_hbm, values_hbm)):
            copy = pltpu.make_async_copy(
                source.at[local], outs[slot_index].at[part], sems.at[2 * slot_index + part]
            )
            copy.start()
            copies.append(copy)
    for copy in copies:
        copy.wait()


def fetch_pages(pool_keys, pool_values, prefix_pages):
    devices = lax.axis_size("blk")
    page_shape = jax.ShapeDtypeStruct((2,) + pool_keys.shape[1:], pool_keys.dtype)
    grid_spec = pltpu.PrefetchScalarGridSpec(
        num_scalar_prefetch=1,
        grid=(),
        in_specs=[pl.BlockSpec(memory_space=pl.ANY)] * 2,
        out_specs=[pl.BlockSpec(memory_space=pltpu.VMEM)] * PMAX,
        scratch_shapes=[pltpu.SemaphoreType.DMA((2 * PMAX,))],
    )
    gathered = pl.pallas_call(
        functools.partial(gather_kernel, devices),
        out_shape=[page_shape] * PMAX,
        grid_spec=grid_spec,
    )(prefix_pages, pool_keys, pool_values)
    return [
        from_behind(gathered[slot_index], "blk", devices - (slot_index * devices // PMAX + 1))
        for slot_index in range(PMAX)
    ]


def relay(key_rows, value_rows, placement, after):
    devices = lax.axis_size("blk")
    here = lax.axis_index("blk")
    blocks = key_rows.shape[0] // PAGE
    width = key_rows.shape[1]
    key_pages = key_rows.reshape(blocks, PAGE, width)
    value_pages = value_rows.reshape(blocks, PAGE, width)
    key_out = jnp.zeros_like(key_pages)
    value_out = jnp.zeros_like(value_pages)
    stacks = [
        jnp.stack([key_pages[block_index], value_pages[block_index]])
        for block_index in range(blocks)
    ]
    stacks, _ = lax.optimization_barrier((stacks, after))
    for block_index in range(blocks):
        offset = (2 * block_index + 1) * devices // (2 * blocks)
        received = from_behind(stacks[block_index], "blk", offset)
        source = (here - offset) % devices
        target = placement[source * blocks + block_index] % blocks
        key_out = lax.dynamic_update_index_in_dim(key_out, received[0], target, 0)
        value_out = lax.dynamic_update_index_in_dim(value_out, received[1], target, 0)
    return (key_out, value_out)


def body(
    hidden_in,
    w_query,
    w_key,
    w_value,
    w_out,
    head_gain,
    eigen_rate,
    pool_keys,
    pool_values,
    req_len,
    prefix_len,
    prefix_pages,
    placement,
):
    tokens_here = hidden_in.shape[0]
    other_w_out = other_half_once_per_chip(w_out)
    width_half = w_query.shape[1]
    heads_here = width_half // HD
    hidden_f = hidden_in.astype(jnp.float32)
    row_scale = lax.rsqrt(jnp.mean(hidden_f * hidden_f, axis=-1, keepdims=True) + epsilon)
    anchor = hidden_f * row_scale
    queries, key_rows, value_rows = projections(
        hidden_in, row_scale, w_query, w_key, w_value, head_gain
    )
    fetched = fetch_pages(pool_keys, pool_values, prefix_pages)
    pairs_here = width_half // (2 * HD)
    split = (pairs_here + 1) // 2
    parts = [
        attention(queries, key_rows, value_rows, fetched, req_len, prefix_len, first, count)
        for first, count in ((0, split), (split, pairs_here - split))
    ]
    other_parts = [from_behind(part, "kv", 1) for part in parts]
    attended = jnp.concatenate(parts, axis=1)
    other_attended = jnp.concatenate(other_parts, axis=1)
    branch = jnp.dot(
        in_kv_order(attended, other_attended, 1),
        in_kv_order(w_out, other_w_out, 0),
        preferred_element_type=jnp.float32,
    )
    updated = anchor + eigen_rate * (rms_scale(branch) - anchor)
    layer_out = rms_scale(updated).astype(jnp.bfloat16)
    new_keys, new_values = relay(key_rows, value_rows, placement, fetched)
    return (layer_out, new_keys, new_values)


def solution(mesh):
    in_specs = (
        P("blk", None),
        P(None, "kv"),
        P(None, "kv"),
        P(None, "kv"),
        P("kv", None),
        P("kv"),
        P(),
        P("blk", None, "kv"),
        P("blk", None, "kv"),
        P("blk"),
        P("blk"),
        P(),
        P(),
    )
    out_specs = (P("blk", None), P("blk", None, "kv"), P("blk", None, "kv"))
    return jax.shard_map(body, mesh=mesh, in_specs=in_specs, out_specs=out_specs, check_vma=False)
```

```python
import functools
import math

import jax
import jax.numpy as jnp
from jax import lax
from jax.experimental import pallas as pl
from jax.experimental.pallas import tpu as pltpu
from jax.sharding import PartitionSpec as P

HD = 64
PAGE = 256
PMAX = 4


epsilon = 1e-06


def from_behind(block, axis, distance):
    devices = range(lax.axis_size(axis))
    route = [((i - distance) % len(devices), i) for i in devices]
    return lax.ppermute(block, axis, route)


def rms_scale(values):
    return values * lax.rsqrt(jnp.mean(values * values, axis=-1, keepdims=True) + epsilon)


def head_normed(projected, head_gain):
    count = projected.shape[0]
    split_heads = projected.reshape(count, -1, HD)
    return (rms_scale(split_heads).reshape(count, -1) * head_gain).astype(jnp.bfloat16)


def attend(query_heads, key_rows, value_rows, visible):
    key_heads = key_rows.reshape(key_rows.shape[0], -1, HD)
    value_heads = value_rows.reshape(value_rows.shape[0], -1, HD)
    scores = jnp.einsum(
        "qhd,khd->hqk", query_heads, key_heads, preferred_element_type=jnp.float32
    ) / math.sqrt(HD)
    weights = jnp.where(visible, jnp.exp(scores), 0.0)
    totals = jnp.sum(weights, axis=-1)
    mixed = jnp.einsum(
        "hqk,khd->qhd",
        weights.astype(jnp.bfloat16),
        value_heads,
        preferred_element_type=jnp.float32,
    )
    return (totals, mixed)


def other_half_once_per_group(w_out, group=4):
    rows = w_out.shape[0] // group
    devices = lax.axis_size("blk")
    member = lax.axis_index("blk") % group
    mine = lax.dynamic_slice_in_dim(w_out, member * rows, rows, 0)
    pulled = from_behind(mine, "kv", 1)
    received = [pulled] + [
        lax.ppermute(pulled, "blk", [(i, i ^ step) for i in range(devices)])
        for step in range(1, group)
    ]
    stacked = jnp.stack(received)
    chunks = [
        lax.dynamic_index_in_dim(stacked, lax.bitwise_xor(member, chunk), 0, keepdims=False)
        for chunk in range(group)
    ]
    return jnp.concatenate(chunks, axis=0)


def in_kv_order(mine, other, axis):
    first = lax.axis_index("kv") == 0
    low = jnp.where(first, mine, other)
    high = jnp.where(first, other, mine)
    return jnp.concatenate([low, high], axis=axis)


def projection_kernel(x_ref, scale_ref, wq_ref, wk_ref, wv_ref, gain_ref, q_ref, k_ref, v_ref):
    hidden = x_ref[...]
    lane = lax.broadcasted_iota(jnp.int32, q_ref.shape, 1)
    first = lane < HD

    def normed(w_ref):
        projected = jnp.dot(hidden, w_ref[...], preferred_element_type=jnp.float32)
        squares = projected * projected
        low = jnp.sum(jnp.where(first, squares, 0.0), axis=1, keepdims=True)
        high = jnp.sum(jnp.where(first, 0.0, squares), axis=1, keepdims=True)
        mean = jnp.where(first, low, high) / HD
        return projected * lax.rsqrt(mean + epsilon) * gain_ref[...]

    q_ref[...] = normed(wq_ref).astype(q_ref.dtype)
    k_ref[...] = normed(wk_ref).astype(k_ref.dtype)
    projected = jnp.dot(hidden, wv_ref[...], preferred_element_type=jnp.float32)
    v_ref[...] = (projected * scale_ref[...]).astype(v_ref.dtype)


def projections(hidden_in, row_scale, w_query, w_key, w_value, head_gain):
    tokens, width = hidden_in.shape
    lanes = 2 * HD
    columns = w_query.shape[1]
    weight_spec = pl.BlockSpec((width, lanes), lambda j: (0, j))
    out_spec = pl.BlockSpec((tokens, lanes), lambda j: (0, j))
    shape = jax.ShapeDtypeStruct((tokens, columns), jnp.bfloat16)
    return pl.pallas_call(
        projection_kernel,
        out_shape=(shape, shape, shape),
        grid=(columns // lanes,),
        in_specs=[
            pl.BlockSpec((tokens, width), lambda j: (0, 0)),
            pl.BlockSpec((tokens, 1), lambda j: (0, 0)),
            weight_spec,
            weight_spec,
            weight_spec,
            pl.BlockSpec((1, lanes), lambda j: (0, j)),
        ],
        out_specs=[out_spec, out_spec, out_spec],
    )(hidden_in, row_scale, w_query, w_key, w_value, head_gain.reshape(1, columns))


def attention_kernel(live_ref, depth_ref, q_ref, k_ref, v_ref, *refs):
    page_refs, out_ref = refs[:-1], refs[-1]
    tile = q_ref.shape[0]
    own = k_ref.shape[0]
    live = live_ref[0]
    depth = depth_ref[0]
    query = q_ref[...]
    lane = lax.broadcasted_iota(jnp.int32, query.shape, 1)
    first = lane < HD
    row = pl.program_id(1) * tile + lax.broadcasted_iota(jnp.int32, (tile, own), 0)
    col = lax.broadcasted_iota(jnp.int32, (tile, own), 1)
    own_visible = (col <= row) & (col < live)
    contract = (((1,), (1,)), ((), ()))
    results = []
    for in_head in (first, jnp.logical_not(first)):
        query_head = jnp.where(in_head, query, jnp.zeros_like(query))
        scores = lax.dot_general(
            query_head, k_ref[...], contract, preferred_element_type=jnp.float32
        ) * (1.0 / math.sqrt(HD))
        weights = jnp.where(own_visible, jnp.exp(scores), 0.0)
        total = jnp.sum(weights, axis=1, keepdims=True)
        mixed = jnp.dot(
            weights.astype(jnp.bfloat16), v_ref[...], preferred_element_type=jnp.float32
        )
        for page in range(PMAX):
            key_page = page_refs[page]
            value_page = page_refs[PMAX + page]
            scores = lax.dot_general(
                query_head, key_page[...], contract, preferred_element_type=jnp.float32
            ) * (1.0 / math.sqrt(HD))
            weights = jnp.where(page < depth, jnp.exp(scores), 0.0)
            total = total + jnp.sum(weights, axis=1, keepdims=True)
            mixed = mixed + jnp.dot(
                weights.astype(jnp.bfloat16), value_page[...], preferred_element_type=jnp.float32
            )
        results.append(mixed / total)
    out_ref[...] = jnp.where(first, results[0], results[1]).astype(out_ref.dtype)


def attention(queries, key_rows, value_rows, pages, req_len, prefix_len, first_pair, pairs):
    tokens = queries.shape[0]
    tile = 256
    lanes = 2 * HD
    width = pairs * lanes
    grid = (pairs, tokens // tile)
    own_spec = pl.BlockSpec((tokens, lanes), lambda h, t, *_: (0, h + first_pair))
    key_spec = pl.BlockSpec((None, PAGE, lanes), lambda h, t, *_: (0, 0, h + first_pair))
    value_spec = pl.BlockSpec((None, PAGE, lanes), lambda h, t, *_: (1, 0, h + first_pair))
    tile_spec = pl.BlockSpec((tile, lanes), lambda h, t, *_: (t, h + first_pair))
    out_spec = pl.BlockSpec((tile, lanes), lambda h, t, *_: (t, h))
    grid_spec = pltpu.PrefetchScalarGridSpec(
        num_scalar_prefetch=2,
        grid=grid,
        in_specs=[tile_spec, own_spec, own_spec] + [key_spec] * PMAX + [value_spec] * PMAX,
        out_specs=out_spec,
    )
    return pl.pallas_call(
        attention_kernel,
        out_shape=jax.ShapeDtypeStruct((tokens, width), jnp.bfloat16),
        grid_spec=grid_spec,
    )(req_len, prefix_len, queries, key_rows, value_rows, *pages, *pages)


def gather_kernel(devices, pages_ref, keys_hbm, values_hbm, *refs):
    outs, sems = refs[:PMAX], refs[PMAX]
    here = lax.axis_index("blk")
    count = keys_hbm.shape[0]
    copies = []
    for slot_index in range(PMAX):
        offset = slot_index * devices // PMAX + 1
        asker = lax.rem(here + (devices - offset), devices)
        local = lax.rem(pages_ref[asker, slot_index], count)
        for part, source in enumerate((keys_hbm, values_hbm)):
            copy = pltpu.make_async_copy(
                source.at[local], outs[slot_index].at[part], sems.at[2 * slot_index + part]
            )
            copy.start()
            copies.append(copy)
    for copy in copies:
        copy.wait()


def fetch_pages(pool_keys, pool_values, prefix_pages):
    devices = lax.axis_size("blk")
    page_shape = jax.ShapeDtypeStruct((2,) + pool_keys.shape[1:], pool_keys.dtype)
    grid_spec = pltpu.PrefetchScalarGridSpec(
        num_scalar_prefetch=1,
        grid=(),
        in_specs=[pl.BlockSpec(memory_space=pl.ANY)] * 2,
        out_specs=[pl.BlockSpec(memory_space=pltpu.VMEM)] * PMAX,
        scratch_shapes=[pltpu.SemaphoreType.DMA((2 * PMAX,))],
    )
    gathered = pl.pallas_call(
        functools.partial(gather_kernel, devices),
        out_shape=[page_shape] * PMAX,
        grid_spec=grid_spec,
    )(prefix_pages, pool_keys, pool_values)
    return [
        from_behind(gathered[slot_index], "blk", devices - (slot_index * devices // PMAX + 1))
        for slot_index in range(PMAX)
    ]


def relay(key_rows, value_rows, placement):
    devices = lax.axis_size("blk")
    here = lax.axis_index("blk")
    blocks = key_rows.shape[0] // PAGE
    width = key_rows.shape[1]
    key_pages = key_rows.reshape(blocks, PAGE, width)
    value_pages = value_rows.reshape(blocks, PAGE, width)
    key_out = jnp.zeros_like(key_pages)
    value_out = jnp.zeros_like(value_pages)
    for block_index in range(blocks):
        offset = (2 * block_index + 1) * devices // (2 * blocks)
        received = from_behind(
            jnp.stack([key_pages[block_index], value_pages[block_index]]), "blk", offset
        )
        source = (here - offset) % devices
        target = placement[source * blocks + block_index] % blocks
        key_out = lax.dynamic_update_index_in_dim(key_out, received[0], target, 0)
        value_out = lax.dynamic_update_index_in_dim(value_out, received[1], target, 0)
    return (key_out, value_out)


def body(
    hidden_in,
    w_query,
    w_key,
    w_value,
    w_out,
    head_gain,
    eigen_rate,
    pool_keys,
    pool_values,
    req_len,
    prefix_len,
    prefix_pages,
    placement,
):
    tokens_here = hidden_in.shape[0]
    other_w_out = other_half_once_per_group(w_out)
    width_half = w_query.shape[1]
    heads_here = width_half // HD
    hidden_f = hidden_in.astype(jnp.float32)
    row_scale = lax.rsqrt(jnp.mean(hidden_f * hidden_f, axis=-1, keepdims=True) + epsilon)
    anchor = hidden_f * row_scale
    queries, key_rows, value_rows = projections(
        hidden_in, row_scale, w_query, w_key, w_value, head_gain
    )
    fetched = fetch_pages(pool_keys, pool_values, prefix_pages)
    pairs_here = width_half // (2 * HD)
    split = (pairs_here + 1) // 2
    parts = [
        attention(queries, key_rows, value_rows, fetched, req_len, prefix_len, first, count)
        for first, count in ((0, split), (split, pairs_here - split))
    ]
    other_parts = [from_behind(part, "kv", 1) for part in parts]
    attended = jnp.concatenate(parts, axis=1)
    other_attended = jnp.concatenate(other_parts, axis=1)
    branch = jnp.dot(
        in_kv_order(attended, other_attended, 1),
        in_kv_order(w_out, other_w_out, 0),
        preferred_element_type=jnp.float32,
    )
    updated = anchor + eigen_rate * (rms_scale(branch) - anchor)
    layer_out = rms_scale(updated).astype(jnp.bfloat16)
    new_keys, new_values = relay(key_rows, value_rows, placement)
    return (layer_out, new_keys, new_values)


def solution(mesh):
    in_specs = (
        P("blk", None),
        P(None, "kv"),
        P(None, "kv"),
        P(None, "kv"),
        P("kv", None),
        P("kv"),
        P(),
        P("blk", None, "kv"),
        P("blk", None, "kv"),
        P("blk"),
        P("blk"),
        P(),
        P(),
    )
    out_specs = (P("blk", None), P("blk", None, "kv"), P("blk", None, "kv"))
    return jax.shard_map(body, mesh=mesh, in_specs=in_specs, out_specs=out_specs, check_vma=False)
```

```python
import functools
import math

import jax
import jax.numpy as jnp
from jax import lax
from jax.experimental import pallas as pl
from jax.experimental.pallas import tpu as pltpu
from jax.sharding import PartitionSpec as P

HD = 64
PAGE = 256
PMAX = 4


epsilon = 1e-06


def from_behind(block, axis, distance):
    devices = range(lax.axis_size(axis))
    route = [((i - distance) % len(devices), i) for i in devices]
    return lax.ppermute(block, axis, route)


def rms_scale(values):
    return values * lax.rsqrt(jnp.mean(values * values, axis=-1, keepdims=True) + epsilon)


def head_normed(projected, head_gain):
    count = projected.shape[0]
    split_heads = projected.reshape(count, -1, HD)
    return (rms_scale(split_heads).reshape(count, -1) * head_gain).astype(jnp.bfloat16)


def attend(query_heads, key_rows, value_rows, visible):
    key_heads = key_rows.reshape(key_rows.shape[0], -1, HD)
    value_heads = value_rows.reshape(value_rows.shape[0], -1, HD)
    scores = jnp.einsum(
        "qhd,khd->hqk", query_heads, key_heads, preferred_element_type=jnp.float32
    ) / math.sqrt(HD)
    weights = jnp.where(visible, jnp.exp(scores), 0.0)
    totals = jnp.sum(weights, axis=-1)
    mixed = jnp.einsum(
        "hqk,khd->qhd",
        weights.astype(jnp.bfloat16),
        value_heads,
        preferred_element_type=jnp.float32,
    )
    return (totals, mixed)


def other_half_once_per_chip(w_out):
    rows = w_out.shape[0] // 2
    core = lax.axis_index("blk") % 2
    mine = lax.dynamic_slice_in_dim(w_out, core * rows, rows, 0)
    pulled = from_behind(mine, "kv", 1)
    devices = lax.axis_size("blk")
    swapped = lax.ppermute(pulled, "blk", [(i, i ^ 1) for i in range(devices)])
    first = core == 0
    return jnp.concatenate(
        [jnp.where(first, pulled, swapped), jnp.where(first, swapped, pulled)], axis=0
    )


def in_kv_order(mine, other, axis):
    first = lax.axis_index("kv") == 0
    low = jnp.where(first, mine, other)
    high = jnp.where(first, other, mine)
    return jnp.concatenate([low, high], axis=axis)


def projection_kernel(x_ref, scale_ref, wq_ref, wk_ref, wv_ref, gain_ref, q_ref, k_ref, v_ref):
    hidden = x_ref[...]
    lane = lax.broadcasted_iota(jnp.int32, q_ref.shape, 1)
    first = lane < HD

    def normed(w_ref):
        projected = jnp.dot(hidden, w_ref[...], preferred_element_type=jnp.float32)
        squares = projected * projected
        low = jnp.sum(jnp.where(first, squares, 0.0), axis=1, keepdims=True)
        high = jnp.sum(jnp.where(first, 0.0, squares), axis=1, keepdims=True)
        mean = jnp.where(first, low, high) / HD
        return projected * lax.rsqrt(mean + epsilon) * gain_ref[...]

    q_ref[...] = normed(wq_ref).astype(q_ref.dtype)
    k_ref[...] = normed(wk_ref).astype(k_ref.dtype)
    projected = jnp.dot(hidden, wv_ref[...], preferred_element_type=jnp.float32)
    v_ref[...] = (projected * scale_ref[...]).astype(v_ref.dtype)


def projections(hidden_in, row_scale, w_query, w_key, w_value, head_gain):
    tokens, width = hidden_in.shape
    lanes = 2 * HD
    columns = w_query.shape[1]
    weight_spec = pl.BlockSpec((width, lanes), lambda j: (0, j))
    out_spec = pl.BlockSpec((tokens, lanes), lambda j: (0, j))
    shape = jax.ShapeDtypeStruct((tokens, columns), jnp.bfloat16)
    return pl.pallas_call(
        projection_kernel,
        out_shape=(shape, shape, shape),
        grid=(columns // lanes,),
        in_specs=[
            pl.BlockSpec((tokens, width), lambda j: (0, 0)),
            pl.BlockSpec((tokens, 1), lambda j: (0, 0)),
            weight_spec,
            weight_spec,
            weight_spec,
            pl.BlockSpec((1, lanes), lambda j: (0, j)),
        ],
        out_specs=[out_spec, out_spec, out_spec],
    )(hidden_in, row_scale, w_query, w_key, w_value, head_gain.reshape(1, columns))


def attention_kernel(live_ref, depth_ref, q_ref, k_ref, v_ref, *refs):
    page_refs, out_ref = refs[:-1], refs[-1]
    tile = q_ref.shape[0]
    own = k_ref.shape[0]
    live = live_ref[0]
    depth = depth_ref[0]
    query = q_ref[...]
    lane = lax.broadcasted_iota(jnp.int32, query.shape, 1)
    first = lane < HD
    row = pl.program_id(1) * tile + lax.broadcasted_iota(jnp.int32, (tile, own), 0)
    col = lax.broadcasted_iota(jnp.int32, (tile, own), 1)
    own_visible = (col <= row) & (col < live)
    contract = (((1,), (1,)), ((), ()))
    results = []
    for in_head in (first, jnp.logical_not(first)):
        query_head = jnp.where(in_head, query, jnp.zeros_like(query))
        scores = lax.dot_general(
            query_head, k_ref[...], contract, preferred_element_type=jnp.float32
        ) * (1.0 / math.sqrt(HD))
        weights = jnp.where(own_visible, jnp.exp(scores), 0.0)
        total = jnp.sum(weights, axis=1, keepdims=True)
        mixed = jnp.dot(
            weights.astype(jnp.bfloat16), v_ref[...], preferred_element_type=jnp.float32
        )
        for page in range(PMAX):
            key_page = page_refs[page]
            value_page = page_refs[PMAX + page]
            scores = lax.dot_general(
                query_head, key_page[...], contract, preferred_element_type=jnp.float32
            ) * (1.0 / math.sqrt(HD))
            weights = jnp.where(page < depth, jnp.exp(scores), 0.0)
            total = total + jnp.sum(weights, axis=1, keepdims=True)
            mixed = mixed + jnp.dot(
                weights.astype(jnp.bfloat16), value_page[...], preferred_element_type=jnp.float32
            )
        results.append(mixed / total)
    out_ref[...] = jnp.where(first, results[0], results[1]).astype(out_ref.dtype)


def attention(queries, key_rows, value_rows, pages, req_len, prefix_len, first_pair, pairs):
    tokens = queries.shape[0]
    tile = 256
    lanes = 2 * HD
    width = pairs * lanes
    grid = (pairs, tokens // tile)
    own_spec = pl.BlockSpec((tokens, lanes), lambda h, t, *_: (0, h + first_pair))
    key_spec = pl.BlockSpec((None, PAGE, lanes), lambda h, t, *_: (0, 0, h + first_pair))
    value_spec = pl.BlockSpec((None, PAGE, lanes), lambda h, t, *_: (1, 0, h + first_pair))
    tile_spec = pl.BlockSpec((tile, lanes), lambda h, t, *_: (t, h + first_pair))
    out_spec = pl.BlockSpec((tile, lanes), lambda h, t, *_: (t, h))
    grid_spec = pltpu.PrefetchScalarGridSpec(
        num_scalar_prefetch=2,
        grid=grid,
        in_specs=[tile_spec, own_spec, own_spec] + [key_spec] * PMAX + [value_spec] * PMAX,
        out_specs=out_spec,
    )
    return pl.pallas_call(
        attention_kernel,
        out_shape=jax.ShapeDtypeStruct((tokens, width), jnp.bfloat16),
        grid_spec=grid_spec,
    )(req_len, prefix_len, queries, key_rows, value_rows, *pages, *pages)


def gather_kernel(devices, pages_ref, keys_hbm, values_hbm, *refs):
    outs, sems = refs[:PMAX], refs[PMAX]
    here = lax.axis_index("blk")
    count = keys_hbm.shape[0]
    copies = []
    for slot_index in range(PMAX):
        offset = slot_index * devices // PMAX + 1
        asker = lax.rem(here + (devices - offset), devices)
        local = lax.rem(pages_ref[asker, slot_index], count)
        for part, source in enumerate((keys_hbm, values_hbm)):
            copy = pltpu.make_async_copy(
                source.at[local], outs[slot_index].at[part], sems.at[2 * slot_index + part]
            )
            copy.start()
            copies.append(copy)
    for copy in copies:
        copy.wait()


def fetch_pages(pool_keys, pool_values, prefix_pages):
    devices = lax.axis_size("blk")
    page_shape = jax.ShapeDtypeStruct((2,) + pool_keys.shape[1:], pool_keys.dtype)
    grid_spec = pltpu.PrefetchScalarGridSpec(
        num_scalar_prefetch=1,
        grid=(),
        in_specs=[pl.BlockSpec(memory_space=pl.ANY)] * 2,
        out_specs=[pl.BlockSpec(memory_space=pltpu.VMEM)] * PMAX,
        scratch_shapes=[pltpu.SemaphoreType.DMA((2 * PMAX,))],
    )
    gathered = pl.pallas_call(
        functools.partial(gather_kernel, devices),
        out_shape=[page_shape] * PMAX,
        grid_spec=grid_spec,
    )(prefix_pages, pool_keys, pool_values)
    return [
        from_behind(gathered[slot_index], "blk", devices - (slot_index * devices // PMAX + 1))
        for slot_index in range(PMAX)
    ]


def relay(key_rows, value_rows, placement):
    devices = lax.axis_size("blk")
    here = lax.axis_index("blk")
    blocks = key_rows.shape[0] // PAGE
    width = key_rows.shape[1]
    key_pages = key_rows.reshape(blocks, PAGE, width)
    value_pages = value_rows.reshape(blocks, PAGE, width)
    key_out = jnp.zeros_like(key_pages)
    value_out = jnp.zeros_like(value_pages)
    for block_index in range(blocks):
        offset = (2 * block_index + 1) * devices // (2 * blocks)
        received = from_behind(
            jnp.stack([key_pages[block_index], value_pages[block_index]]), "blk", offset
        )
        source = (here - offset) % devices
        target = placement[source * blocks + block_index] % blocks
        key_out = lax.dynamic_update_index_in_dim(key_out, received[0], target, 0)
        value_out = lax.dynamic_update_index_in_dim(value_out, received[1], target, 0)
    return (key_out, value_out)


def body(
    hidden_in,
    w_query,
    w_key,
    w_value,
    w_out,
    head_gain,
    eigen_rate,
    pool_keys,
    pool_values,
    req_len,
    prefix_len,
    prefix_pages,
    placement,
):
    tokens_here = hidden_in.shape[0]
    other_w_out = other_half_once_per_chip(w_out)
    width_half = w_query.shape[1]
    heads_here = width_half // HD
    hidden_f = hidden_in.astype(jnp.float32)
    row_scale = lax.rsqrt(jnp.mean(hidden_f * hidden_f, axis=-1, keepdims=True) + epsilon)
    anchor = hidden_f * row_scale
    queries, key_rows, value_rows = projections(
        hidden_in, row_scale, w_query, w_key, w_value, head_gain
    )
    fetched = fetch_pages(pool_keys, pool_values, prefix_pages)
    pairs_here = width_half // (2 * HD)
    parts = [
        attention(queries, key_rows, value_rows, fetched, req_len, prefix_len, 0, pairs_here)
    ]
    other_parts = [from_behind(part, "kv", 1) for part in parts]
    attended = jnp.concatenate(parts, axis=1)
    other_attended = jnp.concatenate(other_parts, axis=1)
    branch = jnp.dot(
        in_kv_order(attended, other_attended, 1),
        in_kv_order(w_out, other_w_out, 0),
        preferred_element_type=jnp.float32,
    )
    updated = anchor + eigen_rate * (rms_scale(branch) - anchor)
    layer_out = rms_scale(updated).astype(jnp.bfloat16)
    new_keys, new_values = relay(key_rows, value_rows, placement)
    return (layer_out, new_keys, new_values)


def solution(mesh):
    in_specs = (
        P("blk", None),
        P(None, "kv"),
        P(None, "kv"),
        P(None, "kv"),
        P("kv", None),
        P("kv"),
        P(),
        P("blk", None, "kv"),
        P("blk", None, "kv"),
        P("blk"),
        P("blk"),
        P(),
        P(),
    )
    out_specs = (P("blk", None), P("blk", None, "kv"), P("blk", None, "kv"))
    return jax.shard_map(body, mesh=mesh, in_specs=in_specs, out_specs=out_specs, check_vma=False)
```

```python
import functools
import math

import jax
import jax.numpy as jnp
from jax import lax
from jax.experimental import pallas as pl
from jax.experimental.pallas import tpu as pltpu
from jax.sharding import PartitionSpec as P

HD = 64
PAGE = 256
PMAX = 4


epsilon = 1e-06


def from_behind(block, axis, distance):
    devices = range(lax.axis_size(axis))
    route = [((i - distance) % len(devices), i) for i in devices]
    return lax.ppermute(block, axis, route)


def rms_scale(values):
    return values * lax.rsqrt(jnp.mean(values * values, axis=-1, keepdims=True) + epsilon)


def head_normed(projected, head_gain):
    count = projected.shape[0]
    split_heads = projected.reshape(count, -1, HD)
    return (rms_scale(split_heads).reshape(count, -1) * head_gain).astype(jnp.bfloat16)


def attend(query_heads, key_rows, value_rows, visible):
    key_heads = key_rows.reshape(key_rows.shape[0], -1, HD)
    value_heads = value_rows.reshape(value_rows.shape[0], -1, HD)
    scores = jnp.einsum(
        "qhd,khd->hqk", query_heads, key_heads, preferred_element_type=jnp.float32
    ) / math.sqrt(HD)
    weights = jnp.where(visible, jnp.exp(scores), 0.0)
    totals = jnp.sum(weights, axis=-1)
    mixed = jnp.einsum(
        "hqk,khd->qhd",
        weights.astype(jnp.bfloat16),
        value_heads,
        preferred_element_type=jnp.float32,
    )
    return (totals, mixed)


def other_half_once_per_chip(w_out):
    rows = w_out.shape[0] // 2
    core = lax.axis_index("blk") % 2
    mine = lax.dynamic_slice_in_dim(w_out, core * rows, rows, 0)
    pulled = from_behind(mine, "kv", 1)
    devices = lax.axis_size("blk")
    swapped = lax.ppermute(pulled, "blk", [(i, i ^ 1) for i in range(devices)])
    first = core == 0
    return jnp.concatenate(
        [jnp.where(first, pulled, swapped), jnp.where(first, swapped, pulled)], axis=0
    )


def in_kv_order(mine, other, axis):
    first = lax.axis_index("kv") == 0
    low = jnp.where(first, mine, other)
    high = jnp.where(first, other, mine)
    return jnp.concatenate([low, high], axis=axis)


def projection_kernel(x_ref, scale_ref, wq_ref, wk_ref, wv_ref, gain_ref, q_ref, k_ref, v_ref):
    hidden = x_ref[...]
    lane = lax.broadcasted_iota(jnp.int32, q_ref.shape, 1)
    first = lane < HD

    def normed(w_ref):
        projected = jnp.dot(hidden, w_ref[...], preferred_element_type=jnp.float32)
        squares = projected * projected
        low = jnp.sum(jnp.where(first, squares, 0.0), axis=1, keepdims=True)
        high = jnp.sum(jnp.where(first, 0.0, squares), axis=1, keepdims=True)
        mean = jnp.where(first, low, high) / HD
        return projected * lax.rsqrt(mean + epsilon) * gain_ref[...]

    q_ref[...] = normed(wq_ref).astype(q_ref.dtype)
    k_ref[...] = normed(wk_ref).astype(k_ref.dtype)
    projected = jnp.dot(hidden, wv_ref[...], preferred_element_type=jnp.float32)
    v_ref[...] = (projected * scale_ref[...]).astype(v_ref.dtype)


def projections(hidden_in, row_scale, w_query, w_key, w_value, head_gain):
    tokens, width = hidden_in.shape
    lanes = 2 * HD
    columns = w_query.shape[1]
    weight_spec = pl.BlockSpec((width, lanes), lambda j: (0, j))
    out_spec = pl.BlockSpec((tokens, lanes), lambda j: (0, j))
    shape = jax.ShapeDtypeStruct((tokens, columns), jnp.bfloat16)
    return pl.pallas_call(
        projection_kernel,
        out_shape=(shape, shape, shape),
        grid=(columns // lanes,),
        in_specs=[
            pl.BlockSpec((tokens, width), lambda j: (0, 0)),
            pl.BlockSpec((tokens, 1), lambda j: (0, 0)),
            weight_spec,
            weight_spec,
            weight_spec,
            pl.BlockSpec((1, lanes), lambda j: (0, j)),
        ],
        out_specs=[out_spec, out_spec, out_spec],
    )(hidden_in, row_scale, w_query, w_key, w_value, head_gain.reshape(1, columns))


def attention_kernel(live_ref, depth_ref, q_ref, k_ref, v_ref, *refs):
    page_refs, out_ref = refs[:-1], refs[-1]
    tile = q_ref.shape[0]
    own = k_ref.shape[0]
    live = live_ref[0]
    depth = depth_ref[0]
    query = q_ref[...]
    lane = lax.broadcasted_iota(jnp.int32, query.shape, 1)
    first = lane < HD
    row = pl.program_id(1) * tile + lax.broadcasted_iota(jnp.int32, (tile, own), 0)
    col = lax.broadcasted_iota(jnp.int32, (tile, own), 1)
    own_visible = (col <= row) & (col < live)
    contract = (((1,), (1,)), ((), ()))
    results = []
    for in_head in (first, jnp.logical_not(first)):
        query_head = jnp.where(in_head, query, jnp.zeros_like(query))
        scores = lax.dot_general(
            query_head, k_ref[...], contract, preferred_element_type=jnp.float32
        ) * (1.0 / math.sqrt(HD))
        weights = jnp.where(own_visible, jnp.exp(scores), 0.0)
        total = jnp.sum(weights, axis=1, keepdims=True)
        mixed = jnp.dot(
            weights.astype(jnp.bfloat16), v_ref[...], preferred_element_type=jnp.float32
        )
        for page in range(PMAX):
            key_page = page_refs[page]
            value_page = page_refs[PMAX + page]
            scores = lax.dot_general(
                query_head, key_page[...], contract, preferred_element_type=jnp.float32
            ) * (1.0 / math.sqrt(HD))
            weights = jnp.where(page < depth, jnp.exp(scores), 0.0)
            total = total + jnp.sum(weights, axis=1, keepdims=True)
            mixed = mixed + jnp.dot(
                weights.astype(jnp.bfloat16), value_page[...], preferred_element_type=jnp.float32
            )
        results.append(mixed / total)
    out_ref[...] = jnp.where(first, results[0], results[1]).astype(out_ref.dtype)


def attention(queries, key_rows, value_rows, pages, req_len, prefix_len, first_pair, pairs):
    tokens = queries.shape[0]
    tile = 256
    lanes = 2 * HD
    width = pairs * lanes
    grid = (pairs, tokens // tile)
    own_spec = pl.BlockSpec((tokens, lanes), lambda h, t, *_: (0, h + first_pair))
    key_spec = pl.BlockSpec((None, PAGE, lanes), lambda h, t, *_: (0, 0, h + first_pair))
    value_spec = pl.BlockSpec((None, PAGE, lanes), lambda h, t, *_: (1, 0, h + first_pair))
    tile_spec = pl.BlockSpec((tile, lanes), lambda h, t, *_: (t, h + first_pair))
    out_spec = pl.BlockSpec((tile, lanes), lambda h, t, *_: (t, h))
    grid_spec = pltpu.PrefetchScalarGridSpec(
        num_scalar_prefetch=2,
        grid=grid,
        in_specs=[tile_spec, own_spec, own_spec] + [key_spec] * PMAX + [value_spec] * PMAX,
        out_specs=out_spec,
    )
    return pl.pallas_call(
        attention_kernel,
        out_shape=jax.ShapeDtypeStruct((tokens, width), jnp.bfloat16),
        grid_spec=grid_spec,
    )(req_len, prefix_len, queries, key_rows, value_rows, *pages, *pages)


def gather_kernel(devices, pages_ref, keys_hbm, values_hbm, *refs):
    outs, sems = refs[:PMAX], refs[PMAX]
    here = lax.axis_index("blk")
    count = keys_hbm.shape[0]
    copies = []
    for slot_index in range(PMAX):
        offset = slot_index * devices // PMAX + 1
        asker = lax.rem(here + (devices - offset), devices)
        local = lax.rem(pages_ref[asker, slot_index], count)
        for part, source in enumerate((keys_hbm, values_hbm)):
            copy = pltpu.make_async_copy(
                source.at[local], outs[slot_index].at[part], sems.at[2 * slot_index + part]
            )
            copy.start()
            copies.append(copy)
    for copy in copies:
        copy.wait()


def fetch_pages(pool_keys, pool_values, prefix_pages):
    devices = lax.axis_size("blk")
    page_shape = jax.ShapeDtypeStruct((2,) + pool_keys.shape[1:], pool_keys.dtype)
    grid_spec = pltpu.PrefetchScalarGridSpec(
        num_scalar_prefetch=1,
        grid=(),
        in_specs=[pl.BlockSpec(memory_space=pl.ANY)] * 2,
        out_specs=[pl.BlockSpec(memory_space=pltpu.VMEM)] * PMAX,
        scratch_shapes=[pltpu.SemaphoreType.DMA((2 * PMAX,))],
    )
    gathered = pl.pallas_call(
        functools.partial(gather_kernel, devices),
        out_shape=[page_shape] * PMAX,
        grid_spec=grid_spec,
    )(prefix_pages, pool_keys, pool_values)
    return [
        from_behind(gathered[slot_index], "blk", devices - (slot_index * devices // PMAX + 1))
        for slot_index in range(PMAX)
    ]


def relay(key_rows, value_rows, placement):
    devices = lax.axis_size("blk")
    here = lax.axis_index("blk")
    blocks = key_rows.shape[0] // PAGE
    width = key_rows.shape[1]
    key_pages = key_rows.reshape(blocks, PAGE, width)
    value_pages = value_rows.reshape(blocks, PAGE, width)
    key_out = jnp.zeros_like(key_pages)
    value_out = jnp.zeros_like(value_pages)
    for block_index in range(blocks):
        offset = (2 * block_index + 1) * devices // (2 * blocks)
        received = from_behind(
            jnp.stack([key_pages[block_index], value_pages[block_index]]), "blk", offset
        )
        source = (here - offset) % devices
        target = placement[source * blocks + block_index] % blocks
        key_out = lax.dynamic_update_index_in_dim(key_out, received[0], target, 0)
        value_out = lax.dynamic_update_index_in_dim(value_out, received[1], target, 0)
    return (key_out, value_out)


def body(
    hidden_in,
    w_query,
    w_key,
    w_value,
    w_out,
    head_gain,
    eigen_rate,
    pool_keys,
    pool_values,
    req_len,
    prefix_len,
    prefix_pages,
    placement,
):
    tokens_here = hidden_in.shape[0]
    other_w_out = other_half_once_per_chip(w_out)
    width_half = w_query.shape[1]
    heads_here = width_half // HD
    hidden_f = hidden_in.astype(jnp.float32)
    row_scale = lax.rsqrt(jnp.mean(hidden_f * hidden_f, axis=-1, keepdims=True) + epsilon)
    anchor = hidden_f * row_scale
    queries, key_rows, value_rows = projections(
        hidden_in, row_scale, w_query, w_key, w_value, head_gain
    )
    fetched = fetch_pages(pool_keys, pool_values, prefix_pages)
    pairs_here = width_half // (2 * HD)
    split = pairs_here - 1
    parts = [
        attention(queries, key_rows, value_rows, fetched, req_len, prefix_len, first, count)
        for first, count in ((0, split), (split, pairs_here - split))
    ]
    other_parts = [from_behind(part, "kv", 1) for part in parts]
    attended = jnp.concatenate(parts, axis=1)
    other_attended = jnp.concatenate(other_parts, axis=1)
    branch = jnp.dot(
        in_kv_order(attended, other_attended, 1),
        in_kv_order(w_out, other_w_out, 0),
        preferred_element_type=jnp.float32,
    )
    updated = anchor + eigen_rate * (rms_scale(branch) - anchor)
    layer_out = rms_scale(updated).astype(jnp.bfloat16)
    new_keys, new_values = relay(key_rows, value_rows, placement)
    return (layer_out, new_keys, new_values)


def solution(mesh):
    in_specs = (
        P("blk", None),
        P(None, "kv"),
        P(None, "kv"),
        P(None, "kv"),
        P("kv", None),
        P("kv"),
        P(),
        P("blk", None, "kv"),
        P("blk", None, "kv"),
        P("blk"),
        P("blk"),
        P(),
        P(),
    )
    out_specs = (P("blk", None), P("blk", None, "kv"), P("blk", None, "kv"))
    return jax.shard_map(body, mesh=mesh, in_specs=in_specs, out_specs=out_specs, check_vma=False)
```

```python
import functools
import math

import jax
import jax.numpy as jnp
from jax import lax
from jax.experimental import pallas as pl
from jax.experimental.pallas import tpu as pltpu
from jax.sharding import PartitionSpec as P

HD = 64
PAGE = 256
PMAX = 4


epsilon = 1e-06


def from_behind(block, axis, distance):
    devices = range(lax.axis_size(axis))
    route = [((i - distance) % len(devices), i) for i in devices]
    return lax.ppermute(block, axis, route)


def rms_scale(values):
    return values * lax.rsqrt(jnp.mean(values * values, axis=-1, keepdims=True) + epsilon)


def head_normed(projected, head_gain):
    count = projected.shape[0]
    split_heads = projected.reshape(count, -1, HD)
    return (rms_scale(split_heads).reshape(count, -1) * head_gain).astype(jnp.bfloat16)


def attend(query_heads, key_rows, value_rows, visible):
    key_heads = key_rows.reshape(key_rows.shape[0], -1, HD)
    value_heads = value_rows.reshape(value_rows.shape[0], -1, HD)
    scores = jnp.einsum(
        "qhd,khd->hqk", query_heads, key_heads, preferred_element_type=jnp.float32
    ) / math.sqrt(HD)
    weights = jnp.where(visible, jnp.exp(scores), 0.0)
    totals = jnp.sum(weights, axis=-1)
    mixed = jnp.einsum(
        "hqk,khd->qhd",
        weights.astype(jnp.bfloat16),
        value_heads,
        preferred_element_type=jnp.float32,
    )
    return (totals, mixed)


def other_half_once_per_chip(w_out):
    rows = w_out.shape[0] // 2
    core = lax.axis_index("blk") % 2
    mine = lax.dynamic_slice_in_dim(w_out, core * rows, rows, 0)
    pulled = from_behind(mine, "kv", 1)
    devices = lax.axis_size("blk")
    swapped = lax.ppermute(pulled, "blk", [(i, i ^ 1) for i in range(devices)])
    first = core == 0
    return jnp.concatenate(
        [jnp.where(first, pulled, swapped), jnp.where(first, swapped, pulled)], axis=0
    )


def in_kv_order(mine, other, axis):
    first = lax.axis_index("kv") == 0
    low = jnp.where(first, mine, other)
    high = jnp.where(first, other, mine)
    return jnp.concatenate([low, high], axis=axis)


def projection_kernel(x_ref, scale_ref, wq_ref, wk_ref, wv_ref, gain_ref, q_ref, k_ref, v_ref):
    hidden = x_ref[...]
    lane = lax.broadcasted_iota(jnp.int32, q_ref.shape, 1)
    first = lane < HD

    def normed(w_ref):
        projected = jnp.dot(hidden, w_ref[...], preferred_element_type=jnp.float32)
        squares = projected * projected
        low = jnp.sum(jnp.where(first, squares, 0.0), axis=1, keepdims=True)
        high = jnp.sum(jnp.where(first, 0.0, squares), axis=1, keepdims=True)
        mean = jnp.where(first, low, high) / HD
        return projected * lax.rsqrt(mean + epsilon) * gain_ref[...]

    q_ref[...] = normed(wq_ref).astype(q_ref.dtype)
    k_ref[...] = normed(wk_ref).astype(k_ref.dtype)
    projected = jnp.dot(hidden, wv_ref[...], preferred_element_type=jnp.float32)
    v_ref[...] = (projected * scale_ref[...]).astype(v_ref.dtype)


def projections(hidden_in, row_scale, w_query, w_key, w_value, head_gain):
    tokens, width = hidden_in.shape
    lanes = 2 * HD
    columns = w_query.shape[1]
    weight_spec = pl.BlockSpec((width, lanes), lambda j: (0, j))
    out_spec = pl.BlockSpec((tokens, lanes), lambda j: (0, j))
    shape = jax.ShapeDtypeStruct((tokens, columns), jnp.bfloat16)
    return pl.pallas_call(
        projection_kernel,
        out_shape=(shape, shape, shape),
        grid=(columns // lanes,),
        in_specs=[
            pl.BlockSpec((tokens, width), lambda j: (0, 0)),
            pl.BlockSpec((tokens, 1), lambda j: (0, 0)),
            weight_spec,
            weight_spec,
            weight_spec,
            pl.BlockSpec((1, lanes), lambda j: (0, j)),
        ],
        out_specs=[out_spec, out_spec, out_spec],
    )(hidden_in, row_scale, w_query, w_key, w_value, head_gain.reshape(1, columns))


def attention_kernel(live_ref, depth_ref, q_ref, k_ref, v_ref, *refs):
    page_refs, out_ref = refs[:-1], refs[-1]
    tile = q_ref.shape[0]
    own = k_ref.shape[0]
    live = live_ref[0]
    depth = depth_ref[0]
    query = q_ref[...]
    lane = lax.broadcasted_iota(jnp.int32, query.shape, 1)
    first = lane < HD
    row = pl.program_id(1) * tile + lax.broadcasted_iota(jnp.int32, (tile, own), 0)
    col = lax.broadcasted_iota(jnp.int32, (tile, own), 1)
    own_visible = (col <= row) & (col < live)
    contract = (((1,), (1,)), ((), ()))
    results = []
    for in_head in (first, jnp.logical_not(first)):
        query_head = jnp.where(in_head, query, jnp.zeros_like(query))
        scores = lax.dot_general(
            query_head, k_ref[...], contract, preferred_element_type=jnp.float32
        ) * (1.0 / math.sqrt(HD))
        weights = jnp.where(own_visible, jnp.exp(scores), 0.0)
        total = jnp.sum(weights, axis=1, keepdims=True)
        mixed = jnp.dot(
            weights.astype(jnp.bfloat16), v_ref[...], preferred_element_type=jnp.float32
        )
        for page in range(PMAX):
            key_page = page_refs[page]
            value_page = page_refs[PMAX + page]
            scores = lax.dot_general(
                query_head, key_page[...], contract, preferred_element_type=jnp.float32
            ) * (1.0 / math.sqrt(HD))
            weights = jnp.where(page < depth, jnp.exp(scores), 0.0)
            total = total + jnp.sum(weights, axis=1, keepdims=True)
            mixed = mixed + jnp.dot(
                weights.astype(jnp.bfloat16), value_page[...], preferred_element_type=jnp.float32
            )
        results.append(mixed / total)
    out_ref[...] = jnp.where(first, results[0], results[1]).astype(out_ref.dtype)


def attention(queries, key_rows, value_rows, pages, req_len, prefix_len, first_pair, pairs):
    tokens = queries.shape[0]
    tile = 256
    lanes = 2 * HD
    width = pairs * lanes
    grid = (pairs, tokens // tile)
    own_spec = pl.BlockSpec((tokens, lanes), lambda h, t, *_: (0, h + first_pair))
    key_spec = pl.BlockSpec((None, PAGE, lanes), lambda h, t, *_: (0, 0, h + first_pair))
    value_spec = pl.BlockSpec((None, PAGE, lanes), lambda h, t, *_: (1, 0, h + first_pair))
    tile_spec = pl.BlockSpec((tile, lanes), lambda h, t, *_: (t, h + first_pair))
    out_spec = pl.BlockSpec((tile, lanes), lambda h, t, *_: (t, h))
    grid_spec = pltpu.PrefetchScalarGridSpec(
        num_scalar_prefetch=2,
        grid=grid,
        in_specs=[tile_spec, own_spec, own_spec] + [key_spec] * PMAX + [value_spec] * PMAX,
        out_specs=out_spec,
    )
    return pl.pallas_call(
        attention_kernel,
        out_shape=jax.ShapeDtypeStruct((tokens, width), jnp.bfloat16),
        grid_spec=grid_spec,
    )(req_len, prefix_len, queries, key_rows, value_rows, *pages, *pages)


def gather_kernel(devices, pages_ref, keys_hbm, values_hbm, *refs):
    outs, sems = refs[:PMAX], refs[PMAX]
    here = lax.axis_index("blk")
    count = keys_hbm.shape[0]
    copies = []
    for slot_index in range(PMAX):
        offset = slot_index * devices // PMAX + 1
        asker = lax.rem(here + (devices - offset), devices)
        local = lax.rem(pages_ref[asker, slot_index], count)
        for part, source in enumerate((keys_hbm, values_hbm)):
            copy = pltpu.make_async_copy(
                source.at[local], outs[slot_index].at[part], sems.at[2 * slot_index + part]
            )
            copy.start()
            copies.append(copy)
    for copy in copies:
        copy.wait()


def fetch_pages(pool_keys, pool_values, prefix_pages):
    devices = lax.axis_size("blk")
    page_shape = jax.ShapeDtypeStruct((2,) + pool_keys.shape[1:], pool_keys.dtype)
    grid_spec = pltpu.PrefetchScalarGridSpec(
        num_scalar_prefetch=1,
        grid=(),
        in_specs=[pl.BlockSpec(memory_space=pl.ANY)] * 2,
        out_specs=[pl.BlockSpec(memory_space=pltpu.VMEM)] * PMAX,
        scratch_shapes=[pltpu.SemaphoreType.DMA((2 * PMAX,))],
    )
    gathered = pl.pallas_call(
        functools.partial(gather_kernel, devices),
        out_shape=[page_shape] * PMAX,
        grid_spec=grid_spec,
    )(prefix_pages, pool_keys, pool_values)
    return [
        from_behind(gathered[slot_index], "blk", devices - (slot_index * devices // PMAX + 1))
        for slot_index in range(PMAX)
    ]


def relay(key_rows, value_rows, placement):
    devices = lax.axis_size("blk")
    here = lax.axis_index("blk")
    blocks = key_rows.shape[0] // PAGE
    width = key_rows.shape[1]
    key_pages = key_rows.reshape(blocks, PAGE, width)
    value_pages = value_rows.reshape(blocks, PAGE, width)
    key_out = jnp.zeros_like(key_pages)
    value_out = jnp.zeros_like(value_pages)
    for block_index in range(blocks):
        offset = (2 * block_index + 1) * devices // (2 * blocks)
        received = from_behind(
            jnp.stack([key_pages[block_index], value_pages[block_index]]), "blk", offset
        )
        source = (here - offset) % devices
        target = placement[source * blocks + block_index] % blocks
        key_out = lax.dynamic_update_index_in_dim(key_out, received[0], target, 0)
        value_out = lax.dynamic_update_index_in_dim(value_out, received[1], target, 0)
    return (key_out, value_out)


def body(
    hidden_in,
    w_query,
    w_key,
    w_value,
    w_out,
    head_gain,
    eigen_rate,
    pool_keys,
    pool_values,
    req_len,
    prefix_len,
    prefix_pages,
    placement,
):
    tokens_here = hidden_in.shape[0]
    other_w_out = other_half_once_per_chip(w_out)
    width_half = w_query.shape[1]
    heads_here = width_half // HD
    hidden_f = hidden_in.astype(jnp.float32)
    row_scale = lax.rsqrt(jnp.mean(hidden_f * hidden_f, axis=-1, keepdims=True) + epsilon)
    anchor = hidden_f * row_scale
    queries, key_rows, value_rows = projections(
        hidden_in, row_scale, w_query, w_key, w_value, head_gain
    )
    fetched = fetch_pages(pool_keys, pool_values, prefix_pages)
    pairs_here = width_half // (2 * HD)
    split = pairs_here // 2
    parts = [
        attention(queries, key_rows, value_rows, fetched, req_len, prefix_len, first, count)
        for first, count in ((0, split), (split, pairs_here - split))
    ]
    other_parts = [from_behind(part, "kv", 1) for part in parts]
    attended = jnp.concatenate(parts, axis=1)
    other_attended = jnp.concatenate(other_parts, axis=1)
    branch = jnp.dot(
        in_kv_order(attended, other_attended, 1),
        in_kv_order(w_out, other_w_out, 0),
        preferred_element_type=jnp.float32,
    )
    updated = anchor + eigen_rate * (rms_scale(branch) - anchor)
    layer_out = rms_scale(updated).astype(jnp.bfloat16)
    new_keys, new_values = relay(key_rows, value_rows, placement)
    return (layer_out, new_keys, new_values)


def solution(mesh):
    in_specs = (
        P("blk", None),
        P(None, "kv"),
        P(None, "kv"),
        P(None, "kv"),
        P("kv", None),
        P("kv"),
        P(),
        P("blk", None, "kv"),
        P("blk", None, "kv"),
        P("blk"),
        P("blk"),
        P(),
        P(),
    )
    out_specs = (P("blk", None), P("blk", None, "kv"), P("blk", None, "kv"))
    return jax.shard_map(body, mesh=mesh, in_specs=in_specs, out_specs=out_specs, check_vma=False)
```

```python
import functools
import math

import jax
import jax.numpy as jnp
from jax import lax
from jax.experimental import pallas as pl
from jax.experimental.pallas import tpu as pltpu
from jax.sharding import PartitionSpec as P

HD = 64
PAGE = 256
PMAX = 4


epsilon = 1e-06


def from_behind(block, axis, distance):
    devices = range(lax.axis_size(axis))
    route = [((i - distance) % len(devices), i) for i in devices]
    return lax.ppermute(block, axis, route)


def rms_scale(values):
    return values * lax.rsqrt(jnp.mean(values * values, axis=-1, keepdims=True) + epsilon)


def head_normed(projected, head_gain):
    count = projected.shape[0]
    split_heads = projected.reshape(count, -1, HD)
    return (rms_scale(split_heads).reshape(count, -1) * head_gain).astype(jnp.bfloat16)


def attend(query_heads, key_rows, value_rows, visible):
    key_heads = key_rows.reshape(key_rows.shape[0], -1, HD)
    value_heads = value_rows.reshape(value_rows.shape[0], -1, HD)
    scores = jnp.einsum(
        "qhd,khd->hqk", query_heads, key_heads, preferred_element_type=jnp.float32
    ) / math.sqrt(HD)
    weights = jnp.where(visible, jnp.exp(scores), 0.0)
    totals = jnp.sum(weights, axis=-1)
    mixed = jnp.einsum(
        "hqk,khd->qhd",
        weights.astype(jnp.bfloat16),
        value_heads,
        preferred_element_type=jnp.float32,
    )
    return (totals, mixed)


def other_half_once_per_chip(w_out):
    rows = w_out.shape[0] // 2
    core = lax.axis_index("blk") % 2
    mine = lax.dynamic_slice_in_dim(w_out, core * rows, rows, 0)
    pulled = from_behind(mine, "kv", 1)
    devices = lax.axis_size("blk")
    swapped = lax.ppermute(pulled, "blk", [(i, i ^ 1) for i in range(devices)])
    first = core == 0
    return jnp.concatenate(
        [jnp.where(first, pulled, swapped), jnp.where(first, swapped, pulled)], axis=0
    )


def in_kv_order(mine, other, axis):
    first = lax.axis_index("kv") == 0
    low = jnp.where(first, mine, other)
    high = jnp.where(first, other, mine)
    return jnp.concatenate([low, high], axis=axis)


def projection_kernel(x_ref, scale_ref, wq_ref, wk_ref, wv_ref, gain_ref, q_ref, k_ref, v_ref):
    hidden = x_ref[...]
    lane = lax.broadcasted_iota(jnp.int32, q_ref.shape, 1)
    first = lane < HD

    def normed(w_ref):
        projected = jnp.dot(hidden, w_ref[...], preferred_element_type=jnp.float32)
        squares = projected * projected
        low = jnp.sum(jnp.where(first, squares, 0.0), axis=1, keepdims=True)
        high = jnp.sum(jnp.where(first, 0.0, squares), axis=1, keepdims=True)
        mean = jnp.where(first, low, high) / HD
        return projected * lax.rsqrt(mean + epsilon) * gain_ref[...]

    q_ref[...] = normed(wq_ref).astype(q_ref.dtype)
    k_ref[...] = normed(wk_ref).astype(k_ref.dtype)
    projected = jnp.dot(hidden, wv_ref[...], preferred_element_type=jnp.float32)
    v_ref[...] = (projected * scale_ref[...]).astype(v_ref.dtype)


def projections(hidden_in, row_scale, w_query, w_key, w_value, head_gain):
    tokens, width = hidden_in.shape
    lanes = 2 * HD
    columns = w_query.shape[1]
    weight_spec = pl.BlockSpec((width, lanes), lambda j: (0, j))
    out_spec = pl.BlockSpec((tokens, lanes), lambda j: (0, j))
    shape = jax.ShapeDtypeStruct((tokens, columns), jnp.bfloat16)
    return pl.pallas_call(
        projection_kernel,
        out_shape=(shape, shape, shape),
        grid=(columns // lanes,),
        in_specs=[
            pl.BlockSpec((tokens, width), lambda j: (0, 0)),
            pl.BlockSpec((tokens, 1), lambda j: (0, 0)),
            weight_spec,
            weight_spec,
            weight_spec,
            pl.BlockSpec((1, lanes), lambda j: (0, j)),
        ],
        out_specs=[out_spec, out_spec, out_spec],
    )(hidden_in, row_scale, w_query, w_key, w_value, head_gain.reshape(1, columns))


def attention_kernel(live_ref, depth_ref, q_ref, k_ref, v_ref, *refs):
    page_refs, out_ref = refs[:-1], refs[-1]
    tile = q_ref.shape[0]
    own = k_ref.shape[0]
    live = live_ref[0]
    depth = depth_ref[0]
    query = q_ref[...]
    lane = lax.broadcasted_iota(jnp.int32, query.shape, 1)
    first = lane < HD
    row = pl.program_id(1) * tile + lax.broadcasted_iota(jnp.int32, (tile, own), 0)
    col = lax.broadcasted_iota(jnp.int32, (tile, own), 1)
    own_visible = (col <= row) & (col < live)
    contract = (((1,), (1,)), ((), ()))
    results = []
    for in_head in (first, jnp.logical_not(first)):
        query_head = jnp.where(in_head, query, jnp.zeros_like(query))
        scores = lax.dot_general(
            query_head, k_ref[...], contract, preferred_element_type=jnp.float32
        ) * (1.0 / math.sqrt(HD))
        weights = jnp.where(own_visible, jnp.exp(scores), 0.0)
        total = jnp.sum(weights, axis=1, keepdims=True)
        mixed = jnp.dot(
            weights.astype(jnp.bfloat16), v_ref[...], preferred_element_type=jnp.float32
        )
        for page in range(PMAX):
            key_page = page_refs[page]
            value_page = page_refs[PMAX + page]
            scores = lax.dot_general(
                query_head, key_page[...], contract, preferred_element_type=jnp.float32
            ) * (1.0 / math.sqrt(HD))
            weights = jnp.where(page < depth, jnp.exp(scores), 0.0)
            total = total + jnp.sum(weights, axis=1, keepdims=True)
            mixed = mixed + jnp.dot(
                weights.astype(jnp.bfloat16), value_page[...], preferred_element_type=jnp.float32
            )
        results.append(mixed / total)
    out_ref[...] = jnp.where(first, results[0], results[1]).astype(out_ref.dtype)


def attention(queries, key_rows, value_rows, pages, req_len, prefix_len, first_pair, pairs):
    tokens = queries.shape[0]
    tile = 512
    lanes = 2 * HD
    width = pairs * lanes
    grid = (pairs, tokens // tile)
    own_spec = pl.BlockSpec((tokens, lanes), lambda h, t, *_: (0, h + first_pair))
    key_spec = pl.BlockSpec((None, PAGE, lanes), lambda h, t, *_: (0, 0, h + first_pair))
    value_spec = pl.BlockSpec((None, PAGE, lanes), lambda h, t, *_: (1, 0, h + first_pair))
    tile_spec = pl.BlockSpec((tile, lanes), lambda h, t, *_: (t, h + first_pair))
    out_spec = pl.BlockSpec((tile, lanes), lambda h, t, *_: (t, h))
    grid_spec = pltpu.PrefetchScalarGridSpec(
        num_scalar_prefetch=2,
        grid=grid,
        in_specs=[tile_spec, own_spec, own_spec] + [key_spec] * PMAX + [value_spec] * PMAX,
        out_specs=out_spec,
    )
    return pl.pallas_call(
        attention_kernel,
        out_shape=jax.ShapeDtypeStruct((tokens, width), jnp.bfloat16),
        grid_spec=grid_spec,
    )(req_len, prefix_len, queries, key_rows, value_rows, *pages, *pages)


def gather_kernel(devices, pages_ref, keys_hbm, values_hbm, *refs):
    outs, sems = refs[:PMAX], refs[PMAX]
    here = lax.axis_index("blk")
    count = keys_hbm.shape[0]
    copies = []
    for slot_index in range(PMAX):
        offset = slot_index * devices // PMAX + 1
        asker = lax.rem(here + (devices - offset), devices)
        local = lax.rem(pages_ref[asker, slot_index], count)
        for part, source in enumerate((keys_hbm, values_hbm)):
            copy = pltpu.make_async_copy(
                source.at[local], outs[slot_index].at[part], sems.at[2 * slot_index + part]
            )
            copy.start()
            copies.append(copy)
    for copy in copies:
        copy.wait()


def fetch_pages(pool_keys, pool_values, prefix_pages):
    devices = lax.axis_size("blk")
    page_shape = jax.ShapeDtypeStruct((2,) + pool_keys.shape[1:], pool_keys.dtype)
    grid_spec = pltpu.PrefetchScalarGridSpec(
        num_scalar_prefetch=1,
        grid=(),
        in_specs=[pl.BlockSpec(memory_space=pl.ANY)] * 2,
        out_specs=[pl.BlockSpec(memory_space=pltpu.VMEM)] * PMAX,
        scratch_shapes=[pltpu.SemaphoreType.DMA((2 * PMAX,))],
    )
    gathered = pl.pallas_call(
        functools.partial(gather_kernel, devices),
        out_shape=[page_shape] * PMAX,
        grid_spec=grid_spec,
    )(prefix_pages, pool_keys, pool_values)
    return [
        from_behind(gathered[slot_index], "blk", devices - (slot_index * devices // PMAX + 1))
        for slot_index in range(PMAX)
    ]


def relay(key_rows, value_rows, placement):
    devices = lax.axis_size("blk")
    here = lax.axis_index("blk")
    blocks = key_rows.shape[0] // PAGE
    width = key_rows.shape[1]
    key_pages = key_rows.reshape(blocks, PAGE, width)
    value_pages = value_rows.reshape(blocks, PAGE, width)
    key_out = jnp.zeros_like(key_pages)
    value_out = jnp.zeros_like(value_pages)
    for block_index in range(blocks):
        offset = (2 * block_index + 1) * devices // (2 * blocks)
        received = from_behind(
            jnp.stack([key_pages[block_index], value_pages[block_index]]), "blk", offset
        )
        source = (here - offset) % devices
        target = placement[source * blocks + block_index] % blocks
        key_out = lax.dynamic_update_index_in_dim(key_out, received[0], target, 0)
        value_out = lax.dynamic_update_index_in_dim(value_out, received[1], target, 0)
    return (key_out, value_out)


def body(
    hidden_in,
    w_query,
    w_key,
    w_value,
    w_out,
    head_gain,
    eigen_rate,
    pool_keys,
    pool_values,
    req_len,
    prefix_len,
    prefix_pages,
    placement,
):
    tokens_here = hidden_in.shape[0]
    other_w_out = other_half_once_per_chip(w_out)
    width_half = w_query.shape[1]
    heads_here = width_half // HD
    hidden_f = hidden_in.astype(jnp.float32)
    row_scale = lax.rsqrt(jnp.mean(hidden_f * hidden_f, axis=-1, keepdims=True) + epsilon)
    anchor = hidden_f * row_scale
    queries, key_rows, value_rows = projections(
        hidden_in, row_scale, w_query, w_key, w_value, head_gain
    )
    fetched = fetch_pages(pool_keys, pool_values, prefix_pages)
    pairs_here = width_half // (2 * HD)
    split = (pairs_here + 1) // 2
    parts = [
        attention(queries, key_rows, value_rows, fetched, req_len, prefix_len, first, count)
        for first, count in ((0, split), (split, pairs_here - split))
    ]
    other_parts = [from_behind(part, "kv", 1) for part in parts]
    attended = jnp.concatenate(parts, axis=1)
    other_attended = jnp.concatenate(other_parts, axis=1)
    branch = jnp.dot(
        in_kv_order(attended, other_attended, 1),
        in_kv_order(w_out, other_w_out, 0),
        preferred_element_type=jnp.float32,
    )
    updated = anchor + eigen_rate * (rms_scale(branch) - anchor)
    layer_out = rms_scale(updated).astype(jnp.bfloat16)
    new_keys, new_values = relay(key_rows, value_rows, placement)
    return (layer_out, new_keys, new_values)


def solution(mesh):
    in_specs = (
        P("blk", None),
        P(None, "kv"),
        P(None, "kv"),
        P(None, "kv"),
        P("kv", None),
        P("kv"),
        P(),
        P("blk", None, "kv"),
        P("blk", None, "kv"),
        P("blk"),
        P("blk"),
        P(),
        P(),
    )
    out_specs = (P("blk", None), P("blk", None, "kv"), P("blk", None, "kv"))
    return jax.shard_map(body, mesh=mesh, in_specs=in_specs, out_specs=out_specs, check_vma=False)
```
